32 devices in a mesh: group: 2 (over y), seq: 4 (over z), head: 2 (over x), sub: 2 (over core).
Axes of the slice: x: 2, y: 2, z: 4, core: 2. Of those that a mesh axis runs over, the one named last changes fastest.
Arguments:
- queries: bfloat16 [4096, 4096], P(('group', 'seq'), ('head', 'sub')), parts along dimension 0, may hold values from -16 to 16
- key_states: bfloat16 [4096, 2048], P(('group', 'seq'), ('head', 'sub')), parts along dimension 0, may hold values from -16 to 16
- value_states: bfloat16 [4096, 2048], P(('group', 'seq'), ('head', 'sub')), parts along dimension 0, may hold values from -6 to 6
- out_grad: bfloat16 [4096, 4096], P(('group', 'seq'), ('head', 'sub')), parts along dimension 0, may hold values from -6 to 6
- layer_inputs: bfloat16 [4608, 4096], P(('head', 'sub'), ('group', 'seq')), parts along dimension 1, may hold values from -6 to 6
- sketch_seeds: int32 [4608, 128], P(('head', 'sub')), may hold values from -2 to 2
Outputs:
- sketch_query: float32 [256, 4096], P(('group', 'seq'), ('head', 'sub')), parts along dimension 0
- sketch_key: float32 [256, 2048], P(('group', 'seq'), ('head', 'sub')), parts along dimension 0
- sketch_value: float32 [256, 2048], P(('group', 'seq'), ('head', 'sub')), parts along dimension 0
The draws below stay inside these ranges and needn't reach their ends.
There are 2 independent parts, one for each index of `group`. The reference program is written for one: setup_inputs(seed, part) draws one part's arguments, and reference() takes and returns one part's arrays. A program takes and returns all parts, laid end to end along the dimension named above; an argument that names none is the same for every part. Nothing has to cross between parts.
All inputs are finite; a program needn't handle non-finite values.
Results may differ from the reference program's by a relative error of at most 0.0055.
Values may be sent and summed in bfloat16 or wider, within the bound.
A program may use at most 256 MiB of HBM per device.

```python
import math
import jax
import jax.numpy as jnp
from jax import lax

D = 4608
Q_HEADS = 32
KV_HEADS = 16
HEAD = 128
R = 128
WINDOW = 2048
LENGTH = 2048


def scaled_states(key, rows, heads):
    noise_key, scale_key = jax.random.split(key)
    base = jnp.clip(jax.random.normal(noise_key, (rows, heads, HEAD), jnp.float32), -4.0, 4.0)
    scales = jnp.exp(jax.random.uniform(scale_key, (rows, heads, 1), jnp.float32, math.log(0.5), math.log(2.0)))
    return (base * scales).reshape(rows, heads * HEAD).astype(jnp.bfloat16)


def draw_queries(key, part):
    return scaled_states(jax.random.fold_in(key, 11), LENGTH, Q_HEADS)


def draw_key_states(key, part):
    return scaled_states(jax.random.fold_in(key, 23), LENGTH, KV_HEADS)


def place_ends(drawn, key, low, high):
    spot = [jax.random.randint(jax.random.fold_in(key, axis), (), 0, length) for axis, length in enumerate(drawn.shape)]
    longest = drawn.shape.index(max(drawn.shape))
    beside = spot[:longest] + [(spot[longest] + 1) % drawn.shape[longest]] + spot[longest + 1:]
    return drawn.at[tuple(spot)].set(low).at[tuple(beside)].set(high)


def shard_levels(own_key, shape, cuts, low, top_value):
    def one(axis_at, shards_of):
        heights = jax.random.uniform(jax.random.fold_in(jax.random.fold_in(own_key, 6), axis_at), (shards_of,), jnp.float32, low / len(cuts), top_value / len(cuts))
        return jnp.repeat(jnp.exp(heights), shape[axis_at] // shards_of).reshape((-1,) + (1,) * (len(shape) - axis_at - 1))

    gain = one(*cuts[0])
    for cut in cuts[1:]:
        gain = gain * one(*cut)
    return gain


def scatter_about(stream_key, shape, scale, most, pieces=(), kind=jnp.bfloat16):
    result = scale * jax.random.normal(stream_key, shape, jnp.float32)
    if pieces:
        result = result * shard_levels(stream_key, shape, pieces, -0.22, 0.18)
    return jnp.clip(result, -most, most).astype(kind)


def setup_inputs(seed: int = 0, part: int = 0) -> dict:
    seeds = jax.random.split(jax.random.key(seed), 7)
    part_splits = jax.random.split(jax.random.fold_in(seeds[6], part), 7)
    queries = draw_queries(jax.random.fold_in(jax.random.fold_in(seeds[6], part), 71), part)
    key_states = draw_key_states(jax.random.fold_in(jax.random.fold_in(seeds[6], part), 71), part)
    value_states = scatter_about(part_splits[2], (LENGTH, KV_HEADS * HEAD), 1.0, 6.0, ((0, 4), (1, 4)))
    out_grad = scatter_about(part_splits[3], (LENGTH, Q_HEADS * HEAD), 1.0, 6.0, ((0, 4), (1, 4)))
    layer_inputs = scatter_about(part_splits[4], (D, LENGTH), 1.0, 6.0, ((0, 4), (1, 4)))
    sketch_seeds = place_ends(jax.random.randint(seeds[5], (D, R), -2, 3), jax.random.fold_in(seeds[5], 1), -2, 2).astype(jnp.int32)
    return dict(queries=queries, key_states=key_states, value_states=value_states, out_grad=out_grad, layer_inputs=layer_inputs, sketch_seeds=sketch_seeds)


cap_value = 50.0
query_scale = 144.0 ** -0.5


def exact_product(form, left, right):
    return jnp.einsum(form, left.astype(jnp.float32), right.astype(jnp.float32))


def band_pass(product, queries, key_states, value_states, out_grad, allowed):
    rows = queries.shape[0]
    keys = key_states.shape[0]
    kv_heads = key_states.shape[1] // HEAD
    groups = queries.shape[1] // key_states.shape[1]
    query_heads = queries.reshape(rows, kv_heads, groups, HEAD)
    key_heads = key_states.reshape(keys, kv_heads, HEAD)
    value_heads = value_states.reshape(keys, kv_heads, HEAD)
    grad_heads = out_grad.reshape(rows, kv_heads, groups, HEAD)
    scores = product("rhgd,khd->hgrk", query_heads, key_heads) * query_scale
    bounded = jnp.tanh(scores / cap_value)
    weight_grad = product("rhgd,khd->hgrk", grad_heads, value_heads)
    powers = jnp.where(allowed, jnp.exp(cap_value * bounded), 0.0)
    totals = jnp.sum(powers, axis=-1, keepdims=True)
    probs = powers / totals
    row_dot = jnp.sum(probs * weight_grad, axis=-1, keepdims=True)
    score_grad = (probs * (weight_grad - row_dot) * (1.0 - bounded * bounded) * query_scale).astype(jnp.bfloat16)
    prob_half = probs.astype(jnp.bfloat16)
    query_grad = product("hgrk,khd->rhgd", score_grad, key_heads).reshape(rows, -1)
    key_grad = product("hgrk,rhgd->khd", score_grad, query_heads).reshape(keys, -1)
    value_grad = product("hgrk,rhgd->khd", prob_half, grad_heads).reshape(keys, -1)
    return query_grad, key_grad, value_grad


def reference(queries, key_states, value_states, out_grad, layer_inputs, sketch_seeds):
    length = queries.shape[0]
    window = WINDOW
    block = min(512, length)
    span = block + window
    kv_width = key_states.shape[1]
    zeros_kv = jnp.zeros((window, kv_width), key_states.dtype)
    key_pad = jnp.concatenate([zeros_kv, key_states], 0)
    value_pad = jnp.concatenate([zeros_kv, value_states], 0)

    def step(carry, start):
        key_acc, value_acc = carry
        query_block = lax.dynamic_slice_in_dim(queries, start, block, 0)
        grad_block = lax.dynamic_slice_in_dim(out_grad, start, block, 0)
        key_block = lax.dynamic_slice_in_dim(key_pad, start, span, 0)
        value_block = lax.dynamic_slice_in_dim(value_pad, start, span, 0)
        query_pos = start + jnp.arange(block, dtype=jnp.int32)
        key_pos = start - window + jnp.arange(span, dtype=jnp.int32)
        spacing = query_pos[:, None] - key_pos[None, :]
        allowed = (key_pos[None, :] >= 0) & (spacing >= 0) & (spacing < window)
        query_grad, key_grad, value_grad = band_pass(exact_product, query_block, key_block, value_block, grad_block, allowed)
        key_acc = lax.dynamic_update_slice_in_dim(key_acc, lax.dynamic_slice_in_dim(key_acc, start, span, 0) + key_grad, start, 0)
        value_acc = lax.dynamic_update_slice_in_dim(value_acc, lax.dynamic_slice_in_dim(value_acc, start, span, 0) + value_grad, start, 0)
        return (key_acc, value_acc), query_grad

    starts = jnp.arange(length // block, dtype=jnp.int32) * block
    init = (jnp.zeros((length + window, kv_width), jnp.float32), jnp.zeros((length + window, kv_width), jnp.float32))
    (key_acc, value_acc), query_blocks = lax.scan(step, init, starts)
    query_grad = query_blocks.reshape(length, -1)
    gradients = jnp.concatenate([query_grad, key_acc[window:], value_acc[window:]], 1)
    mixed = jnp.dot(layer_inputs.T, sketch_seeds.astype(jnp.bfloat16), preferred_element_type=jnp.float32)
    projected = (mixed * (2.0 * D * length) ** -0.5).astype(jnp.bfloat16)
    sketch = jnp.dot(projected.astype(jnp.float32).T, gradients, precision=lax.Precision.HIGHEST)
    query_width = queries.shape[1]
    return sketch[:, :query_width], sketch[:, query_width:query_width + kv_width], sketch[:, query_width + kv_width:]
```

```python
import functools
import math

import jax
import jax.numpy as jnp
from jax import lax
from jax.experimental import pallas as pl
from jax.experimental.pallas import tpu as pltpu
from jax.sharding import PartitionSpec as P

D = 4608
HEAD = 128
WINDOW = 2048
CAP = 50.0
QUERY_SCALE = 144.0 ** (-0.5)
CHUNK = 256
MESH = pl.DeviceIdType.MESH


def mm(left, right, dims):
    return lax.dot_general(left, right, (dims, ((), ())), preferred_element_type=jnp.float32)


def attention_kernel(
    shards, reach_full, reach, folds, subs, peers, mix_scale,
    q_hbm, k_hbm, v_hbm, g_hbm, x_hbm, seed_hbm, oq_ref, ok_ref, ov_ref,
    q_ref, g_ref, x_ref, seed_ref, qg, q_t, kv, pg_s, w_s, z_s, dn_s, pm_s, acc_s, db_s,
    part, part_in, mixed_s, sketch, stage, stage_in,
    send_sem, recv_sem, part_send, part_recv, hop_send, hop_recv, share_send, share_recv,
    row_send, row_recv, qg_send, qg_recv, load_sem,
):
    tokens = q_ref.shape[0]
    query_width = q_ref.shape[1]
    kv_width = k_hbm.shape[1]
    kv_heads = kv_width // HEAD
    groups = query_width // kv_width
    chunks = tokens // CHUNK
    share = tokens // peers
    me = lax.axis_index("seq")
    peer = lax.axis_index("head") * subs + lax.axis_index("sub")
    blocks = jnp.minimum(me, reach)

    def last(h):
        return shards - 1 - jnp.maximum(h - (kv_heads - 1 - folds), 0)


    def cols(head):
        return pl.ds(pl.multiple_of(head * HEAD, HEAD), HEAD)

    def peer_at(offset):
        other = lax.rem(peer + offset, peers)
        return other, {"head": lax.div(other, subs), "sub": lax.rem(other, subs)}

    def seq_at(offset):
        other = lax.rem(me + offset, shards)
        return other, {"seq": other}

    def remote(src, dst, send, recv, device):
        return pltpu.make_async_remote_copy(
            src_ref=src, dst_ref=dst, send_sem=send, recv_sem=recv,
            device_id=device, device_id_type=MESH,
        )

    def loop(low, high, fn):
        def step(i, carry):
            fn(i)
            return carry

        lax.fori_loop(low, high, step, 0)

    def hop(h, b, way=1):
        return remote(
            kv.at[h, b], kv.at[h, b], send_sem.at[h, b], recv_sem.at[h, b], {"seq": me + way}
        )

    def row_hop(h, row):
        at = (h - (kv_heads - folds), row - (shards - folds))
        return remote(
            qg.at[at], qg.at[at], qg_send.at[at], qg_recv.at[at], {"seq": me - 1}
        )

    def part_copy(offset):
        other, device = peer_at(offset)
        rows = pl.ds(pl.multiple_of(other * share, share), share)
        return remote(
            part.at[rows], part_in.at[offset], part_send.at[offset], part_recv.at[offset], device
        )

    mine = pl.ds(pl.multiple_of(peer * share, share), share)

    def mixed_along(offset):
        _, device = seq_at(offset)
        return remote(
            mixed_s.at[me, mine], mixed_s.at[me, mine], hop_send.at[offset], hop_recv.at[offset],
            device,
        )

    def mixed_share(b, offset):
        _, device = peer_at(offset)
        return remote(
            mixed_s.at[b, mine], mixed_s.at[b, mine], share_send.at[b, offset],
            share_recv.at[b, offset], device,
        )

    def row_copy(h, offset):
        other, device = seq_at(offset)
        return remote(
            stage.at[h, other], stage_in.at[h, offset], row_send.at[h, offset],
            row_recv.at[h, offset], device,
        )

    barrier = pltpu.get_barrier_semaphore()

    def greet_peer(offset):
        pl.semaphore_signal(barrier, inc=1, device_id=peer_at(offset)[1], device_id_type=MESH)

    def greet_seq(offset):
        pl.semaphore_signal(barrier, inc=1, device_id=seq_at(offset)[1], device_id_type=MESH)

    loop(1, peers, greet_peer)
    loop(1, shards, greet_seq)
    def load_kv(h, which):
        source = (k_hbm, v_hbm)[which]
        return pltpu.make_async_copy(
            source.at[:, cols(h)], kv.at[h, me, which], load_sem.at[4 + which * kv_heads + h]
        )

    loads = [
        pltpu.make_async_copy(source, target, load_sem.at[i])
        for i, (source, target) in enumerate(
            ((seed_hbm, seed_ref), (x_hbm, x_ref), (q_hbm, q_ref), (g_hbm, g_ref))
        )
    ]
    for h in range(kv_heads):
        load_kv(h, 0).start()
        load_kv(h, 1).start()
    for load in loads:
        load.start()
    for h in range(kv_heads):
        load_kv(h, 0).wait()
        load_kv(h, 1).wait()
    pl.semaphore_wait(barrier, peers + shards - 2)

    early = 1

    def send_own(low, high):
        def one(h):
            @pl.when(me < last(h))
            def _():
                hop(h, me).start()

        if reach > 0:
            loop(low, high, one)

    def send_folded(h):
        @pl.when(me > last(h))
        def _():
            at = (h - (kv_heads - folds), me - (shards - folds))
            width = groups * HEAD
            qg[at + (0,)] = q_ref[:, h * width : (h + 1) * width]
            qg[at + (1,)] = g_ref[:, h * width : (h + 1) * width]
            if h < kv_heads - 1:
                hop(h, me, -1).start()
            row_hop(h, me).start()

    send_own(0, early)
    if folds > 0:
        @pl.when(me > last(kv_heads - 1))
        def _():
            hop(kv_heads - 1, me, -1).start()

    loads[0].wait()
    loads[1].wait()
    seeds = seed_ref[...].astype(jnp.float32).astype(jnp.bfloat16)
    part[...] = mm(seeds, x_ref[...], ((0,), (0,))).T
    loop(1, peers, lambda offset: part_copy(offset).start())
    part_in[0] = part[mine, :]
    loop(1, peers, lambda offset: part_copy(offset).wait_recv())
    total = part_in[0]
    for offset in range(1, peers):
        total = total + part_in[offset]
    mixed_s[me, mine, :] = (total * mix_scale).astype(jnp.bfloat16)

    def spread(b):
        loop(1, peers, lambda offset: mixed_share(b, offset).start())

    def spread_from(offset):
        mixed_along(offset).wait_recv()
        spread(seq_at(shards - offset)[0])

    def gathered(b):
        loop(1, peers, lambda offset: mixed_share(b, offset).wait_recv())

    loop(1, shards, lambda offset: mixed_along(offset).start())
    spread(me)
    send_own(early, kv_heads)
    loads[2].wait()
    loads[3].wait()
    for h in reversed(range(kv_heads - folds, kv_heads)):
        send_folded(h)
    loop(1, shards, spread_from)

    def first_pass(h, row, qh, gh, d, c, row0, kind):
        rows = tokens - row0
        kk = kv[h, row - d, 0, pl.ds(c * CHUNK, CHUNK), :]
        vv = kv[h, row - d, 1, pl.ds(c * CHUNK, CHUNK), :]
        mixed = mixed_s[row - d, pl.ds(c * CHUNK, CHUNK), :]
        scores = mm(qh[row0:], kk, ((1,), (1,)))
        weight = mm(gh[row0:], vv, ((1,), (1,)))
        bounded = jnp.tanh(scores * (QUERY_SCALE / CAP))
        power = jnp.exp2(bounded * (CAP / math.log(2.0)))
        if kind is not None:
            qi = row0 + lax.broadcasted_iota(jnp.int32, (rows, CHUNK), 0)
            kj = c * CHUNK + lax.broadcasted_iota(jnp.int32, (rows, CHUNK), 1)
            keep = qi >= kj if kind == "causal" else qi < kj
            power = jnp.where(keep, power, 0.0)
        slot = d * chunks + c
        pg_s[slot, pl.ds(row0, rows), :] = power - power * (bounded * bounded)
        w_s[slot, pl.ds(row0, rows), :] = weight
        pw = power * weight
        at = pl.ds(row0, rows)
        z_s[at, :] += power[:, :HEAD] + power[:, HEAD:]
        dn_s[at, :] += pw[:, :HEAD] + pw[:, HEAD:]
        pm_s[at, :] += mm(power.astype(jnp.bfloat16), mixed, ((1,), (0,)))

    def second_pass(h, row, d, c, row0):
        rows = tokens - row0
        at = pl.ds(row0, rows)
        slot = d * chunks + c
        kk = kv[h, row - d, 0, pl.ds(c * CHUNK, CHUNK), :]
        mixed = mixed_s[row - d, pl.ds(c * CHUNK, CHUNK), :]
        dot = db_s[at, :]
        grad = pg_s[slot, at, :] * (w_s[slot, at, :] - jnp.concatenate([dot, dot], 1))
        acc_s[at, :] += mm(
            grad.astype(jnp.bfloat16), jnp.concatenate([kk, mixed], 1), ((1,), (0,))
        )

    full = reach if reach < reach_full else reach_full - 1

    def each_block(row, fn):
        for c in range(chunks):
            fn(0, c, c * CHUNK, "causal")

        def step(d, carry):
            for c in range(chunks):
                fn(d, c, 0, None)
            return carry

        lax.fori_loop(1, jnp.minimum(row, full) + 1, step, 0)
        if full < reach:
            @pl.when(row >= reach)
            def _():
                for c in range(chunks):
                    fn(reach, c, 0, "window")

    def arrivals(h):
        def arrive(d):
            hop(h, me - d).wait_recv()

            @pl.when((me < last(h)) & (d < reach))
            def _():
                hop(h, me - d).start()

        @pl.when(me <= last(h))
        def _():
            loop(1, blocks + 1, arrive)

    def pass_folded():
        for folded in reversed(range(kv_heads - folds, kv_heads)):
            for row in range(shards - folds + 1, shards):
                @pl.when((me > last(folded)) & (me < row))
                def _():
                    hop(folded, row, -1).wait_recv()
                    hop(folded, row, -1).start()
                    row_hop(folded, row).wait_recv()
                    row_hop(folded, row).start()

    def kv_head(h, carry):
        @pl.when((h > 1) | ((h == 1) & (me != 1)))
        def _():
            arrivals(h)

        count = jnp.where(me < last(h), 1, jnp.where(me == last(h), shards - last(h), 0))
        loop(0, count, lambda extra: row_task(h, me + extra, extra))

        @pl.when(me <= last(h))
        def _():
            stage[h] = sketch[h].astype(stage.dtype)
            loop(1, shards, lambda offset: row_copy(h, offset).start())

        return carry

    def row_task(h, row, extra):
        if folds > 0:
            @pl.when(extra > 0)
            def _():
                hop(h, row, -1).wait_recv()
                row_hop(h, row).wait_recv()
                at = (h - (kv_heads - folds), row - (shards - folds))
                for member in range(groups):
                    q_t[member] = qg[at + (0, slice(None), pl.ds(member * HEAD, HEAD))]
                    q_t[groups + member] = qg[at + (1, slice(None), pl.ds(member * HEAD, HEAD))]

        @pl.when(extra == 0)
        def _():
            for member in range(groups):
                q_t[member] = q_ref[:, cols(h * groups + member)]
                q_t[groups + member] = g_ref[:, cols(h * groups + member)]

        own_mixed = mixed_s[row]

        def member_step(member, inner):
            qh = q_t[member]
            gh = q_t[groups + member]
            z_s[...] = jnp.zeros_like(z_s)
            dn_s[...] = jnp.zeros_like(dn_s)
            pm_s[...] = jnp.zeros_like(pm_s)
            acc_s[...] = jnp.zeros_like(acc_s)
            each_block(row, lambda d, c, row0, kind: first_pass(h, row, qh, gh, d, c, row0, kind))
            inverse = 1.0 / jnp.sum(z_s[...], axis=1, keepdims=True)
            dot = jnp.sum(dn_s[...], axis=1, keepdims=True) * inverse
            db_s[...] = jnp.broadcast_to(dot, db_s.shape)
            each_block(row, lambda d, c, row0, kind: second_pass(h, row, d, c, row0))
            scale = inverse * QUERY_SCALE
            dq = (acc_s[:, :HEAD] * scale).astype(jnp.bfloat16)
            dm = (acc_s[:, HEAD:] * scale).astype(jnp.bfloat16)
            pm = (pm_s[...] * inverse).astype(jnp.bfloat16)
            q_part = mm(own_mixed, dq, ((0,), (0,)))
            k_part = mm(dm, qh, ((0,), (0,)))
            v_part = mm(pm, gh, ((0,), (0,)))
            blocked = (shards, own_rows, HEAD)
            sketch[h, :, :, cols(2 + member)] += q_part.reshape(blocked)
            sketch[h, :, :, :HEAD] += k_part.reshape(blocked)
            sketch[h, :, :, HEAD : 2 * HEAD] += v_part.reshape(blocked)
            return inner

        lax.fori_loop(0, groups, member_step, 0)

    sketch[...] = jnp.zeros_like(sketch)
    own_rows = sketch.shape[2]
    arrivals(0)
    pass_folded()
    if kv_heads > 1:
        @pl.when(me == 1)
        def _():
            arrivals(1)

    loop(0, shards, gathered)
    lax.fori_loop(0, kv_heads, kv_head, 0)

    def collect(h):
        def add(offset):
            @pl.when(seq_at(shards - offset)[0] <= last(h))
            def _():
                row_copy(h, offset).wait_recv()
                sketch[h, me] += stage_in[h, offset].astype(jnp.float32)

        loop(1, shards, add)
        rows = sketch[h, me]
        ok_ref[:, cols(h)] = rows[:, :HEAD]
        ov_ref[:, cols(h)] = rows[:, HEAD : 2 * HEAD]
        for member in range(groups):
            oq_ref[:, cols(h * groups + member)] = rows[:, (2 + member) * HEAD : (3 + member) * HEAD]

    loop(0, kv_heads, collect)

    loop(1, peers, lambda offset: part_copy(offset).wait_send())
    loop(1, shards, lambda offset: mixed_along(offset).wait_send())
    loop(0, shards, lambda b: loop(1, peers, lambda offset: mixed_share(b, offset).wait_send()))

    def drain_rows(h):
        @pl.when(me <= last(h))
        def _():
            loop(1, shards, lambda offset: row_copy(h, offset).wait_send())

    loop(0, kv_heads, drain_rows)

    def drain(h):
        @pl.when(me < last(h))
        def _():
            loop(0, jnp.minimum(me, reach - 1) + 1, lambda d: hop(h, me - d).wait_send())

    if reach > 0:
        loop(0, kv_heads, drain)
    for h in range(kv_heads - folds, kv_heads):
        for row in range(shards - folds, shards):
            @pl.when((me > last(h)) & (me <= row))
            def _():
                hop(h, row, -1).wait_send()
                row_hop(h, row).wait_send()


STEP_H, STEP_B, STEP_ROW, STEP_SLOT, STEP_HALF = 1, 4, 16, 64, 512
INIT, FINAL, SEND, WAIT_KV, PASS_KV, WAIT_Q, RELAY = (1024 << i for i in range(7))
FOREIGN = 4


def step_of(h, b, row, slot, half, *flags):
    return h * STEP_H + b * STEP_B + row * STEP_ROW + slot * STEP_SLOT + half * STEP_HALF + sum(flags)


STEPS = (
    [step_of(h, 0, 0, h, 0, INIT, FINAL, SEND) for h in range(4)],
    [
        code
        for h in range(4)
        for code in (
            step_of(h, 1, 1, h, 0, INIT),
            step_of(h, 0, 1, h, 0, FINAL, WAIT_KV, *((PASS_KV,) if h < 3 else (SEND,))),
        )
    ]
    + [
        step_of(3, 1, 2, 4, 0, INIT, WAIT_Q),
        step_of(3, 0, 2, 4, 0),
        step_of(3, 2, 2, 4, 0, WAIT_KV, FINAL),
        step_of(3, 1, 3, 5, 0, INIT, WAIT_Q),
        step_of(3, 0, 3, 5, 0),
        step_of(3, 2, 3, 5, 0),
        step_of(3, 3, 3, 5, 0, WAIT_KV, FINAL, SEND),
    ],
    [
        step_of(0, 2, 2, 0, 0, INIT),
        step_of(0, 1, 2, 0, 0, WAIT_KV, PASS_KV),
        step_of(1, 2, 2, 1, 1, INIT),
        step_of(1, 1, 2, 1, 1, WAIT_KV, PASS_KV),
        step_of(0, 0, 2, 0, 0, WAIT_KV, PASS_KV, RELAY, FINAL, SEND),
        step_of(1, 0, 2, 1, 1, WAIT_KV, PASS_KV, FINAL, SEND),
        step_of(2, 2, 2, 2, 0, INIT),
        step_of(2, 2, 3, 4, 1, INIT, WAIT_Q),
        step_of(2, 1, 2, 2, 0, WAIT_KV),
        step_of(2, 1, 3, 4, 1),
        step_of(2, 3, 3, 4, 1, WAIT_KV),
        step_of(2, 0, 2, 2, 0, WAIT_KV, FINAL),
        step_of(2, 0, 3, 4, 1, FINAL, SEND),
    ],
    [
        step_of(0, 3, 3, 0, 0, INIT),
        step_of(1, 3, 3, 1, 1, INIT),
        step_of(0, 2, 3, 0, 0, WAIT_KV),
        step_of(1, 2, 3, 1, 1, WAIT_KV),
        step_of(0, 1, 3, 0, 0, WAIT_KV),
        step_of(1, 1, 3, 1, 1, WAIT_KV),
        step_of(0, 0, 3, 0, 0, WAIT_KV, FINAL, SEND),
        step_of(1, 0, 3, 1, 1, WAIT_KV, FINAL, SEND),
    ],
)


def balanced_kernel(
    subs, peers, mix_scale,
    q_hbm, k_hbm, v_hbm, g_hbm, x_hbm, seed_hbm, oq_ref, ok_ref, ov_ref,
    x_ref, seed_ref, qg, kv, pg_s, w_s, z_s, dn_s, pm_s, acc_s, db_s,
    part, part_in, mixed_s, sketch, stage, stage_in, fold_in,
    kv_send, kv_recv, q_send, q_recv, part_send, part_recv, hop_send, hop_recv,
    share_send, share_recv, row_send, row_recv, fold_send, fold_recv, load_sem,
):
    shards, kv_heads = 4, 4
    tokens = qg.shape[3]
    groups = qg.shape[2]
    chunks = tokens // CHUNK
    share = tokens // peers
    own_rows = sketch.shape[2]
    me = lax.axis_index("seq")
    peer = lax.axis_index("head") * subs + lax.axis_index("sub")

    def cols(head):
        return pl.ds(pl.multiple_of(head * HEAD, HEAD), HEAD)

    def peer_at(offset):
        other = lax.rem(peer + offset, peers)
        return other, {"head": lax.div(other, subs), "sub": lax.rem(other, subs)}

    def seq_at(offset):
        other = lax.rem(me + offset, shards)
        return other, {"seq": other}

    def remote(src, dst, send, recv, device):
        return pltpu.make_async_remote_copy(
            src_ref=src, dst_ref=dst, send_sem=send, recv_sem=recv,
            device_id=device, device_id_type=MESH,
        )

    def loop(low, high, fn):
        def step(i, carry):
            fn(i)
            return carry

        lax.fori_loop(low, high, step, 0)

    def kv_hop(h, b, way=1):
        return remote(
            kv.at[h, b], kv.at[h, b], kv_send.at[h, b], kv_recv.at[h, b], {"seq": me + way}
        )

    def q_hop(source, target):
        at = target - FOREIGN
        return remote(
            qg.at[source], qg.at[target], q_send.at[at], q_recv.at[at], {"seq": me - 1}
        )

    def part_copy(offset):
        other, device = peer_at(offset)
        rows = pl.ds(pl.multiple_of(other * share, share), share)
        return remote(
            part.at[rows], part_in.at[offset], part_send.at[offset], part_recv.at[offset], device
        )

    mine = pl.ds(pl.multiple_of(peer * share, share), share)

    def mixed_along(offset):
        _, device = seq_at(offset)
        return remote(
            mixed_s.at[me, mine], mixed_s.at[me, mine], hop_send.at[offset], hop_recv.at[offset],
            device,
        )

    def mixed_share(b, offset):
        _, device = peer_at(offset)
        return remote(
            mixed_s.at[b, mine], mixed_s.at[b, mine], share_send.at[b, offset],
            share_recv.at[b, offset], device,
        )

    def row_copy(h, target, sender):
        return remote(
            stage.at[h, target], stage_in.at[h, sender], row_send.at[h, target],
            row_recv.at[h, sender], {"seq": target},
        )

    def fold_copy(h):
        return remote(
            stage.at[h, pl.ds(1, shards - 1)], fold_in.at[h], fold_send.at[h], fold_recv.at[h],
            {"seq": 1},
        )

    barrier = pltpu.get_barrier_semaphore()

    def greet_peer(offset):
        pl.semaphore_signal(barrier, inc=1, device_id=peer_at(offset)[1], device_id_type=MESH)

    def greet_seq(offset):
        pl.semaphore_signal(barrier, inc=1, device_id=seq_at(offset)[1], device_id_type=MESH)

    loop(1, peers, greet_peer)
    loop(1, shards, greet_seq)

    def load_kv(h, which):
        source = (k_hbm, v_hbm)[which]
        return pltpu.make_async_copy(
            source.at[:, cols(h)], kv.at[h, me, which], load_sem.at[2 + which * kv_heads + h]
        )

    def load_qg(h, which, member):
        source = (q_hbm, g_hbm)[which]
        at = 2 + 2 * kv_heads + (h * 2 + which) * groups + member
        return pltpu.make_async_copy(
            source.at[:, cols(h * groups + member)], qg.at[h, which, member], load_sem.at[at]
        )

    load_seed = pltpu.make_async_copy(seed_hbm, seed_ref, load_sem.at[0])
    load_x = pltpu.make_async_copy(x_hbm, x_ref, load_sem.at[1])

    def each_kv(fn):
        for which in range(2):
            loop(0, kv_heads, lambda h: fn(load_kv(h, which)))

    def each_qg(fn):
        for which in range(2):
            for member in range(groups):
                loop(0, kv_heads, lambda h: fn(load_qg(h, which, member)))

    each_kv(lambda copy: copy.start())
    load_seed.start()
    load_x.start()
    each_qg(lambda copy: copy.start())
    each_kv(lambda copy: copy.wait())
    pl.semaphore_wait(barrier, peers + shards - 2)

    @pl.when(me < 3)
    def _():
        kv_hop(0, me).start()

    @pl.when(me > 1)
    def _():
        kv_hop(3, me, -1).start()

    load_seed.wait()
    load_x.wait()
    seeds = seed_ref[...].astype(jnp.float32).astype(jnp.bfloat16)
    part[...] = mm(seeds, x_ref[...], ((0,), (0,))).T
    loop(1, peers, lambda offset: part_copy(offset).start())
    part_in[0] = part[mine, :]
    loop(1, peers, lambda offset: part_copy(offset).wait_recv())
    total = part_in[0]
    for offset in range(1, peers):
        total = total + part_in[offset]
    mixed_s[me, mine, :] = (total * mix_scale).astype(jnp.bfloat16)

    def spread(b):
        loop(1, peers, lambda offset: mixed_share(b, offset).start())

    def spread_from(offset):
        mixed_along(offset).wait_recv()
        spread(seq_at(shards - offset)[0])

    def gathered(b):
        loop(1, peers, lambda offset: mixed_share(b, offset).wait_recv())

    loop(1, shards, lambda offset: mixed_along(offset).start())
    spread(me)
    each_qg(lambda copy: copy.wait())

    @pl.when(me == 0)
    def _():
        loop(1, kv_heads, lambda h: kv_hop(h, 0).start())

    @pl.when(me == 1)
    def _():
        kv_hop(1, 1).start()

    @pl.when(me == 2)
    def _():
        kv_hop(1, 2).start()
        q_hop(3, 4).start()

    @pl.when(me == 3)
    def _():
        q_hop(3, 5).start()
        q_hop(2, 4).start()
        kv_hop(2, 3, -1).start()

    sketch[...] = jnp.zeros_like(sketch)

    def first_pass(h, b, slot, half, d, c, row0, causal):
        rows = tokens - row0
        at = pl.ds(row0, rows)
        keys = pl.ds(c * CHUNK, CHUNK)
        qh = qg[slot, 0, :, at, :].reshape(groups * rows, HEAD)
        gh = qg[slot, 1, :, at, :].reshape(groups * rows, HEAD)
        scores = mm(qh, kv[h, b, 0, keys, :], ((1,), (1,)))
        weight = mm(gh, kv[h, b, 1, keys, :], ((1,), (1,)))
        bounded = jnp.tanh(scores * (QUERY_SCALE / CAP))
        power = jnp.exp2(bounded * (CAP / math.log(2.0)))
        if causal:
            qi = lax.broadcasted_iota(jnp.int32, (groups, rows, CHUNK), 1)
            kj = lax.broadcasted_iota(jnp.int32, (groups, rows, CHUNK), 2)
            keep = (row0 + qi >= c * CHUNK + kj).reshape(groups * rows, CHUNK)
            power = jnp.where(keep, power, 0.0)
        whole = (groups, rows, CHUNK)
        folded = (groups, rows, HEAD)
        put = half * shards + d
        pg_s[put, c, :, at, :] = (power - power * (bounded * bounded)).reshape(whole)
        w_s[put, c, :, at, :] = weight.reshape(whole)
        pw = power * weight
        z_s[half, :, at, :] += (power[:, :HEAD] + power[:, HEAD:]).reshape(folded)
        dn_s[half, :, at, :] += (pw[:, :HEAD] + pw[:, HEAD:]).reshape(folded)
        pm = mm(power.astype(jnp.bfloat16), mixed_s[b, keys, :], ((1,), (0,)))
        pm_s[half, :, at, :] += pm.reshape(folded)

    def second_pass(h, b, half, d, c, row0):
        rows = tokens - row0
        at = pl.ds(row0, rows)
        keys = pl.ds(c * CHUNK, CHUNK)
        put = half * shards + d
        dot = db_s[:, at, :]
        grad = pg_s[put, c, :, at, :] * (w_s[put, c, :, at, :] - jnp.concatenate([dot, dot], 2))
        sides = jnp.concatenate([kv[h, b, 0, keys, :], mixed_s[b, keys, :]], 1)
        term = mm(grad.astype(jnp.bfloat16).reshape(groups * rows, CHUNK), sides, ((1,), (0,)))
        acc_s[:, at, :] += term.reshape(groups, rows, 2 * HEAD)

    def finish_row(h, row, slot, half):
        inverse = 1.0 / jnp.sum(z_s[half], axis=2, keepdims=True)
        dot = jnp.sum(dn_s[half], axis=2, keepdims=True) * inverse
        db_s[...] = jnp.broadcast_to(dot, db_s.shape)
        acc_s[...] = jnp.zeros_like(acc_s)
        for c in range(chunks):
            second_pass(h, row, half, 0, c, c * CHUNK)

        def rest(d):
            for c in range(chunks):
                second_pass(h, row - d, half, d, c, 0)

        loop(1, row + 1, rest)
        scale = inverse * QUERY_SCALE
        dq = (acc_s[:, :, :HEAD] * scale).astype(jnp.bfloat16)
        dm = (acc_s[:, :, HEAD:] * scale).astype(jnp.bfloat16)
        pm = (pm_s[half] * inverse).astype(jnp.bfloat16)
        stacked = (groups * tokens, HEAD)
        blocked = (shards, own_rows, HEAD)
        k_part = mm(dm.reshape(stacked), qg[slot, 0].reshape(stacked), ((0,), (0,)))
        v_part = mm(pm.reshape(stacked), qg[slot, 1].reshape(stacked), ((0,), (0,)))
        sketch[h, :, :, :HEAD] += k_part.reshape(blocked)
        sketch[h, :, :, HEAD : 2 * HEAD] += v_part.reshape(blocked)
        q_part = mm(mixed_s[row], jnp.concatenate([dq[m] for m in range(groups)], 1), ((0,), (0,)))
        sketch[h, :, :, 2 * HEAD :] += q_part.reshape(shards, own_rows, groups * HEAD)

    def send_head(h):
        @pl.when(me == 1)
        def _():
            fold_copy(h).wait_recv()
            sketch[h, pl.ds(1, shards - 1)] += fold_in[h].astype(jnp.float32)

        stage[h] = sketch[h].astype(stage.dtype)

        @pl.when(me == 0)
        def _():
            fold_copy(h).start()

        @pl.when(me > 0)
        def _():
            loop(1, shards, lambda offset: row_copy(h, seq_at(offset)[0], me).start())

    def one_step(index):
        code = jnp.int32(0)
        for shard, codes in enumerate(STEPS):
            for i, value in enumerate(codes):
                code = jnp.where((me == shard) & (index == i), value, code)

        def field(unit, size):
            return lax.rem(lax.div(code, unit), size)

        def flag(unit):
            return field(unit, 2) == 1

        h, b, row = field(STEP_H, 4), field(STEP_B, 4), field(STEP_ROW, 4)
        slot, half = field(STEP_SLOT, 8), field(STEP_HALF, 2)

        @pl.when(index == 1)
        def _():
            loop(1, shards, spread_from)
            loop(1, shards, lambda offset: gathered(seq_at(offset)[0]))

        @pl.when(flag(WAIT_Q))
        def _():
            q_hop(slot, slot).wait_recv()

        @pl.when(flag(WAIT_KV))
        def _():
            kv_hop(h, b).wait_recv()

        @pl.when(flag(PASS_KV))
        def _():
            kv_hop(h, b).start()

            @pl.when((me == 1) & (h == 1))
            def _():
                kv_hop(2, 1).start()

        @pl.when(flag(RELAY))
        def _():
            q_hop(5, 5).wait_recv()
            q_hop(5, 5).start()
            kv_hop(3, 3, -1).wait_recv()
            kv_hop(3, 3, -1).start()

        @pl.when(flag(INIT))
        def _():
            z_s[half] = jnp.zeros(z_s.shape[1:], z_s.dtype)
            dn_s[half] = jnp.zeros(dn_s.shape[1:], dn_s.dtype)
            pm_s[half] = jnp.zeros(pm_s.shape[1:], pm_s.dtype)

        @pl.when(b == row)
        def _():
            for c in range(chunks):
                first_pass(h, b, slot, half, 0, c, c * CHUNK, True)

        @pl.when(b != row)
        def _():
            for c in range(chunks):
                first_pass(h, b, slot, half, row - b, c, 0, False)

        @pl.when(flag(FINAL))
        def _():
            finish_row(h, row, slot, half)

        @pl.when(flag(SEND))
        def _():
            held = (me == 1) & (row == 1)
            loop(jnp.where(held, 0, h), jnp.where(held, h, h + 1), send_head)

    gathered(me)
    count = jnp.int32(0)
    for shard, codes in enumerate(STEPS):
        count = jnp.where(me == shard, len(codes), count)
    loop(0, count, one_step)

    def heads_of(sender):
        return jnp.where(sender == 2, 3, jnp.where(sender == 3, 2, jnp.where(sender == 1, 4, 0)))

    def collect(h):
        def add(sender):
            @pl.when((sender != me) & (h < heads_of(sender)))
            def _():
                row_copy(h, me, sender).wait_recv()
                sketch[h, me] += stage_in[h, sender].astype(jnp.float32)

        loop(1, shards, add)
        rows = sketch[h, me]
        ok_ref[:, cols(h)] = rows[:, :HEAD]
        ov_ref[:, cols(h)] = rows[:, HEAD : 2 * HEAD]
        for member in range(groups):
            oq_ref[:, cols(h * groups + member)] = rows[:, (2 + member) * HEAD : (3 + member) * HEAD]

    loop(0, kv_heads, collect)

    loop(1, peers, lambda offset: part_copy(offset).wait_send())
    loop(1, shards, lambda offset: mixed_along(offset).wait_send())
    loop(0, shards, lambda b: loop(1, peers, lambda offset: mixed_share(b, offset).wait_send()))
    loop(
        0, heads_of(me),
        lambda h: loop(1, shards, lambda offset: row_copy(h, seq_at(offset)[0], me).wait_send()),
    )

    @pl.when(me == 0)
    def _():
        loop(0, kv_heads, lambda h: fold_copy(h).wait_send())

    up = jnp.where(me == 0, 4, jnp.where(me == 1, 3, jnp.where(me == 2, 2, 0)))
    loop(0, up, lambda h: loop(0, me + 1, lambda b: kv_hop(h, b).wait_send()))

    @pl.when(me == 2)
    def _():
        kv_hop(3, 2, -1).wait_send()
        kv_hop(3, 3, -1).wait_send()
        q_hop(3, 4).wait_send()
        q_hop(5, 5).wait_send()

    @pl.when(me == 3)
    def _():
        kv_hop(3, 3, -1).wait_send()
        kv_hop(2, 3, -1).wait_send()
        q_hop(3, 5).wait_send()
        q_hop(2, 4).wait_send()


def balanced(queries, key_states, value_states, out_grad, layer_inputs, sketch_seeds):
    tokens, query_width = queries.shape
    kv_width = key_states.shape[1]
    kv_heads = kv_width // HEAD
    groups = query_width // kv_width
    shards = lax.axis_size("seq")
    subs = lax.axis_size("sub")
    peers = lax.axis_size("head") * subs
    features = layer_inputs.shape[0]
    rank = sketch_seeds.shape[1]
    chunks = tokens // CHUNK
    own_rows = rank // shards
    width = (groups + 2) * HEAD
    f32, bf16, dma = jnp.float32, jnp.bfloat16, pltpu.SemaphoreType.DMA
    return pl.pallas_call(
        functools.partial(balanced_kernel, subs, peers, (2.0 * D * tokens * shards) ** (-0.5)),
        out_shape=(
            jax.ShapeDtypeStruct((own_rows, query_width), f32),
            jax.ShapeDtypeStruct((own_rows, kv_width), f32),
            jax.ShapeDtypeStruct((own_rows, kv_width), f32),
        ),
        in_specs=[pl.BlockSpec(memory_space=pltpu.HBM)] * 6,
        out_specs=(pl.BlockSpec(memory_space=pltpu.VMEM),) * 3,
        scratch_shapes=[
            pltpu.VMEM((features, tokens), bf16),
            pltpu.VMEM((features, rank), sketch_seeds.dtype),
            pltpu.VMEM((kv_heads + 2, 2, groups, tokens, HEAD), bf16),
            pltpu.VMEM((kv_heads, shards, 2, tokens, HEAD), bf16),
            pltpu.VMEM((2 * shards, chunks, groups, tokens, CHUNK), f32),
            pltpu.VMEM((2 * shards, chunks, groups, tokens, CHUNK), f32),
            pltpu.VMEM((2, groups, tokens, HEAD), f32),
            pltpu.VMEM((2, groups, tokens, HEAD), f32),
            pltpu.VMEM((2, groups, tokens, rank), f32),
            pltpu.VMEM((groups, tokens, HEAD + rank), f32),
            pltpu.VMEM((groups, tokens, HEAD), f32),
            pltpu.VMEM((tokens, rank), f32),
            pltpu.VMEM((peers, tokens // peers, rank), f32),
            pltpu.VMEM((shards, tokens, rank), bf16),
            pltpu.VMEM((kv_heads, shards, own_rows, width), f32),
            pltpu.VMEM((kv_heads, shards, own_rows, width), bf16),
            pltpu.VMEM((kv_heads, shards, own_rows, width), bf16),
            pltpu.VMEM((kv_heads, shards - 1, own_rows, width), bf16),
            dma((kv_heads, shards)), dma((kv_heads, shards)),
            dma((2,)), dma((2,)),
            dma((peers,)), dma((peers,)),
            dma((shards,)), dma((shards,)),
            dma((shards, peers)), dma((shards, peers)),
            dma((kv_heads, shards)), dma((kv_heads, shards)),
            dma((kv_heads,)), dma((kv_heads,)),
            dma((2 + 2 * kv_heads * (1 + groups),)),
        ],
        compiler_params=pltpu.CompilerParams(
            collective_id=0, has_side_effects=True, vmem_limit_bytes=62 * 2**20
        ),
    )(queries, key_states, value_states, out_grad, layer_inputs, sketch_seeds)


def per_device(queries, key_states, value_states, out_grad, layer_inputs, sketch_seeds):
    tokens, query_width = queries.shape
    kv_width = key_states.shape[1]
    kv_heads = kv_width // HEAD
    shards = lax.axis_size("seq")
    length = tokens * shards
    reach_full = WINDOW // tokens
    reach = min(reach_full, shards - 1)
    rank = sketch_seeds.shape[1]
    subs = lax.axis_size("sub")
    peers = lax.axis_size("head") * subs
    groups = query_width // kv_width
    if shards == 4 and kv_heads == 4 and reach < reach_full and tokens == 2 * CHUNK:
        return balanced(queries, key_states, value_states, out_grad, layer_inputs, sketch_seeds)
    folds = 0
    features = layer_inputs.shape[0]
    slots = (reach + 1) * (tokens // CHUNK)
    own_rows = rank // shards
    width = (query_width + 2 * kv_width) // kv_heads
    f32, bf16, dma = jnp.float32, jnp.bfloat16, pltpu.SemaphoreType.DMA
    return pl.pallas_call(
        functools.partial(
            attention_kernel, shards, reach_full, reach, folds, subs, peers,
            (2.0 * D * length) ** (-0.5),
        ),
        out_shape=(
            jax.ShapeDtypeStruct((own_rows, query_width), f32),
            jax.ShapeDtypeStruct((own_rows, kv_width), f32),
            jax.ShapeDtypeStruct((own_rows, kv_width), f32),
        ),
        in_specs=[pl.BlockSpec(memory_space=pltpu.HBM)] * 6,
        out_specs=(pl.BlockSpec(memory_space=pltpu.VMEM),) * 3,
        scratch_shapes=[
            pltpu.VMEM((tokens, query_width), bf16),
            pltpu.VMEM((tokens, query_width), bf16),
            pltpu.VMEM((features, tokens), bf16),
            pltpu.VMEM((features, rank), sketch_seeds.dtype),
            pltpu.VMEM((max(folds, 1), max(folds, 1), 2, tokens, groups * HEAD), bf16),
            pltpu.VMEM((2 * groups, tokens, HEAD), bf16),
            pltpu.VMEM((kv_heads, shards, 2, tokens, HEAD), bf16),
            pltpu.VMEM((slots, tokens, CHUNK), f32),
            pltpu.VMEM((slots, tokens, CHUNK), f32),
            pltpu.VMEM((tokens, HEAD), f32),
            pltpu.VMEM((tokens, HEAD), f32),
            pltpu.VMEM((tokens, rank), f32),
            pltpu.VMEM((tokens, HEAD + rank), f32),
            pltpu.VMEM((tokens, HEAD), f32),
            pltpu.VMEM((tokens, rank), f32),
            pltpu.VMEM((peers, tokens // peers, rank), f32),
            pltpu.VMEM((shards, tokens, rank), bf16),
            pltpu.VMEM((kv_heads, shards, own_rows, width), f32),
            pltpu.VMEM((kv_heads, shards, own_rows, width), bf16),
            pltpu.VMEM((kv_heads, shards, own_rows, width), bf16),
            dma((kv_heads, shards)), dma((kv_heads, shards)),
            dma((peers,)), dma((peers,)),
            dma((shards,)), dma((shards,)),
            dma((shards, peers)), dma((shards, peers)),
            dma((kv_heads, shards)), dma((kv_heads, shards)),
            dma((max(folds, 1), max(folds, 1))), dma((max(folds, 1), max(folds, 1))),
            dma((4 + 2 * kv_heads,)),
        ],
        compiler_params=pltpu.CompilerParams(
            collective_id=0, has_side_effects=True, vmem_limit_bytes=62 * 2**20
        ),
    )(queries, key_states, value_states, out_grad, layer_inputs, sketch_seeds)


def solution(mesh):
    placed = (
        P(("group", "seq"), ("head", "sub")),
        P(("group", "seq"), ("head", "sub")),
        P(("group", "seq"), ("head", "sub")),
        P(("group", "seq"), ("head", "sub")),
        P(("head", "sub"), ("group", "seq")),
        P(("head", "sub"), None),
    )
    return jax.shard_map(
        per_device,
        mesh=mesh,
        in_specs=placed,
        out_specs=(
            P(("group", "seq"), ("head", "sub")),
            P(("group", "seq"), ("head", "sub")),
            P(("group", "seq"), ("head", "sub")),
        ),
        check_vma=False,
    )
```

```python
import functools
import math

import jax
import jax.numpy as jnp
from jax import lax
from jax.experimental import pallas as pl
from jax.experimental.pallas import tpu as pltpu
from jax.sharding import PartitionSpec as P

D = 4608
HEAD = 128
WINDOW = 2048
CAP = 50.0
QUERY_SCALE = 144.0 ** (-0.5)
CHUNK = 256
MESH = pl.DeviceIdType.MESH


def mm(left, right, dims):
    return lax.dot_general(left, right, (dims, ((), ())), preferred_element_type=jnp.float32)


def attention_kernel(
    shards, reach_full, reach, folds, subs, peers, mix_scale,
    q_hbm, k_hbm, v_hbm, g_hbm, x_hbm, seed_hbm, oq_ref, ok_ref, ov_ref,
    q_ref, g_ref, x_ref, seed_ref, qg, q_t, kv, pg_s, w_s, z_s, dn_s, pm_s, acc_s, db_s,
    part, part_in, mixed_s, sketch, stage, stage_in,
    send_sem, recv_sem, part_send, part_recv, hop_send, hop_recv, share_send, share_recv,
    row_send, row_recv, qg_send, qg_recv, load_sem,
):
    tokens = q_ref.shape[0]
    query_width = q_ref.shape[1]
    kv_width = k_hbm.shape[1]
    kv_heads = kv_width // HEAD
    groups = query_width // kv_width
    chunks = tokens // CHUNK
    share = tokens // peers
    me = lax.axis_index("seq")
    peer = lax.axis_index("head") * subs + lax.axis_index("sub")
    blocks = jnp.minimum(me, reach)

    def last(h):
        return shards - 1 - jnp.maximum(h - (kv_heads - 1 - folds), 0)


    def cols(head):
        return pl.ds(pl.multiple_of(head * HEAD, HEAD), HEAD)

    def peer_at(offset):
        other = lax.rem(peer + offset, peers)
        return other, {"head": lax.div(other, subs), "sub": lax.rem(other, subs)}

    def seq_at(offset):
        other = lax.rem(me + offset, shards)
        return other, {"seq": other}

    def remote(src, dst, send, recv, device):
        return pltpu.make_async_remote_copy(
            src_ref=src, dst_ref=dst, send_sem=send, recv_sem=recv,
            device_id=device, device_id_type=MESH,
        )

    def loop(low, high, fn):
        def step(i, carry):
            fn(i)
            return carry

        lax.fori_loop(low, high, step, 0)

    def hop(h, b, way=1):
        return remote(
            kv.at[h, b], kv.at[h, b], send_sem.at[h, b], recv_sem.at[h, b], {"seq": me + way}
        )

    def row_hop(h, row):
        at = (h - (kv_heads - folds), row - (shards - folds))
        return remote(
            qg.at[at], qg.at[at], qg_send.at[at], qg_recv.at[at], {"seq": me - 1}
        )

    def part_copy(offset):
        other, device = peer_at(offset)
        rows = pl.ds(pl.multiple_of(other * share, share), share)
        return remote(
            part.at[rows], part_in.at[offset], part_send.at[offset], part_recv.at[offset], device
        )

    mine = pl.ds(pl.multiple_of(peer * share, share), share)

    def mixed_along(offset):
        _, device = seq_at(offset)
        return remote(
            mixed_s.at[me, mine], mixed_s.at[me, mine], hop_send.at[offset], hop_recv.at[offset],
            device,
        )

    def mixed_share(b, offset):
        _, device = peer_at(offset)
        return remote(
            mixed_s.at[b, mine], mixed_s.at[b, mine], share_send.at[b, offset],
            share_recv.at[b, offset], device,
        )

    def row_copy(h, offset):
        other, device = seq_at(offset)
        return remote(
            stage.at[h, other], stage_in.at[h, offset], row_send.at[h, offset],
            row_recv.at[h, offset], device,
        )

    barrier = pltpu.get_barrier_semaphore()

    def greet_peer(offset):
        pl.semaphore_signal(barrier, inc=1, device_id=peer_at(offset)[1], device_id_type=MESH)

    def greet_seq(offset):
        pl.semaphore_signal(barrier, inc=1, device_id=seq_at(offset)[1], device_id_type=MESH)

    loop(1, peers, greet_peer)
    loop(1, shards, greet_seq)
    def load_kv(h, which):
        source = (k_hbm, v_hbm)[which]
        return pltpu.make_async_copy(
            source.at[:, cols(h)], kv.at[h, me, which], load_sem.at[4 + which * kv_heads + h]
        )

    loads = [
        pltpu.make_async_copy(source, target, load_sem.at[i])
        for i, (source, target) in enumerate(
            ((seed_hbm, seed_ref), (x_hbm, x_ref), (q_hbm, q_ref), (g_hbm, g_ref))
        )
    ]
    for h in range(kv_heads):
        load_kv(h, 0).start()
        load_kv(h, 1).start()
    for load in loads:
        load.start()
    for h in range(kv_heads):
        load_kv(h, 0).wait()
        load_kv(h, 1).wait()
    pl.semaphore_wait(barrier, peers + shards - 2)

    early = 1

    def send_own(low, high):
        def one(h):
            @pl.when(me < last(h))
            def _():
                hop(h, me).start()

        if reach > 0:
            loop(low, high, one)

    def send_folded(h):
        @pl.when(me > last(h))
        def _():
            at = (h - (kv_heads - folds), me - (shards - folds))
            width = groups * HEAD
            qg[at + (0,)] = q_ref[:, h * width : (h + 1) * width]
            qg[at + (1,)] = g_ref[:, h * width : (h + 1) * width]
            if h < kv_heads - 1:
                hop(h, me, -1).start()
            row_hop(h, me).start()

    send_own(0, early)
    if folds > 0:
        @pl.when(me > last(kv_heads - 1))
        def _():
            hop(kv_heads - 1, me, -1).start()

    loads[0].wait()
    loads[1].wait()
    seeds = seed_ref[...].astype(jnp.float32).astype(jnp.bfloat16)
    part[...] = mm(seeds, x_ref[...], ((0,), (0,))).T
    loop(1, peers, lambda offset: part_copy(offset).start())
    part_in[0] = part[mine, :]
    loop(1, peers, lambda offset: part_copy(offset).wait_recv())
    total = part_in[0]
    for offset in range(1, peers):
        total = total + part_in[offset]
    mixed_s[me, mine, :] = (total * mix_scale).astype(jnp.bfloat16)

    def spread(b):
        loop(1, peers, lambda offset: mixed_share(b, offset).start())

    def spread_from(offset):
        mixed_along(offset).wait_recv()
        spread(seq_at(shards - offset)[0])

    def gathered(b):
        loop(1, peers, lambda offset: mixed_share(b, offset).wait_recv())

    loop(1, shards, lambda offset: mixed_along(offset).start())
    spread(me)
    send_own(early, kv_heads)
    loads[2].wait()
    loads[3].wait()
    for h in reversed(range(kv_heads - folds, kv_heads)):
        send_folded(h)
    loop(1, shards, spread_from)

    def first_pass(h, row, qh, gh, d, c, row0, kind):
        rows = tokens - row0
        kk = kv[h, row - d, 0, pl.ds(c * CHUNK, CHUNK), :]
        vv = kv[h, row - d, 1, pl.ds(c * CHUNK, CHUNK), :]
        mixed = mixed_s[row - d, pl.ds(c * CHUNK, CHUNK), :]
        scores = mm(qh[row0:], kk, ((1,), (1,)))
        weight = mm(gh[row0:], vv, ((1,), (1,)))
        bounded = jnp.tanh(scores * (QUERY_SCALE / CAP))
        power = jnp.exp2(bounded * (CAP / math.log(2.0)))
        if kind is not None:
            qi = row0 + lax.broadcasted_iota(jnp.int32, (rows, CHUNK), 0)
            kj = c * CHUNK + lax.broadcasted_iota(jnp.int32, (rows, CHUNK), 1)
            keep = qi >= kj if kind == "causal" else qi < kj
            power = jnp.where(keep, power, 0.0)
        slot = d * chunks + c
        pg_s[slot, pl.ds(row0, rows), :] = power - power * (bounded * bounded)
        w_s[slot, pl.ds(row0, rows), :] = weight
        pw = power * weight
        at = pl.ds(row0, rows)
        z_s[at, :] += power[:, :HEAD] + power[:, HEAD:]
        dn_s[at, :] += pw[:, :HEAD] + pw[:, HEAD:]
        pm_s[at, :] += mm(power.astype(jnp.bfloat16), mixed, ((1,), (0,)))

    def second_pass(h, row, d, c, row0):
        rows = tokens - row0
        at = pl.ds(row0, rows)
        slot = d * chunks + c
        kk = kv[h, row - d, 0, pl.ds(c * CHUNK, CHUNK), :]
        mixed = mixed_s[row - d, pl.ds(c * CHUNK, CHUNK), :]
        dot = db_s[at, :]
        grad = pg_s[slot, at, :] * (w_s[slot, at, :] - jnp.concatenate([dot, dot], 1))
        acc_s[at, :] += mm(
            grad.astype(jnp.bfloat16), jnp.concatenate([kk, mixed], 1), ((1,), (0,))
        )

    full = reach if reach < reach_full else reach_full - 1

    def each_block(row, fn):
        for c in range(chunks):
            fn(0, c, c * CHUNK, "causal")

        def step(d, carry):
            for c in range(chunks):
                fn(d, c, 0, None)
            return carry

        lax.fori_loop(1, jnp.minimum(row, full) + 1, step, 0)
        if full < reach:
            @pl.when(row >= reach)
            def _():
                for c in range(chunks):
                    fn(reach, c, 0, "window")

    def arrivals(h):
        def arrive(d):
            hop(h, me - d).wait_recv()

            @pl.when((me < last(h)) & (d < reach))
            def _():
                hop(h, me - d).start()

        @pl.when(me <= last(h))
        def _():
            loop(1, blocks + 1, arrive)

    def pass_folded():
        for folded in reversed(range(kv_heads - folds, kv_heads)):
            for row in range(shards - folds + 1, shards):
                @pl.when((me > last(folded)) & (me < row))
                def _():
                    hop(folded, row, -1).wait_recv()
                    hop(folded, row, -1).start()
                    row_hop(folded, row).wait_recv()
                    row_hop(folded, row).start()

    def kv_head(h, carry):
        @pl.when((h > 1) | ((h == 1) & (me != 1)))
        def _():
            arrivals(h)

        count = jnp.where(me < last(h), 1, jnp.where(me == last(h), shards - last(h), 0))
        loop(0, count, lambda extra: row_task(h, me + extra, extra))

        @pl.when(me <= last(h))
        def _():
            stage[h] = sketch[h].astype(stage.dtype)
            loop(1, shards, lambda offset: row_copy(h, offset).start())

        return carry

    def row_task(h, row, extra):
        if folds > 0:
            @pl.when(extra > 0)
            def _():
                hop(h, row, -1).wait_recv()
                row_hop(h, row).wait_recv()
                at = (h - (kv_heads - folds), row - (shards - folds))
                for member in range(groups):
                    q_t[member] = qg[at + (0, slice(None), pl.ds(member * HEAD, HEAD))]
                    q_t[groups + member] = qg[at + (1, slice(None), pl.ds(member * HEAD, HEAD))]

        @pl.when(extra == 0)
        def _():
            for member in range(groups):
                q_t[member] = q_ref[:, cols(h * groups + member)]
                q_t[groups + member] = g_ref[:, cols(h * groups + member)]

        own_mixed = mixed_s[row]

        def member_step(member, inner):
            qh = q_t[member]
            gh = q_t[groups + member]
            z_s[...] = jnp.zeros_like(z_s)
            dn_s[...] = jnp.zeros_like(dn_s)
            pm_s[...] = jnp.zeros_like(pm_s)
            acc_s[...] = jnp.zeros_like(acc_s)
            each_block(row, lambda d, c, row0, kind: first_pass(h, row, qh, gh, d, c, row0, kind))
            inverse = 1.0 / jnp.sum(z_s[...], axis=1, keepdims=True)
            dot = jnp.sum(dn_s[...], axis=1, keepdims=True) * inverse
            db_s[...] = jnp.broadcast_to(dot, db_s.shape)
            each_block(row, lambda d, c, row0, kind: second_pass(h, row, d, c, row0))
            scale = inverse * QUERY_SCALE
            dq = (acc_s[:, :HEAD] * scale).astype(jnp.bfloat16)
            dm = (acc_s[:, HEAD:] * scale).astype(jnp.bfloat16)
            pm = (pm_s[...] * inverse).astype(jnp.bfloat16)
            q_part = mm(own_mixed, dq, ((0,), (0,)))
            k_part = mm(dm, qh, ((0,), (0,)))
            v_part = mm(pm, gh, ((0,), (0,)))
            blocked = (shards, own_rows, HEAD)
            sketch[h, :, :, cols(2 + member)] += q_part.reshape(blocked)
            sketch[h, :, :, :HEAD] += k_part.reshape(blocked)
            sketch[h, :, :, HEAD : 2 * HEAD] += v_part.reshape(blocked)
            return inner

        lax.fori_loop(0, groups, member_step, 0)

    sketch[...] = jnp.zeros_like(sketch)
    own_rows = sketch.shape[2]
    arrivals(0)
    pass_folded()
    if kv_heads > 1:
        @pl.when(me == 1)
        def _():
            arrivals(1)

    loop(0, shards, gathered)
    lax.fori_loop(0, kv_heads, kv_head, 0)

    def collect(h):
        def add(offset):
            @pl.when(seq_at(shards - offset)[0] <= last(h))
            def _():
                row_copy(h, offset).wait_recv()
                sketch[h, me] += stage_in[h, offset].astype(jnp.float32)

        loop(1, shards, add)
        rows = sketch[h, me]
        ok_ref[:, cols(h)] = rows[:, :HEAD]
        ov_ref[:, cols(h)] = rows[:, HEAD : 2 * HEAD]
        for member in range(groups):
            oq_ref[:, cols(h * groups + member)] = rows[:, (2 + member) * HEAD : (3 + member) * HEAD]

    loop(0, kv_heads, collect)

    loop(1, peers, lambda offset: part_copy(offset).wait_send())
    loop(1, shards, lambda offset: mixed_along(offset).wait_send())
    loop(0, shards, lambda b: loop(1, peers, lambda offset: mixed_share(b, offset).wait_send()))

    def drain_rows(h):
        @pl.when(me <= last(h))
        def _():
            loop(1, shards, lambda offset: row_copy(h, offset).wait_send())

    loop(0, kv_heads, drain_rows)

    def drain(h):
        @pl.when(me < last(h))
        def _():
            loop(0, jnp.minimum(me, reach - 1) + 1, lambda d: hop(h, me - d).wait_send())

    if reach > 0:
        loop(0, kv_heads, drain)
    for h in range(kv_heads - folds, kv_heads):
        for row in range(shards - folds, shards):
            @pl.when((me > last(h)) & (me <= row))
            def _():
                hop(h, row, -1).wait_send()
                row_hop(h, row).wait_send()


STEP_H, STEP_B, STEP_ROW, STEP_SLOT, STEP_HALF = 1, 4, 16, 64, 512
INIT, FINAL, SEND, WAIT_KV, PASS_KV, WAIT_Q, RELAY = (1024 << i for i in range(7))
FOREIGN = 4


def step_of(h, b, row, slot, half, *flags):
    return h * STEP_H + b * STEP_B + row * STEP_ROW + slot * STEP_SLOT + half * STEP_HALF + sum(flags)


STEPS = (
    [step_of(h, 0, 0, h, 0, INIT, FINAL, SEND) for h in range(4)],
    [
        code
        for h in range(4)
        for code in (
            step_of(h, 1, 1, h, 0, INIT),
            step_of(h, 0, 1, h, 0, FINAL, WAIT_KV, *((PASS_KV,) if h < 3 else (SEND,))),
        )
    ]
    + [
        step_of(3, 1, 2, 4, 0, INIT, WAIT_Q),
        step_of(3, 0, 2, 4, 0),
        step_of(3, 2, 2, 4, 0, WAIT_KV, FINAL),
        step_of(3, 1, 3, 5, 0, INIT, WAIT_Q),
        step_of(3, 0, 3, 5, 0),
        step_of(3, 2, 3, 5, 0),
        step_of(3, 3, 3, 5, 0, WAIT_KV, FINAL, SEND),
    ],
    [
        step_of(0, 2, 2, 0, 0, INIT),
        step_of(0, 1, 2, 0, 0, WAIT_KV, PASS_KV),
        step_of(1, 2, 2, 1, 1, INIT),
        step_of(1, 1, 2, 1, 1, WAIT_KV, PASS_KV),
        step_of(0, 0, 2, 0, 0, WAIT_KV, PASS_KV, RELAY, FINAL, SEND),
        step_of(1, 0, 2, 1, 1, WAIT_KV, PASS_KV, FINAL, SEND),
        step_of(2, 2, 2, 2, 0, INIT),
        step_of(2, 2, 3, 4, 1, INIT, WAIT_Q),
        step_of(2, 1, 2, 2, 0, WAIT_KV),
        step_of(2, 1, 3, 4, 1),
        step_of(2, 3, 3, 4, 1, WAIT_KV),
        step_of(2, 0, 2, 2, 0, WAIT_KV, FINAL),
        step_of(2, 0, 3, 4, 1, FINAL, SEND),
    ],
    [
        step_of(0, 3, 3, 0, 0, INIT),
        step_of(1, 3, 3, 1, 1, INIT),
        step_of(0, 2, 3, 0, 0, WAIT_KV),
        step_of(1, 2, 3, 1, 1, WAIT_KV),
        step_of(0, 1, 3, 0, 0, WAIT_KV),
        step_of(1, 1, 3, 1, 1, WAIT_KV),
        step_of(0, 0, 3, 0, 0, WAIT_KV, FINAL, SEND),
        step_of(1, 0, 3, 1, 1, WAIT_KV, FINAL, SEND),
    ],
)


def balanced_kernel(
    subs, peers, mix_scale,
    q_hbm, k_hbm, v_hbm, g_hbm, x_hbm, seed_hbm, out_ref,
    x_ref, seed_ref, qg, kv, pg_s, w_s, z_s, dn_s, pm_s, acc_s, db_s,
    part, part_in, mixed_s, sketch, stage, stage_in, fold_in,
    kv_send, kv_recv, q_send, q_recv, part_send, part_recv, hop_send, hop_recv,
    share_send, share_recv, row_send, row_recv, fold_send, fold_recv, load_sem,
):
    shards, kv_heads = 4, 4
    tokens = qg.shape[3]
    groups = qg.shape[2]
    chunks = tokens // CHUNK
    share = tokens // peers
    own_rows = sketch.shape[2]
    me = lax.axis_index("seq")
    peer = lax.axis_index("head") * subs + lax.axis_index("sub")

    def cols(head):
        return pl.ds(pl.multiple_of(head * HEAD, HEAD), HEAD)

    def peer_at(offset):
        other = lax.rem(peer + offset, peers)
        return other, {"head": lax.div(other, subs), "sub": lax.rem(other, subs)}

    def seq_at(offset):
        other = lax.rem(me + offset, shards)
        return other, {"seq": other}

    def remote(src, dst, send, recv, device):
        return pltpu.make_async_remote_copy(
            src_ref=src, dst_ref=dst, send_sem=send, recv_sem=recv,
            device_id=device, device_id_type=MESH,
        )

    def loop(low, high, fn):
        def step(i, carry):
            fn(i)
            return carry

        lax.fori_loop(low, high, step, 0)

    def kv_hop(h, b, way=1):
        return remote(
            kv.at[h, b], kv.at[h, b], kv_send.at[h, b], kv_recv.at[h, b], {"seq": me + way}
        )

    def q_hop(source, target):
        at = target - FOREIGN
        return remote(
            qg.at[source], qg.at[target], q_send.at[at], q_recv.at[at], {"seq": me - 1}
        )

    def part_copy(offset):
        other, device = peer_at(offset)
        rows = pl.ds(pl.multiple_of(other * share, share), share)
        return remote(
            part.at[rows], part_in.at[offset], part_send.at[offset], part_recv.at[offset], device
        )

    mine = pl.ds(pl.multiple_of(peer * share, share), share)

    def mixed_along(offset):
        _, device = seq_at(offset)
        return remote(
            mixed_s.at[me, mine], mixed_s.at[me, mine], hop_send.at[offset], hop_recv.at[offset],
            device,
        )

    def mixed_share(b, offset):
        _, device = peer_at(offset)
        return remote(
            mixed_s.at[b, mine], mixed_s.at[b, mine], share_send.at[b, offset],
            share_recv.at[b, offset], device,
        )

    def row_copy(h, target, sender):
        return remote(
            stage.at[h, target], stage_in.at[h, sender], row_send.at[h, target],
            row_recv.at[h, sender], {"seq": target},
        )

    def fold_copy(h):
        return remote(
            stage.at[h, pl.ds(1, shards - 1)], fold_in.at[h], fold_send.at[h], fold_recv.at[h],
            {"seq": 1},
        )

    barrier = pltpu.get_barrier_semaphore()

    def greet_peer(offset):
        pl.semaphore_signal(barrier, inc=1, device_id=peer_at(offset)[1], device_id_type=MESH)

    def greet_seq(offset):
        pl.semaphore_signal(barrier, inc=1, device_id=seq_at(offset)[1], device_id_type=MESH)

    loop(1, peers, greet_peer)
    loop(1, shards, greet_seq)

    def load_kv(h, which):
        source = (k_hbm, v_hbm)[which]
        return pltpu.make_async_copy(
            source.at[:, cols(h)], kv.at[h, me, which], load_sem.at[2 + which * kv_heads + h]
        )

    def load_qg(h, which, member):
        source = (q_hbm, g_hbm)[which]
        at = 2 + 2 * kv_heads + (h * 2 + which) * groups + member
        return pltpu.make_async_copy(
            source.at[:, cols(h * groups + member)], qg.at[h, which, member], load_sem.at[at]
        )

    load_seed = pltpu.make_async_copy(seed_hbm, seed_ref, load_sem.at[0])
    load_x = pltpu.make_async_copy(x_hbm, x_ref, load_sem.at[1])

    def each_kv(fn):
        for which in range(2):
            loop(0, kv_heads, lambda h: fn(load_kv(h, which)))

    def each_qg(fn):
        for which in range(2):
            for member in range(groups):
                loop(0, kv_heads, lambda h: fn(load_qg(h, which, member)))

    each_kv(lambda copy: copy.start())
    load_seed.start()
    load_x.start()
    each_qg(lambda copy: copy.start())
    each_kv(lambda copy: copy.wait())
    pl.semaphore_wait(barrier, peers + shards - 2)

    @pl.when(me < 3)
    def _():
        kv_hop(0, me).start()

    @pl.when(me > 1)
    def _():
        kv_hop(3, me, -1).start()

    load_seed.wait()
    load_x.wait()
    seeds = seed_ref[...].astype(jnp.float32).astype(jnp.bfloat16)
    part[...] = mm(seeds, x_ref[...], ((0,), (0,))).T
    loop(1, peers, lambda offset: part_copy(offset).start())
    part_in[0] = part[mine, :]
    loop(1, peers, lambda offset: part_copy(offset).wait_recv())
    total = part_in[0]
    for offset in range(1, peers):
        total = total + part_in[offset]
    mixed_s[me, mine, :] = (total * mix_scale).astype(jnp.bfloat16)

    def spread(b):
        loop(1, peers, lambda offset: mixed_share(b, offset).start())

    def spread_from(offset):
        mixed_along(offset).wait_recv()
        spread(seq_at(shards - offset)[0])

    def gathered(b):
        loop(1, peers, lambda offset: mixed_share(b, offset).wait_recv())

    loop(1, shards, lambda offset: mixed_along(offset).start())
    spread(me)
    each_qg(lambda copy: copy.wait())

    @pl.when(me == 0)
    def _():
        loop(1, kv_heads, lambda h: kv_hop(h, 0).start())

    @pl.when(me == 1)
    def _():
        kv_hop(1, 1).start()

    @pl.when(me == 2)
    def _():
        kv_hop(1, 2).start()
        q_hop(3, 4).start()

    @pl.when(me == 3)
    def _():
        q_hop(3, 5).start()
        q_hop(2, 4).start()
        kv_hop(2, 3, -1).start()

    sketch[...] = jnp.zeros_like(sketch)

    def first_pass(h, b, slot, half, d, c, row0, causal):
        rows = tokens - row0
        at = pl.ds(row0, rows)
        keys = pl.ds(c * CHUNK, CHUNK)
        qh = qg[slot, 0, :, at, :].reshape(groups * rows, HEAD)
        gh = qg[slot, 1, :, at, :].reshape(groups * rows, HEAD)
        scores = mm(qh, kv[h, b, 0, keys, :], ((1,), (1,)))
        weight = mm(gh, kv[h, b, 1, keys, :], ((1,), (1,)))
        bounded = jnp.tanh(scores * (QUERY_SCALE / CAP))
        power = jnp.exp2(bounded * (CAP / math.log(2.0)))
        if causal:
            qi = lax.broadcasted_iota(jnp.int32, (groups, rows, CHUNK), 1)
            kj = lax.broadcasted_iota(jnp.int32, (groups, rows, CHUNK), 2)
            keep = (row0 + qi >= c * CHUNK + kj).reshape(groups * rows, CHUNK)
            power = jnp.where(keep, power, 0.0)
        whole = (groups, rows, CHUNK)
        folded = (groups, rows, HEAD)
        put = half * shards + d
        pg_s[put, c, :, at, :] = (power - power * (bounded * bounded)).reshape(whole)
        w_s[put, c, :, at, :] = weight.reshape(whole)
        pw = power * weight
        z_s[half, :, at, :] += (power[:, :HEAD] + power[:, HEAD:]).reshape(folded)
        dn_s[half, :, at, :] += (pw[:, :HEAD] + pw[:, HEAD:]).reshape(folded)
        pm = mm(power.astype(jnp.bfloat16), mixed_s[b, keys, :], ((1,), (0,)))
        pm_s[half, :, at, :] += pm.reshape(folded)

    def second_pass(h, b, half, d, c, row0):
        rows = tokens - row0
        at = pl.ds(row0, rows)
        keys = pl.ds(c * CHUNK, CHUNK)
        put = half * shards + d
        dot = db_s[:, at, :]
        grad = pg_s[put, c, :, at, :] * (w_s[put, c, :, at, :] - jnp.concatenate([dot, dot], 2))
        sides = jnp.concatenate([kv[h, b, 0, keys, :], mixed_s[b, keys, :]], 1)
        term = mm(grad.astype(jnp.bfloat16).reshape(groups * rows, CHUNK), sides, ((1,), (0,)))
        acc_s[:, at, :] += term.reshape(groups, rows, 2 * HEAD)

    def finish_row(h, row, slot, half):
        inverse = 1.0 / jnp.sum(z_s[half], axis=2, keepdims=True)
        dot = jnp.sum(dn_s[half], axis=2, keepdims=True) * inverse
        db_s[...] = jnp.broadcast_to(dot, db_s.shape)
        acc_s[...] = jnp.zeros_like(acc_s)
        for c in range(chunks):
            second_pass(h, row, half, 0, c, c * CHUNK)

        def rest(d):
            for c in range(chunks):
                second_pass(h, row - d, half, d, c, 0)

        loop(1, row + 1, rest)
        scale = inverse * QUERY_SCALE
        dq = (acc_s[:, :, :HEAD] * scale).astype(jnp.bfloat16)
        dm = (acc_s[:, :, HEAD:] * scale).astype(jnp.bfloat16)
        pm = (pm_s[half] * inverse).astype(jnp.bfloat16)
        stacked = (groups * tokens, HEAD)
        blocked = (shards, own_rows, HEAD)
        k_part = mm(dm.reshape(stacked), qg[slot, 0].reshape(stacked), ((0,), (0,)))
        v_part = mm(pm.reshape(stacked), qg[slot, 1].reshape(stacked), ((0,), (0,)))
        sketch[h, :, :, :HEAD] += k_part.reshape(blocked)
        sketch[h, :, :, HEAD : 2 * HEAD] += v_part.reshape(blocked)
        q_part = mm(mixed_s[row], jnp.concatenate([dq[m] for m in range(groups)], 1), ((0,), (0,)))
        sketch[h, :, :, 2 * HEAD :] += q_part.reshape(shards, own_rows, groups * HEAD)

    def send_head(h):
        @pl.when(me == 1)
        def _():
            fold_copy(h).wait_recv()
            sketch[h, pl.ds(1, shards - 1)] += fold_in[h].astype(jnp.float32)

        stage[h] = sketch[h].astype(stage.dtype)

        @pl.when(me == 0)
        def _():
            fold_copy(h).start()

        @pl.when(me > 0)
        def _():
            loop(1, shards, lambda offset: row_copy(h, seq_at(offset)[0], me).start())

    def one_step(index):
        code = jnp.int32(0)
        for shard, codes in enumerate(STEPS):
            for i, value in enumerate(codes):
                code = jnp.where((me == shard) & (index == i), value, code)

        def field(unit, size):
            return lax.rem(lax.div(code, unit), size)

        def flag(unit):
            return field(unit, 2) == 1

        h, b, row = field(STEP_H, 4), field(STEP_B, 4), field(STEP_ROW, 4)
        slot, half = field(STEP_SLOT, 8), field(STEP_HALF, 2)

        @pl.when(index == 1)
        def _():
            loop(1, shards, spread_from)
            loop(1, shards, lambda offset: gathered(seq_at(offset)[0]))

        @pl.when(flag(WAIT_Q))
        def _():
            q_hop(slot, slot).wait_recv()

        @pl.when(flag(WAIT_KV))
        def _():
            kv_hop(h, b).wait_recv()

        @pl.when(flag(PASS_KV))
        def _():
            kv_hop(h, b).start()

            @pl.when((me == 1) & (h == 1))
            def _():
                kv_hop(2, 1).start()

        @pl.when(flag(RELAY))
        def _():
            q_hop(5, 5).wait_recv()
            q_hop(5, 5).start()
            kv_hop(3, 3, -1).wait_recv()
            kv_hop(3, 3, -1).start()

        @pl.when(flag(INIT))
        def _():
            z_s[half] = jnp.zeros(z_s.shape[1:], z_s.dtype)
            dn_s[half] = jnp.zeros(dn_s.shape[1:], dn_s.dtype)
            pm_s[half] = jnp.zeros(pm_s.shape[1:], pm_s.dtype)

        @pl.when(b == row)
        def _():
            for c in range(chunks):
                first_pass(h, b, slot, half, 0, c, c * CHUNK, True)

        @pl.when(b != row)
        def _():
            for c in range(chunks):
                first_pass(h, b, slot, half, row - b, c, 0, False)

        @pl.when(flag(FINAL))
        def _():
            finish_row(h, row, slot, half)

        @pl.when(flag(SEND))
        def _():
            held = (me == 1) & (row == 1)
            loop(jnp.where(held, 0, h), jnp.where(held, h, h + 1), send_head)

    gathered(me)
    count = jnp.int32(0)
    for shard, codes in enumerate(STEPS):
        count = jnp.where(me == shard, len(codes), count)
    loop(0, count, one_step)

    def heads_of(sender):
        return jnp.where(sender == 2, 3, jnp.where(sender == 3, 2, jnp.where(sender == 1, 4, 0)))

    def collect(h):
        def add(sender):
            @pl.when((sender != me) & (h < heads_of(sender)))
            def _():
                row_copy(h, me, sender).wait_recv()
                sketch[h, me] += stage_in[h, sender].astype(jnp.float32)

        loop(1, shards, add)
        out_ref[h] = sketch[h, me]

    loop(0, kv_heads, collect)

    loop(1, peers, lambda offset: part_copy(offset).wait_send())
    loop(1, shards, lambda offset: mixed_along(offset).wait_send())
    loop(0, shards, lambda b: loop(1, peers, lambda offset: mixed_share(b, offset).wait_send()))
    loop(
        0, heads_of(me),
        lambda h: loop(1, shards, lambda offset: row_copy(h, seq_at(offset)[0], me).wait_send()),
    )

    @pl.when(me == 0)
    def _():
        loop(0, kv_heads, lambda h: fold_copy(h).wait_send())

    up = jnp.where(me == 0, 4, jnp.where(me == 1, 3, jnp.where(me == 2, 2, 0)))
    loop(0, up, lambda h: loop(0, me + 1, lambda b: kv_hop(h, b).wait_send()))

    @pl.when(me == 2)
    def _():
        kv_hop(3, 2, -1).wait_send()
        kv_hop(3, 3, -1).wait_send()
        q_hop(3, 4).wait_send()
        q_hop(5, 5).wait_send()

    @pl.when(me == 3)
    def _():
        kv_hop(3, 3, -1).wait_send()
        kv_hop(2, 3, -1).wait_send()
        q_hop(3, 5).wait_send()
        q_hop(2, 4).wait_send()


def unpack_kernel(packed, oq_ref, ok_ref, ov_ref):
    kv_heads = packed.shape[0]
    queries = packed.shape[2] - 2 * HEAD
    for h in range(kv_heads):
        ok_ref[:, h * HEAD : (h + 1) * HEAD] = packed[h, :, :HEAD]
        ov_ref[:, h * HEAD : (h + 1) * HEAD] = packed[h, :, HEAD : 2 * HEAD]
        oq_ref[:, h * queries : (h + 1) * queries] = packed[h, :, 2 * HEAD :]


def balanced(queries, key_states, value_states, out_grad, layer_inputs, sketch_seeds):
    tokens, query_width = queries.shape
    kv_width = key_states.shape[1]
    kv_heads = kv_width // HEAD
    groups = query_width // kv_width
    shards = lax.axis_size("seq")
    subs = lax.axis_size("sub")
    peers = lax.axis_size("head") * subs
    features = layer_inputs.shape[0]
    rank = sketch_seeds.shape[1]
    chunks = tokens // CHUNK
    own_rows = rank // shards
    width = (groups + 2) * HEAD
    f32, bf16, dma = jnp.float32, jnp.bfloat16, pltpu.SemaphoreType.DMA
    packed = pl.pallas_call(
        functools.partial(balanced_kernel, subs, peers, (2.0 * D * tokens * shards) ** (-0.5)),
        out_shape=jax.ShapeDtypeStruct((kv_heads, own_rows, width), f32),
        in_specs=[pl.BlockSpec(memory_space=pltpu.HBM)] * 6,
        out_specs=pl.BlockSpec(memory_space=pltpu.VMEM),
        scratch_shapes=[
            pltpu.VMEM((features, tokens), bf16),
            pltpu.VMEM((features, rank), sketch_seeds.dtype),
            pltpu.VMEM((kv_heads + 2, 2, groups, tokens, HEAD), bf16),
            pltpu.VMEM((kv_heads, shards, 2, tokens, HEAD), bf16),
            pltpu.VMEM((2 * shards, chunks, groups, tokens, CHUNK), f32),
            pltpu.VMEM((2 * shards, chunks, groups, tokens, CHUNK), f32),
            pltpu.VMEM((2, groups, tokens, HEAD), f32),
            pltpu.VMEM((2, groups, tokens, HEAD), f32),
            pltpu.VMEM((2, groups, tokens, rank), f32),
            pltpu.VMEM((groups, tokens, HEAD + rank), f32),
            pltpu.VMEM((groups, tokens, HEAD), f32),
            pltpu.VMEM((tokens, rank), f32),
            pltpu.VMEM((peers, tokens // peers, rank), f32),
            pltpu.VMEM((shards, tokens, rank), bf16),
            pltpu.VMEM((kv_heads, shards, own_rows, width), f32),
            pltpu.VMEM((kv_heads, shards, own_rows, width), bf16),
            pltpu.VMEM((kv_heads, shards, own_rows, width), bf16),
            pltpu.VMEM((kv_heads, shards - 1, own_rows, width), bf16),
            dma((kv_heads, shards)), dma((kv_heads, shards)),
            dma((2,)), dma((2,)),
            dma((peers,)), dma((peers,)),
            dma((shards,)), dma((shards,)),
            dma((shards, peers)), dma((shards, peers)),
            dma((kv_heads, shards)), dma((kv_heads, shards)),
            dma((kv_heads,)), dma((kv_heads,)),
            dma((2 + 2 * kv_heads * (1 + groups),)),
        ],
        compiler_params=pltpu.CompilerParams(
            collective_id=0, has_side_effects=True, vmem_limit_bytes=62 * 2**20
        ),
    )(queries, key_states, value_states, out_grad, layer_inputs, sketch_seeds)
    return pl.pallas_call(
        unpack_kernel,
        out_shape=(
            jax.ShapeDtypeStruct((own_rows, query_width), f32),
            jax.ShapeDtypeStruct((own_rows, kv_width), f32),
            jax.ShapeDtypeStruct((own_rows, kv_width), f32),
        ),
        in_specs=[pl.BlockSpec(memory_space=pltpu.VMEM)],
        out_specs=(pl.BlockSpec(memory_space=pltpu.VMEM),) * 3,
    )(packed)


def per_device(queries, key_states, value_states, out_grad, layer_inputs, sketch_seeds):
    tokens, query_width = queries.shape
    kv_width = key_states.shape[1]
    kv_heads = kv_width // HEAD
    shards = lax.axis_size("seq")
    length = tokens * shards
    reach_full = WINDOW // tokens
    reach = min(reach_full, shards - 1)
    rank = sketch_seeds.shape[1]
    subs = lax.axis_size("sub")
    peers = lax.axis_size("head") * subs
    groups = query_width // kv_width
    if shards == 4 and kv_heads == 4 and reach < reach_full and tokens == 2 * CHUNK:
        return balanced(queries, key_states, value_states, out_grad, layer_inputs, sketch_seeds)
    folds = 0
    features = layer_inputs.shape[0]
    slots = (reach + 1) * (tokens // CHUNK)
    own_rows = rank // shards
    width = (query_width + 2 * kv_width) // kv_heads
    f32, bf16, dma = jnp.float32, jnp.bfloat16, pltpu.SemaphoreType.DMA
    return pl.pallas_call(
        functools.partial(
            attention_kernel, shards, reach_full, reach, folds, subs, peers,
            (2.0 * D * length) ** (-0.5),
        ),
        out_shape=(
            jax.ShapeDtypeStruct((own_rows, query_width), f32),
            jax.ShapeDtypeStruct((own_rows, kv_width), f32),
            jax.ShapeDtypeStruct((own_rows, kv_width), f32),
        ),
        in_specs=[pl.BlockSpec(memory_space=pltpu.HBM)] * 6,
        out_specs=(pl.BlockSpec(memory_space=pltpu.VMEM),) * 3,
        scratch_shapes=[
            pltpu.VMEM((tokens, query_width), bf16),
            pltpu.VMEM((tokens, query_width), bf16),
            pltpu.VMEM((features, tokens), bf16),
            pltpu.VMEM((features, rank), sketch_seeds.dtype),
            pltpu.VMEM((max(folds, 1), max(folds, 1), 2, tokens, groups * HEAD), bf16),
            pltpu.VMEM((2 * groups, tokens, HEAD), bf16),
            pltpu.VMEM((kv_heads, shards, 2, tokens, HEAD), bf16),
            pltpu.VMEM((slots, tokens, CHUNK), f32),
            pltpu.VMEM((slots, tokens, CHUNK), f32),
            pltpu.VMEM((tokens, HEAD), f32),
            pltpu.VMEM((tokens, HEAD), f32),
            pltpu.VMEM((tokens, rank), f32),
            pltpu.VMEM((tokens, HEAD + rank), f32),
            pltpu.VMEM((tokens, HEAD), f32),
            pltpu.VMEM((tokens, rank), f32),
            pltpu.VMEM((peers, tokens // peers, rank), f32),
            pltpu.VMEM((shards, tokens, rank), bf16),
            pltpu.VMEM((kv_heads, shards, own_rows, width), f32),
            pltpu.VMEM((kv_heads, shards, own_rows, width), bf16),
            pltpu.VMEM((kv_heads, shards, own_rows, width), bf16),
            dma((kv_heads, shards)), dma((kv_heads, shards)),
            dma((peers,)), dma((peers,)),
            dma((shards,)), dma((shards,)),
            dma((shards, peers)), dma((shards, peers)),
            dma((kv_heads, shards)), dma((kv_heads, shards)),
            dma((max(folds, 1), max(folds, 1))), dma((max(folds, 1), max(folds, 1))),
            dma((4 + 2 * kv_heads,)),
        ],
        compiler_params=pltpu.CompilerParams(
            collective_id=0, has_side_effects=True, vmem_limit_bytes=62 * 2**20
        ),
    )(queries, key_states, value_states, out_grad, layer_inputs, sketch_seeds)


def solution(mesh):
    placed = (
        P(("group", "seq"), ("head", "sub")),
        P(("group", "seq"), ("head", "sub")),
        P(("group", "seq"), ("head", "sub")),
        P(("group", "seq"), ("head", "sub")),
        P(("head", "sub"), ("group", "seq")),
        P(("head", "sub"), None),
    )
    return jax.shard_map(
        per_device,
        mesh=mesh,
        in_specs=placed,
        out_specs=(
            P(("group", "seq"), ("head", "sub")),
            P(("group", "seq"), ("head", "sub")),
            P(("group", "seq"), ("head", "sub")),
        ),
        check_vma=False,
    )
```

```python
import functools
import math

import jax
import jax.numpy as jnp
from jax import lax
from jax.experimental import pallas as pl
from jax.experimental.pallas import tpu as pltpu
from jax.sharding import PartitionSpec as P

D = 4608
HEAD = 128
WINDOW = 2048
CAP = 50.0
QUERY_SCALE = 144.0 ** (-0.5)
CHUNK = 256
MESH = pl.DeviceIdType.MESH


def mm(left, right, dims):
    return lax.dot_general(left, right, (dims, ((), ())), preferred_element_type=jnp.float32)


def attention_kernel(
    shards, reach_full, reach, folds, subs, peers, mix_scale,
    q_hbm, k_hbm, v_hbm, g_hbm, x_hbm, seed_hbm, oq_ref, ok_ref, ov_ref,
    q_ref, g_ref, x_ref, seed_ref, qg, q_t, kv, pg_s, w_s, z_s, dn_s, pm_s, acc_s, db_s,
    part, part_in, mixed_s, sketch, stage, stage_in,
    send_sem, recv_sem, part_send, part_recv, hop_send, hop_recv, share_send, share_recv,
    row_send, row_recv, qg_send, qg_recv, load_sem,
):
    tokens = q_ref.shape[0]
    query_width = q_ref.shape[1]
    kv_width = k_hbm.shape[1]
    kv_heads = kv_width // HEAD
    groups = query_width // kv_width
    chunks = tokens // CHUNK
    share = tokens // peers
    me = lax.axis_index("seq")
    peer = lax.axis_index("head") * subs + lax.axis_index("sub")
    blocks = jnp.minimum(me, reach)

    def last(h):
        return shards - 1 - jnp.maximum(h - (kv_heads - 1 - folds), 0)


    def cols(head):
        return pl.ds(pl.multiple_of(head * HEAD, HEAD), HEAD)

    def peer_at(offset):
        other = lax.rem(peer + offset, peers)
        return other, {"head": lax.div(other, subs), "sub": lax.rem(other, subs)}

    def seq_at(offset):
        other = lax.rem(me + offset, shards)
        return other, {"seq": other}

    def remote(src, dst, send, recv, device):
        return pltpu.make_async_remote_copy(
            src_ref=src, dst_ref=dst, send_sem=send, recv_sem=recv,
            device_id=device, device_id_type=MESH,
        )

    def loop(low, high, fn):
        def step(i, carry):
            fn(i)
            return carry

        lax.fori_loop(low, high, step, 0)

    def hop(h, b, way=1):
        return remote(
            kv.at[h, b], kv.at[h, b], send_sem.at[h, b], recv_sem.at[h, b], {"seq": me + way}
        )

    def row_hop(h, row):
        at = (h - (kv_heads - folds), row - (shards - folds))
        return remote(
            qg.at[at], qg.at[at], qg_send.at[at], qg_recv.at[at], {"seq": me - 1}
        )

    def part_copy(offset):
        other, device = peer_at(offset)
        rows = pl.ds(pl.multiple_of(other * share, share), share)
        return remote(
            part.at[rows], part_in.at[offset], part_send.at[offset], part_recv.at[offset], device
        )

    mine = pl.ds(pl.multiple_of(peer * share, share), share)

    def mixed_along(offset):
        _, device = seq_at(offset)
        return remote(
            mixed_s.at[me, mine], mixed_s.at[me, mine], hop_send.at[offset], hop_recv.at[offset],
            device,
        )

    def mixed_share(b, offset):
        _, device = peer_at(offset)
        return remote(
            mixed_s.at[b, mine], mixed_s.at[b, mine], share_send.at[b, offset],
            share_recv.at[b, offset], device,
        )

    def row_copy(h, offset):
        other, device = seq_at(offset)
        return remote(
            stage.at[h, other], stage_in.at[h, offset], row_send.at[h, offset],
            row_recv.at[h, offset], device,
        )

    barrier = pltpu.get_barrier_semaphore()

    def greet_peer(offset):
        pl.semaphore_signal(barrier, inc=1, device_id=peer_at(offset)[1], device_id_type=MESH)

    def greet_seq(offset):
        pl.semaphore_signal(barrier, inc=1, device_id=seq_at(offset)[1], device_id_type=MESH)

    loop(1, peers, greet_peer)
    loop(1, shards, greet_seq)
    def load_kv(h, which):
        source = (k_hbm, v_hbm)[which]
        return pltpu.make_async_copy(
            source.at[:, cols(h)], kv.at[h, me, which], load_sem.at[4 + which * kv_heads + h]
        )

    loads = [
        pltpu.make_async_copy(source, target, load_sem.at[i])
        for i, (source, target) in enumerate(
            ((seed_hbm, seed_ref), (x_hbm, x_ref), (q_hbm, q_ref), (g_hbm, g_ref))
        )
    ]
    for h in range(kv_heads):
        load_kv(h, 0).start()
        load_kv(h, 1).start()
    for load in loads:
        load.start()
    for h in range(kv_heads):
        load_kv(h, 0).wait()
        load_kv(h, 1).wait()
    pl.semaphore_wait(barrier, peers + shards - 2)

    early = 1

    def send_own(low, high):
        def one(h):
            @pl.when(me < last(h))
            def _():
                hop(h, me).start()

        if reach > 0:
            loop(low, high, one)

    def send_folded(h):
        @pl.when(me > last(h))
        def _():
            at = (h - (kv_heads - folds), me - (shards - folds))
            width = groups * HEAD
            qg[at + (0,)] = q_ref[:, h * width : (h + 1) * width]
            qg[at + (1,)] = g_ref[:, h * width : (h + 1) * width]
            if h < kv_heads - 1:
                hop(h, me, -1).start()
            row_hop(h, me).start()

    send_own(0, early)
    if folds > 0:
        @pl.when(me > last(kv_heads - 1))
        def _():
            hop(kv_heads - 1, me, -1).start()

    loads[0].wait()
    loads[1].wait()
    seeds = seed_ref[...].astype(jnp.float32).astype(jnp.bfloat16)
    part[...] = mm(seeds, x_ref[...], ((0,), (0,))).T
    loop(1, peers, lambda offset: part_copy(offset).start())
    part_in[0] = part[mine, :]
    loop(1, peers, lambda offset: part_copy(offset).wait_recv())
    total = part_in[0]
    for offset in range(1, peers):
        total = total + part_in[offset]
    mixed_s[me, mine, :] = (total * mix_scale).astype(jnp.bfloat16)

    def spread(b):
        loop(1, peers, lambda offset: mixed_share(b, offset).start())

    def spread_from(offset):
        mixed_along(offset).wait_recv()
        spread(seq_at(shards - offset)[0])

    def gathered(b):
        loop(1, peers, lambda offset: mixed_share(b, offset).wait_recv())

    loop(1, shards, lambda offset: mixed_along(offset).start())
    spread(me)
    send_own(early, kv_heads)
    loads[2].wait()
    loads[3].wait()
    for h in reversed(range(kv_heads - folds, kv_heads)):
        send_folded(h)
    loop(1, shards, spread_from)

    def first_pass(h, row, qh, gh, d, c, row0, kind):
        rows = tokens - row0
        kk = kv[h, row - d, 0, pl.ds(c * CHUNK, CHUNK), :]
        vv = kv[h, row - d, 1, pl.ds(c * CHUNK, CHUNK), :]
        mixed = mixed_s[row - d, pl.ds(c * CHUNK, CHUNK), :]
        scores = mm(qh[row0:], kk, ((1,), (1,)))
        weight = mm(gh[row0:], vv, ((1,), (1,)))
        bounded = jnp.tanh(scores * (QUERY_SCALE / CAP))
        power = jnp.exp2(bounded * (CAP / math.log(2.0)))
        if kind is not None:
            qi = row0 + lax.broadcasted_iota(jnp.int32, (rows, CHUNK), 0)
            kj = c * CHUNK + lax.broadcasted_iota(jnp.int32, (rows, CHUNK), 1)
            keep = qi >= kj if kind == "causal" else qi < kj
            power = jnp.where(keep, power, 0.0)
        slot = d * chunks + c
        pg_s[slot, pl.ds(row0, rows), :] = power - power * (bounded * bounded)
        w_s[slot, pl.ds(row0, rows), :] = weight
        pw = power * weight
        at = pl.ds(row0, rows)
        z_s[at, :] += power[:, :HEAD] + power[:, HEAD:]
        dn_s[at, :] += pw[:, :HEAD] + pw[:, HEAD:]
        pm_s[at, :] += mm(power.astype(jnp.bfloat16), mixed, ((1,), (0,)))

    def second_pass(h, row, d, c, row0):
        rows = tokens - row0
        at = pl.ds(row0, rows)
        slot = d * chunks + c
        kk = kv[h, row - d, 0, pl.ds(c * CHUNK, CHUNK), :]
        mixed = mixed_s[row - d, pl.ds(c * CHUNK, CHUNK), :]
        dot = db_s[at, :]
        grad = pg_s[slot, at, :] * (w_s[slot, at, :] - jnp.concatenate([dot, dot], 1))
        acc_s[at, :] += mm(
            grad.astype(jnp.bfloat16), jnp.concatenate([kk, mixed], 1), ((1,), (0,))
        )

    full = reach if reach < reach_full else reach_full - 1

    def each_block(row, fn):
        for c in range(chunks):
            fn(0, c, c * CHUNK, "causal")

        def step(d, carry):
            for c in range(chunks):
                fn(d, c, 0, None)
            return carry

        lax.fori_loop(1, jnp.minimum(row, full) + 1, step, 0)
        if full < reach:
            @pl.when(row >= reach)
            def _():
                for c in range(chunks):
                    fn(reach, c, 0, "window")

    def arrivals(h):
        def arrive(d):
            hop(h, me - d).wait_recv()

            @pl.when((me < last(h)) & (d < reach))
            def _():
                hop(h, me - d).start()

        @pl.when(me <= last(h))
        def _():
            loop(1, blocks + 1, arrive)

    def pass_folded():
        for folded in reversed(range(kv_heads - folds, kv_heads)):
            for row in range(shards - folds + 1, shards):
                @pl.when((me > last(folded)) & (me < row))
                def _():
                    hop(folded, row, -1).wait_recv()
                    hop(folded, row, -1).start()
                    row_hop(folded, row).wait_recv()
                    row_hop(folded, row).start()

    def kv_head(h, carry):
        @pl.when((h > 1) | ((h == 1) & (me != 1)))
        def _():
            arrivals(h)

        count = jnp.where(me < last(h), 1, jnp.where(me == last(h), shards - last(h), 0))
        loop(0, count, lambda extra: row_task(h, me + extra, extra))

        @pl.when(me <= last(h))
        def _():
            stage[h] = sketch[h].astype(stage.dtype)
            loop(1, shards, lambda offset: row_copy(h, offset).start())

        return carry

    def row_task(h, row, extra):
        if folds > 0:
            @pl.when(extra > 0)
            def _():
                hop(h, row, -1).wait_recv()
                row_hop(h, row).wait_recv()
                at = (h - (kv_heads - folds), row - (shards - folds))
                for member in range(groups):
                    q_t[member] = qg[at + (0, slice(None), pl.ds(member * HEAD, HEAD))]
                    q_t[groups + member] = qg[at + (1, slice(None), pl.ds(member * HEAD, HEAD))]

        @pl.when(extra == 0)
        def _():
            for member in range(groups):
                q_t[member] = q_ref[:, cols(h * groups + member)]
                q_t[groups + member] = g_ref[:, cols(h * groups + member)]

        own_mixed = mixed_s[row]

        def member_step(member, inner):
            qh = q_t[member]
            gh = q_t[groups + member]
            z_s[...] = jnp.zeros_like(z_s)
            dn_s[...] = jnp.zeros_like(dn_s)
            pm_s[...] = jnp.zeros_like(pm_s)
            acc_s[...] = jnp.zeros_like(acc_s)
            each_block(row, lambda d, c, row0, kind: first_pass(h, row, qh, gh, d, c, row0, kind))
            inverse = 1.0 / jnp.sum(z_s[...], axis=1, keepdims=True)
            dot = jnp.sum(dn_s[...], axis=1, keepdims=True) * inverse
            db_s[...] = jnp.broadcast_to(dot, db_s.shape)
            each_block(row, lambda d, c, row0, kind: second_pass(h, row, d, c, row0))
            scale = inverse * QUERY_SCALE
            dq = (acc_s[:, :HEAD] * scale).astype(jnp.bfloat16)
            dm = (acc_s[:, HEAD:] * scale).astype(jnp.bfloat16)
            pm = (pm_s[...] * inverse).astype(jnp.bfloat16)
            q_part = mm(own_mixed, dq, ((0,), (0,)))
            k_part = mm(dm, qh, ((0,), (0,)))
            v_part = mm(pm, gh, ((0,), (0,)))
            blocked = (shards, own_rows, HEAD)
            sketch[h, :, :, cols(2 + member)] += q_part.reshape(blocked)
            sketch[h, :, :, :HEAD] += k_part.reshape(blocked)
            sketch[h, :, :, HEAD : 2 * HEAD] += v_part.reshape(blocked)
            return inner

        lax.fori_loop(0, groups, member_step, 0)

    sketch[...] = jnp.zeros_like(sketch)
    own_rows = sketch.shape[2]
    arrivals(0)
    pass_folded()
    if kv_heads > 1:
        @pl.when(me == 1)
        def _():
            arrivals(1)

    loop(0, shards, gathered)
    lax.fori_loop(0, kv_heads, kv_head, 0)

    def collect(h):
        def add(offset):
            @pl.when(seq_at(shards - offset)[0] <= last(h))
            def _():
                row_copy(h, offset).wait_recv()
                sketch[h, me] += stage_in[h, offset].astype(jnp.float32)

        loop(1, shards, add)
        rows = sketch[h, me]
        ok_ref[:, cols(h)] = rows[:, :HEAD]
        ov_ref[:, cols(h)] = rows[:, HEAD : 2 * HEAD]
        for member in range(groups):
            oq_ref[:, cols(h * groups + member)] = rows[:, (2 + member) * HEAD : (3 + member) * HEAD]

    loop(0, kv_heads, collect)

    loop(1, peers, lambda offset: part_copy(offset).wait_send())
    loop(1, shards, lambda offset: mixed_along(offset).wait_send())
    loop(0, shards, lambda b: loop(1, peers, lambda offset: mixed_share(b, offset).wait_send()))

    def drain_rows(h):
        @pl.when(me <= last(h))
        def _():
            loop(1, shards, lambda offset: row_copy(h, offset).wait_send())

    loop(0, kv_heads, drain_rows)

    def drain(h):
        @pl.when(me < last(h))
        def _():
            loop(0, jnp.minimum(me, reach - 1) + 1, lambda d: hop(h, me - d).wait_send())

    if reach > 0:
        loop(0, kv_heads, drain)
    for h in range(kv_heads - folds, kv_heads):
        for row in range(shards - folds, shards):
            @pl.when((me > last(h)) & (me <= row))
            def _():
                hop(h, row, -1).wait_send()
                row_hop(h, row).wait_send()


STEP_H, STEP_B, STEP_ROW, STEP_SLOT, STEP_HALF = 1, 4, 16, 64, 512
INIT, FINAL, SEND, WAIT_KV, PASS_KV, WAIT_Q, RELAY = (1024 << i for i in range(7))
HOP, GATHER = 1 << 19, 1 << 22
FOREIGN = 4


def step_of(h, b, row, slot, half, *flags):
    return h * STEP_H + b * STEP_B + row * STEP_ROW + slot * STEP_SLOT + half * STEP_HALF + sum(flags)


STEPS = (
    [step_of(h, 0, 0, h, 0, INIT, FINAL, SEND) for h in range(4)],
    [
        step_of(0, 1, 1, 0, 0, INIT),
        step_of(1, 1, 1, 1, 1, INIT, HOP),
        step_of(0, 0, 1, 0, 0, WAIT_KV, PASS_KV, GATHER, FINAL),
        step_of(1, 0, 1, 1, 1, WAIT_KV, PASS_KV, FINAL),
        step_of(2, 1, 1, 2, 0, INIT, 3 * HOP),
        step_of(2, 0, 1, 2, 0, WAIT_KV, PASS_KV, FINAL),
        step_of(3, 1, 1, 3, 0, INIT, 4 * HOP),
        step_of(3, 0, 1, 3, 0, WAIT_KV, FINAL, SEND),
        step_of(3, 1, 2, 4, 0, INIT, WAIT_Q, 3 * GATHER),
        step_of(3, 0, 2, 4, 0),
        step_of(3, 2, 2, 4, 0, WAIT_KV, FINAL),
        step_of(3, 1, 3, 5, 0, INIT, WAIT_Q, 4 * GATHER),
        step_of(3, 0, 3, 5, 0),
        step_of(3, 2, 3, 5, 0),
        step_of(3, 3, 3, 5, 0, WAIT_KV, FINAL, SEND),
    ],
    [
        step_of(0, 2, 2, 0, 0, INIT),
        step_of(1, 2, 2, 1, 1, INIT, 2 * HOP),
        step_of(0, 1, 2, 0, 0, WAIT_KV, PASS_KV, 4 * HOP, 2 * GATHER),
        step_of(1, 1, 2, 1, 1, WAIT_KV, PASS_KV, HOP),
        step_of(0, 0, 2, 0, 0, WAIT_KV, PASS_KV, RELAY, GATHER, FINAL, SEND),
        step_of(1, 0, 2, 1, 1, WAIT_KV, PASS_KV, FINAL, SEND),
        step_of(2, 2, 2, 2, 0, INIT),
        step_of(2, 2, 3, 4, 1, INIT, WAIT_Q, 4 * GATHER),
        step_of(2, 1, 2, 2, 0, WAIT_KV),
        step_of(2, 1, 3, 4, 1),
        step_of(2, 3, 3, 4, 1, WAIT_KV),
        step_of(2, 0, 2, 2, 0, WAIT_KV, FINAL),
        step_of(2, 0, 3, 4, 1, FINAL, SEND),
    ],
    [
        step_of(0, 3, 3, 0, 0, INIT),
        step_of(1, 3, 3, 1, 1, INIT, 3 * HOP),
        step_of(0, 2, 3, 0, 0, WAIT_KV, 3 * GATHER),
        step_of(1, 2, 3, 1, 1, WAIT_KV, 2 * HOP),
        step_of(0, 1, 3, 0, 0, WAIT_KV, 2 * GATHER),
        step_of(1, 1, 3, 1, 1, WAIT_KV, HOP),
        step_of(0, 0, 3, 0, 0, WAIT_KV, GATHER, FINAL, SEND),
        step_of(1, 0, 3, 1, 1, WAIT_KV, FINAL, SEND),
    ],
)


def balanced_kernel(
    subs, peers, mix_scale,
    q_hbm, k_hbm, v_hbm, g_hbm, x_hbm, seed_hbm, out_ref,
    x_ref, seed_ref, qg, kv, pg_s, w_s, z_s, dn_s, pm_s, acc_s, db_s,
    part, part_in, mixed_s, sketch, stage, stage_in, fold_in,
    kv_send, kv_recv, q_send, q_recv, part_send, part_recv, hop_send, hop_recv,
    share_send, share_recv, row_send, row_recv, fold_send, fold_recv, load_sem,
):
    shards, kv_heads = 4, 4
    tokens = qg.shape[3]
    groups = qg.shape[2]
    chunks = tokens // CHUNK
    share = tokens // peers
    own_rows = sketch.shape[2]
    me = lax.axis_index("seq")
    peer = lax.axis_index("head") * subs + lax.axis_index("sub")

    def cols(head):
        return pl.ds(pl.multiple_of(head * HEAD, HEAD), HEAD)

    def peer_at(offset):
        other = lax.rem(peer + offset, peers)
        return other, {"head": lax.div(other, subs), "sub": lax.rem(other, subs)}

    def seq_at(offset):
        other = lax.rem(me + offset, shards)
        return other, {"seq": other}

    def remote(src, dst, send, recv, device):
        return pltpu.make_async_remote_copy(
            src_ref=src, dst_ref=dst, send_sem=send, recv_sem=recv,
            device_id=device, device_id_type=MESH,
        )

    def loop(low, high, fn):
        def step(i, carry):
            fn(i)
            return carry

        lax.fori_loop(low, high, step, 0)

    def kv_hop(h, b, way=1):
        return remote(
            kv.at[h, b], kv.at[h, b], kv_send.at[h, b], kv_recv.at[h, b], {"seq": me + way}
        )

    def q_hop(source, target):
        at = target - FOREIGN
        return remote(
            qg.at[source], qg.at[target], q_send.at[at], q_recv.at[at], {"seq": me - 1}
        )

    def part_copy(offset):
        other, device = peer_at(offset)
        rows = pl.ds(pl.multiple_of(other * share, share), share)
        return remote(
            part.at[rows], part_in.at[offset], part_send.at[offset], part_recv.at[offset], device
        )

    mine = pl.ds(pl.multiple_of(peer * share, share), share)

    def mixed_hop(b, way):
        return remote(
            mixed_s.at[b, mine], mixed_s.at[b, mine], hop_send.at[b, (way + 1) // 2],
            hop_recv.at[b], {"seq": me + way},
        )

    def mixed_share(b, offset):
        _, device = peer_at(offset)
        return remote(
            mixed_s.at[b, mine], mixed_s.at[b, mine], share_send.at[b, offset],
            share_recv.at[b, offset], device,
        )

    def row_copy(h, target, sender):
        return remote(
            stage.at[h, target], stage_in.at[h, sender], row_send.at[h, target],
            row_recv.at[h, sender], {"seq": target},
        )

    def fold_copy(h):
        return remote(
            stage.at[h, pl.ds(1, shards - 1)], fold_in.at[h], fold_send.at[h], fold_recv.at[h],
            {"seq": 1},
        )

    barrier = pltpu.get_barrier_semaphore()

    def greet_peer(offset):
        pl.semaphore_signal(barrier, inc=1, device_id=peer_at(offset)[1], device_id_type=MESH)

    def greet_seq(offset):
        pl.semaphore_signal(barrier, inc=1, device_id=seq_at(offset)[1], device_id_type=MESH)

    loop(1, peers, greet_peer)
    loop(1, shards, greet_seq)

    def load_kv(h, which):
        source = (k_hbm, v_hbm)[which]
        return pltpu.make_async_copy(
            source.at[:, cols(h)], kv.at[h, me, which], load_sem.at[2 + which * kv_heads + h]
        )

    def load_qg(h, which, member):
        source = (q_hbm, g_hbm)[which]
        at = 2 + 2 * kv_heads + (h * 2 + which) * groups + member
        return pltpu.make_async_copy(
            source.at[:, cols(h * groups + member)], qg.at[h, which, member], load_sem.at[at]
        )

    load_seed = pltpu.make_async_copy(seed_hbm, seed_ref, load_sem.at[0])
    load_x = pltpu.make_async_copy(x_hbm, x_ref, load_sem.at[1])

    def each_kv(fn):
        for which in range(2):
            loop(0, kv_heads, lambda h: fn(load_kv(h, which)))

    def each_qg(fn):
        for which in range(2):
            for member in range(groups):
                loop(0, kv_heads, lambda h: fn(load_qg(h, which, member)))

    each_kv(lambda copy: copy.start())
    load_seed.start()
    load_x.start()
    each_qg(lambda copy: copy.start())
    each_kv(lambda copy: copy.wait())
    pl.semaphore_wait(barrier, peers + shards - 2)

    @pl.when(me < 3)
    def _():
        kv_hop(0, me).start()

    @pl.when(me > 1)
    def _():
        kv_hop(3, me, -1).start()

    load_seed.wait()
    load_x.wait()
    seeds = seed_ref[...].astype(jnp.float32).astype(jnp.bfloat16)
    part[...] = mm(seeds, x_ref[...], ((0,), (0,))).T
    loop(1, peers, lambda offset: part_copy(offset).start())
    part_in[0] = part[mine, :]
    loop(1, peers, lambda offset: part_copy(offset).wait_recv())
    total = part_in[0]
    for offset in range(1, peers):
        total = total + part_in[offset]
    mixed_s[me, mine, :] = (total * mix_scale).astype(jnp.bfloat16)

    def spread(b):
        loop(1, peers, lambda offset: mixed_share(b, offset).start())

    def pass_mixed(b):
        mixed_hop(b, 1).wait_recv()

        @pl.when((b < me) & (me < shards - 1))
        def _():
            mixed_hop(b, 1).start()

        @pl.when((b > me) & (me > 1))
        def _():
            mixed_hop(b, -1).start()

        spread(b)

    def gathered(b):
        loop(1, peers, lambda offset: mixed_share(b, offset).wait_recv())

    @pl.when(me < shards - 1)
    def _():
        mixed_hop(me, 1).start()

    @pl.when(me > 1)
    def _():
        mixed_hop(me, -1).start()

    spread(me)
    each_qg(lambda copy: copy.wait())

    @pl.when(me == 0)
    def _():
        loop(1, kv_heads, lambda h: kv_hop(h, 0).start())

    @pl.when(me == 1)
    def _():
        kv_hop(1, 1).start()

    @pl.when(me == 2)
    def _():
        kv_hop(1, 2).start()
        q_hop(3, 4).start()

    @pl.when(me == 3)
    def _():
        q_hop(3, 5).start()
        q_hop(2, 4).start()
        kv_hop(2, 3, -1).start()

    sketch[...] = jnp.zeros_like(sketch)

    def first_pass(h, b, slot, half, d, c, row0, causal):
        rows = tokens - row0
        at = pl.ds(row0, rows)
        keys = pl.ds(c * CHUNK, CHUNK)
        qh = qg[slot, 0, :, at, :].reshape(groups * rows, HEAD)
        gh = qg[slot, 1, :, at, :].reshape(groups * rows, HEAD)
        scores = mm(qh, kv[h, b, 0, keys, :], ((1,), (1,)))
        weight = mm(gh, kv[h, b, 1, keys, :], ((1,), (1,)))
        bounded = jnp.tanh(scores * (QUERY_SCALE / CAP))
        power = jnp.exp2(bounded * (CAP / math.log(2.0)))
        if causal:
            qi = lax.broadcasted_iota(jnp.int32, (groups, rows, CHUNK), 1)
            kj = lax.broadcasted_iota(jnp.int32, (groups, rows, CHUNK), 2)
            keep = (row0 + qi >= c * CHUNK + kj).reshape(groups * rows, CHUNK)
            power = jnp.where(keep, power, 0.0)
        whole = (groups, rows, CHUNK)
        folded = (groups, rows, HEAD)
        put = half * shards + d
        pg_s[put, c, :, at, :] = (power - power * (bounded * bounded)).reshape(whole)
        w_s[put, c, :, at, :] = weight.reshape(whole)
        pw = power * weight
        z_s[half, :, at, :] += (power[:, :HEAD] + power[:, HEAD:]).reshape(folded)
        dn_s[half, :, at, :] += (pw[:, :HEAD] + pw[:, HEAD:]).reshape(folded)
        pm = mm(power.astype(jnp.bfloat16), mixed_s[b, keys, :], ((1,), (0,)))
        pm_s[half, :, at, :] += pm.reshape(folded)

    def second_pass(h, b, half, d, c, row0):
        rows = tokens - row0
        at = pl.ds(row0, rows)
        keys = pl.ds(c * CHUNK, CHUNK)
        put = half * shards + d
        dot = db_s[:, at, :]
        grad = pg_s[put, c, :, at, :] * (w_s[put, c, :, at, :] - jnp.concatenate([dot, dot], 2))
        sides = jnp.concatenate([kv[h, b, 0, keys, :], mixed_s[b, keys, :]], 1)
        term = mm(grad.astype(jnp.bfloat16).reshape(groups * rows, CHUNK), sides, ((1,), (0,)))
        acc_s[:, at, :] += term.reshape(groups, rows, 2 * HEAD)

    def finish_row(h, row, slot, half):
        inverse = 1.0 / jnp.sum(z_s[half], axis=2, keepdims=True)
        dot = jnp.sum(dn_s[half], axis=2, keepdims=True) * inverse
        db_s[...] = jnp.broadcast_to(dot, db_s.shape)
        acc_s[...] = jnp.zeros_like(acc_s)
        for c in range(chunks):
            second_pass(h, row, half, 0, c, c * CHUNK)

        def rest(d):
            for c in range(chunks):
                second_pass(h, row - d, half, d, c, 0)

        loop(1, row + 1, rest)
        scale = inverse * QUERY_SCALE
        dq = (acc_s[:, :, :HEAD] * scale).astype(jnp.bfloat16)
        dm = (acc_s[:, :, HEAD:] * scale).astype(jnp.bfloat16)
        pm = (pm_s[half] * inverse).astype(jnp.bfloat16)
        stacked = (groups * tokens, HEAD)
        blocked = (shards, own_rows, HEAD)
        k_part = mm(dm.reshape(stacked), qg[slot, 0].reshape(stacked), ((0,), (0,)))
        v_part = mm(pm.reshape(stacked), qg[slot, 1].reshape(stacked), ((0,), (0,)))
        sketch[h, :, :, :HEAD] += k_part.reshape(blocked)
        sketch[h, :, :, HEAD : 2 * HEAD] += v_part.reshape(blocked)
        q_part = mm(mixed_s[row], jnp.concatenate([dq[m] for m in range(groups)], 1), ((0,), (0,)))
        sketch[h, :, :, 2 * HEAD :] += q_part.reshape(shards, own_rows, groups * HEAD)

    def send_head(h):
        @pl.when(me == 1)
        def _():
            fold_copy(h).wait_recv()
            sketch[h, pl.ds(1, shards - 1)] += fold_in[h].astype(jnp.float32)

        stage[h] = sketch[h].astype(stage.dtype)

        @pl.when(me == 0)
        def _():
            fold_copy(h).start()

        @pl.when(me > 0)
        def _():
            loop(1, shards, lambda offset: row_copy(h, seq_at(offset)[0], me).start())

    def one_step(index):
        code = jnp.int32(0)
        for shard, codes in enumerate(STEPS):
            for i, value in enumerate(codes):
                code = jnp.where((me == shard) & (index == i), value, code)

        def field(unit, size):
            return lax.rem(lax.div(code, unit), size)

        def flag(unit):
            return field(unit, 2) == 1

        h, b, row = field(STEP_H, 4), field(STEP_B, 4), field(STEP_ROW, 4)
        slot, half = field(STEP_SLOT, 8), field(STEP_HALF, 2)

        @pl.when(flag(WAIT_Q))
        def _():
            q_hop(slot, slot).wait_recv()

        @pl.when(flag(WAIT_KV))
        def _():
            kv_hop(h, b).wait_recv()

        @pl.when(flag(PASS_KV))
        def _():
            kv_hop(h, b).start()

            @pl.when((me == 1) & (h == 1))
            def _():
                kv_hop(2, 1).start()

        @pl.when(flag(RELAY))
        def _():
            q_hop(5, 5).wait_recv()
            q_hop(5, 5).start()
            kv_hop(3, 3, -1).wait_recv()
            kv_hop(3, 3, -1).start()

        hopped, wanted = field(HOP, 8), field(GATHER, 8)

        @pl.when(hopped > 0)
        def _():
            pass_mixed(hopped - 1)

        @pl.when(wanted > 0)
        def _():
            gathered(wanted - 1)

        @pl.when(flag(INIT))
        def _():
            z_s[half] = jnp.zeros(z_s.shape[1:], z_s.dtype)
            dn_s[half] = jnp.zeros(dn_s.shape[1:], dn_s.dtype)
            pm_s[half] = jnp.zeros(pm_s.shape[1:], pm_s.dtype)

        @pl.when(b == row)
        def _():
            for c in range(chunks):
                first_pass(h, b, slot, half, 0, c, c * CHUNK, True)

        @pl.when(b != row)
        def _():
            for c in range(chunks):
                first_pass(h, b, slot, half, row - b, c, 0, False)

        @pl.when(flag(FINAL))
        def _():
            finish_row(h, row, slot, half)

        @pl.when(flag(SEND))
        def _():
            held = (me == 1) & (row == 1)
            loop(jnp.where(held, 0, h), jnp.where(held, h, h + 1), send_head)

    gathered(me)
    count = jnp.int32(0)
    for shard, codes in enumerate(STEPS):
        count = jnp.where(me == shard, len(codes), count)
    loop(0, count, one_step)

    def heads_of(sender):
        return jnp.where(sender == 2, 3, jnp.where(sender == 3, 2, jnp.where(sender == 1, 4, 0)))

    def collect(h):
        def add(sender):
            @pl.when((sender != me) & (h < heads_of(sender)))
            def _():
                row_copy(h, me, sender).wait_recv()
                sketch[h, me] += stage_in[h, sender].astype(jnp.float32)

        loop(1, shards, add)
        out_ref[h] = sketch[h, me]

    loop(0, kv_heads, collect)

    loop(1, peers, lambda offset: part_copy(offset).wait_send())

    @pl.when(me < shards - 1)
    def _():
        loop(0, me + 1, lambda b: mixed_hop(b, 1).wait_send())

    @pl.when(me > 1)
    def _():
        loop(me, shards, lambda b: mixed_hop(b, -1).wait_send())

    def drain_share(b):
        @pl.when((me > 0) | (b <= 0))
        def _():
            loop(1, peers, lambda offset: mixed_share(b, offset).wait_send())

    loop(0, shards, drain_share)
    loop(
        0, heads_of(me),
        lambda h: loop(1, shards, lambda offset: row_copy(h, seq_at(offset)[0], me).wait_send()),
    )

    @pl.when(me == 0)
    def _():
        loop(0, kv_heads, lambda h: fold_copy(h).wait_send())

    up = jnp.where(me == 0, 4, jnp.where(me == 1, 3, jnp.where(me == 2, 2, 0)))
    loop(0, up, lambda h: loop(0, me + 1, lambda b: kv_hop(h, b).wait_send()))

    @pl.when(me == 2)
    def _():
        kv_hop(3, 2, -1).wait_send()
        kv_hop(3, 3, -1).wait_send()
        q_hop(3, 4).wait_send()
        q_hop(5, 5).wait_send()

    @pl.when(me == 3)
    def _():
        kv_hop(3, 3, -1).wait_send()
        kv_hop(2, 3, -1).wait_send()
        q_hop(3, 5).wait_send()
        q_hop(2, 4).wait_send()


def unpack_kernel(packed, oq_ref, ok_ref, ov_ref):
    kv_heads = packed.shape[0]
    queries = packed.shape[2] - 2 * HEAD
    for h in range(kv_heads):
        ok_ref[:, h * HEAD : (h + 1) * HEAD] = packed[h, :, :HEAD]
        ov_ref[:, h * HEAD : (h + 1) * HEAD] = packed[h, :, HEAD : 2 * HEAD]
        oq_ref[:, h * queries : (h + 1) * queries] = packed[h, :, 2 * HEAD :]


def balanced(queries, key_states, value_states, out_grad, layer_inputs, sketch_seeds):
    tokens, query_width = queries.shape
    kv_width = key_states.shape[1]
    kv_heads = kv_width // HEAD
    groups = query_width // kv_width
    shards = lax.axis_size("seq")
    subs = lax.axis_size("sub")
    peers = lax.axis_size("head") * subs
    features = layer_inputs.shape[0]
    rank = sketch_seeds.shape[1]
    chunks = tokens // CHUNK
    own_rows = rank // shards
    width = (groups + 2) * HEAD
    f32, bf16, dma = jnp.float32, jnp.bfloat16, pltpu.SemaphoreType.DMA
    packed = pl.pallas_call(
        functools.partial(balanced_kernel, subs, peers, (2.0 * D * tokens * shards) ** (-0.5)),
        out_shape=jax.ShapeDtypeStruct((kv_heads, own_rows, width), f32),
        in_specs=[pl.BlockSpec(memory_space=pltpu.HBM)] * 6,
        out_specs=pl.BlockSpec(memory_space=pltpu.VMEM),
        scratch_shapes=[
            pltpu.VMEM((features, tokens), bf16),
            pltpu.VMEM((features, rank), sketch_seeds.dtype),
            pltpu.VMEM((kv_heads + 2, 2, groups, tokens, HEAD), bf16),
            pltpu.VMEM((kv_heads, shards, 2, tokens, HEAD), bf16),
            pltpu.VMEM((2 * shards, chunks, groups, tokens, CHUNK), f32),
            pltpu.VMEM((2 * shards, chunks, groups, tokens, CHUNK), f32),
            pltpu.VMEM((2, groups, tokens, HEAD), f32),
            pltpu.VMEM((2, groups, tokens, HEAD), f32),
            pltpu.VMEM((2, groups, tokens, rank), f32),
            pltpu.VMEM((groups, tokens, HEAD + rank), f32),
            pltpu.VMEM((groups, tokens, HEAD), f32),
            pltpu.VMEM((tokens, rank), f32),
            pltpu.VMEM((peers, tokens // peers, rank), f32),
            pltpu.VMEM((shards, tokens, rank), bf16),
            pltpu.VMEM((kv_heads, shards, own_rows, width), f32),
            pltpu.VMEM((kv_heads, shards, own_rows, width), bf16),
            pltpu.VMEM((kv_heads, shards, own_rows, width), bf16),
            pltpu.VMEM((kv_heads, shards - 1, own_rows, width), bf16),
            dma((kv_heads, shards)), dma((kv_heads, shards)),
            dma((2,)), dma((2,)),
            dma((peers,)), dma((peers,)),
            dma((shards, 2)), dma((shards,)),
            dma((shards, peers)), dma((shards, peers)),
            dma((kv_heads, shards)), dma((kv_heads, shards)),
            dma((kv_heads,)), dma((kv_heads,)),
            dma((2 + 2 * kv_heads * (1 + groups),)),
        ],
        compiler_params=pltpu.CompilerParams(
            collective_id=0, has_side_effects=True, vmem_limit_bytes=62 * 2**20
        ),
    )(queries, key_states, value_states, out_grad, layer_inputs, sketch_seeds)
    return pl.pallas_call(
        unpack_kernel,
        out_shape=(
            jax.ShapeDtypeStruct((own_rows, query_width), f32),
            jax.ShapeDtypeStruct((own_rows, kv_width), f32),
            jax.ShapeDtypeStruct((own_rows, kv_width), f32),
        ),
        in_specs=[pl.BlockSpec(memory_space=pltpu.VMEM)],
        out_specs=(pl.BlockSpec(memory_space=pltpu.VMEM),) * 3,
    )(packed)


def per_device(queries, key_states, value_states, out_grad, layer_inputs, sketch_seeds):
    tokens, query_width = queries.shape
    kv_width = key_states.shape[1]
    kv_heads = kv_width // HEAD
    shards = lax.axis_size("seq")
    length = tokens * shards
    reach_full = WINDOW // tokens
    reach = min(reach_full, shards - 1)
    rank = sketch_seeds.shape[1]
    subs = lax.axis_size("sub")
    peers = lax.axis_size("head") * subs
    groups = query_width // kv_width
    if shards == 4 and kv_heads == 4 and reach < reach_full and tokens == 2 * CHUNK:
        return balanced(queries, key_states, value_states, out_grad, layer_inputs, sketch_seeds)
    folds = 0
    features = layer_inputs.shape[0]
    slots = (reach + 1) * (tokens // CHUNK)
    own_rows = rank // shards
    width = (query_width + 2 * kv_width) // kv_heads
    f32, bf16, dma = jnp.float32, jnp.bfloat16, pltpu.SemaphoreType.DMA
    return pl.pallas_call(
        functools.partial(
            attention_kernel, shards, reach_full, reach, folds, subs, peers,
            (2.0 * D * length) ** (-0.5),
        ),
        out_shape=(
            jax.ShapeDtypeStruct((own_rows, query_width), f32),
            jax.ShapeDtypeStruct((own_rows, kv_width), f32),
            jax.ShapeDtypeStruct((own_rows, kv_width), f32),
        ),
        in_specs=[pl.BlockSpec(memory_space=pltpu.HBM)] * 6,
        out_specs=(pl.BlockSpec(memory_space=pltpu.VMEM),) * 3,
        scratch_shapes=[
            pltpu.VMEM((tokens, query_width), bf16),
            pltpu.VMEM((tokens, query_width), bf16),
            pltpu.VMEM((features, tokens), bf16),
            pltpu.VMEM((features, rank), sketch_seeds.dtype),
            pltpu.VMEM((max(folds, 1), max(folds, 1), 2, tokens, groups * HEAD), bf16),
            pltpu.VMEM((2 * groups, tokens, HEAD), bf16),
            pltpu.VMEM((kv_heads, shards, 2, tokens, HEAD), bf16),
            pltpu.VMEM((slots, tokens, CHUNK), f32),
            pltpu.VMEM((slots, tokens, CHUNK), f32),
            pltpu.VMEM((tokens, HEAD), f32),
            pltpu.VMEM((tokens, HEAD), f32),
            pltpu.VMEM((tokens, rank), f32),
            pltpu.VMEM((tokens, HEAD + rank), f32),
            pltpu.VMEM((tokens, HEAD), f32),
            pltpu.VMEM((tokens, rank), f32),
            pltpu.VMEM((peers, tokens // peers, rank), f32),
            pltpu.VMEM((shards, tokens, rank), bf16),
            pltpu.VMEM((kv_heads, shards, own_rows, width), f32),
            pltpu.VMEM((kv_heads, shards, own_rows, width), bf16),
            pltpu.VMEM((kv_heads, shards, own_rows, width), bf16),
            dma((kv_heads, shards)), dma((kv_heads, shards)),
            dma((peers,)), dma((peers,)),
            dma((shards,)), dma((shards,)),
            dma((shards, peers)), dma((shards, peers)),
            dma((kv_heads, shards)), dma((kv_heads, shards)),
            dma((max(folds, 1), max(folds, 1))), dma((max(folds, 1), max(folds, 1))),
            dma((4 + 2 * kv_heads,)),
        ],
        compiler_params=pltpu.CompilerParams(
            collective_id=0, has_side_effects=True, vmem_limit_bytes=62 * 2**20
        ),
    )(queries, key_states, value_states, out_grad, layer_inputs, sketch_seeds)


def solution(mesh):
    placed = (
        P(("group", "seq"), ("head", "sub")),
        P(("group", "seq"), ("head", "sub")),
        P(("group", "seq"), ("head", "sub")),
        P(("group", "seq"), ("head", "sub")),
        P(("head", "sub"), ("group", "seq")),
        P(("head", "sub"), None),
    )
    return jax.shard_map(
        per_device,
        mesh=mesh,
        in_specs=placed,
        out_specs=(
            P(("group", "seq"), ("head", "sub")),
            P(("group", "seq"), ("head", "sub")),
            P(("group", "seq"), ("head", "sub")),
        ),
        check_vma=False,
    )
```

```python
import functools
import math

import jax
import jax.numpy as jnp
from jax import lax
from jax.experimental import pallas as pl
from jax.experimental.pallas import tpu as pltpu
from jax.sharding import PartitionSpec as P

D = 4608
HEAD = 128
WINDOW = 2048
CAP = 50.0
QUERY_SCALE = 144.0 ** (-0.5)
CHUNK = 256
MESH = pl.DeviceIdType.MESH


def mm(left, right, dims):
    return lax.dot_general(left, right, (dims, ((), ())), preferred_element_type=jnp.float32)


def attention_kernel(
    shards, reach_full, reach, folds, subs, peers, mix_scale,
    q_hbm, k_hbm, v_hbm, g_hbm, x_hbm, seed_hbm, oq_ref, ok_ref, ov_ref,
    q_ref, g_ref, x_ref, seed_ref, qg, q_t, kv, pg_s, w_s, z_s, dn_s, pm_s, acc_s, db_s,
    part, part_in, mixed_s, sketch, stage, stage_in,
    send_sem, recv_sem, part_send, part_recv, hop_send, hop_recv, share_send, share_recv,
    row_send, row_recv, qg_send, qg_recv, load_sem,
):
    tokens = q_ref.shape[0]
    query_width = q_ref.shape[1]
    kv_width = k_hbm.shape[1]
    kv_heads = kv_width // HEAD
    groups = query_width // kv_width
    chunks = tokens // CHUNK
    share = tokens // peers
    me = lax.axis_index("seq")
    peer = lax.axis_index("head") * subs + lax.axis_index("sub")
    blocks = jnp.minimum(me, reach)

    def last(h):
        return shards - 1 - jnp.maximum(h - (kv_heads - 1 - folds), 0)


    def cols(head):
        return pl.ds(pl.multiple_of(head * HEAD, HEAD), HEAD)

    def peer_at(offset):
        other = lax.rem(peer + offset, peers)
        return other, {"head": lax.div(other, subs), "sub": lax.rem(other, subs)}

    def seq_at(offset):
        other = lax.rem(me + offset, shards)
        return other, {"seq": other}

    def remote(src, dst, send, recv, device):
        return pltpu.make_async_remote_copy(
            src_ref=src, dst_ref=dst, send_sem=send, recv_sem=recv,
            device_id=device, device_id_type=MESH,
        )

    def loop(low, high, fn):
        def step(i, carry):
            fn(i)
            return carry

        lax.fori_loop(low, high, step, 0)

    def hop(h, b, way=1):
        return remote(
            kv.at[h, b], kv.at[h, b], send_sem.at[h, b], recv_sem.at[h, b], {"seq": me + way}
        )

    def row_hop(h, row):
        at = (h - (kv_heads - folds), row - (shards - folds))
        return remote(
            qg.at[at], qg.at[at], qg_send.at[at], qg_recv.at[at], {"seq": me - 1}
        )

    def part_copy(offset):
        other, device = peer_at(offset)
        rows = pl.ds(pl.multiple_of(other * share, share), share)
        return remote(
            part.at[rows], part_in.at[offset], part_send.at[offset], part_recv.at[offset], device
        )

    mine = pl.ds(pl.multiple_of(peer * share, share), share)

    def mixed_along(offset):
        _, device = seq_at(offset)
        return remote(
            mixed_s.at[me, mine], mixed_s.at[me, mine], hop_send.at[offset], hop_recv.at[offset],
            device,
        )

    def mixed_share(b, offset):
        _, device = peer_at(offset)
        return remote(
            mixed_s.at[b, mine], mixed_s.at[b, mine], share_send.at[b, offset],
            share_recv.at[b, offset], device,
        )

    def row_copy(h, offset):
        other, device = seq_at(offset)
        return remote(
            stage.at[h, other], stage_in.at[h, offset], row_send.at[h, offset],
            row_recv.at[h, offset], device,
        )

    barrier = pltpu.get_barrier_semaphore()

    def greet_peer(offset):
        pl.semaphore_signal(barrier, inc=1, device_id=peer_at(offset)[1], device_id_type=MESH)

    def greet_seq(offset):
        pl.semaphore_signal(barrier, inc=1, device_id=seq_at(offset)[1], device_id_type=MESH)

    loop(1, peers, greet_peer)
    loop(1, shards, greet_seq)
    def load_kv(h, which):
        source = (k_hbm, v_hbm)[which]
        return pltpu.make_async_copy(
            source.at[:, cols(h)], kv.at[h, me, which], load_sem.at[4 + which * kv_heads + h]
        )

    loads = [
        pltpu.make_async_copy(source, target, load_sem.at[i])
        for i, (source, target) in enumerate(
            ((seed_hbm, seed_ref), (x_hbm, x_ref), (q_hbm, q_ref), (g_hbm, g_ref))
        )
    ]
    for h in range(kv_heads):
        load_kv(h, 0).start()
        load_kv(h, 1).start()
    for load in loads:
        load.start()
    for h in range(kv_heads):
        load_kv(h, 0).wait()
        load_kv(h, 1).wait()
    pl.semaphore_wait(barrier, peers + shards - 2)

    early = 1

    def send_own(low, high):
        def one(h):
            @pl.when(me < last(h))
            def _():
                hop(h, me).start()

        if reach > 0:
            loop(low, high, one)

    def send_folded(h):
        @pl.when(me > last(h))
        def _():
            at = (h - (kv_heads - folds), me - (shards - folds))
            width = groups * HEAD
            qg[at + (0,)] = q_ref[:, h * width : (h + 1) * width]
            qg[at + (1,)] = g_ref[:, h * width : (h + 1) * width]
            if h < kv_heads - 1:
                hop(h, me, -1).start()
            row_hop(h, me).start()

    send_own(0, early)
    if folds > 0:
        @pl.when(me > last(kv_heads - 1))
        def _():
            hop(kv_heads - 1, me, -1).start()

    loads[0].wait()
    loads[1].wait()
    seeds = seed_ref[...].astype(jnp.float32).astype(jnp.bfloat16)
    part[...] = mm(seeds, x_ref[...], ((0,), (0,))).T
    loop(1, peers, lambda offset: part_copy(offset).start())
    part_in[0] = part[mine, :]
    loop(1, peers, lambda offset: part_copy(offset).wait_recv())
    total = part_in[0]
    for offset in range(1, peers):
        total = total + part_in[offset]
    mixed_s[me, mine, :] = (total * mix_scale).astype(jnp.bfloat16)

    def spread(b):
        loop(1, peers, lambda offset: mixed_share(b, offset).start())

    def spread_from(offset):
        mixed_along(offset).wait_recv()
        spread(seq_at(shards - offset)[0])

    def gathered(b):
        loop(1, peers, lambda offset: mixed_share(b, offset).wait_recv())

    loop(1, shards, lambda offset: mixed_along(offset).start())
    spread(me)
    send_own(early, kv_heads)
    loads[2].wait()
    loads[3].wait()
    for h in reversed(range(kv_heads - folds, kv_heads)):
        send_folded(h)
    loop(1, shards, spread_from)

    def first_pass(h, row, qh, gh, d, c, row0, kind):
        rows = tokens - row0
        kk = kv[h, row - d, 0, pl.ds(c * CHUNK, CHUNK), :]
        vv = kv[h, row - d, 1, pl.ds(c * CHUNK, CHUNK), :]
        mixed = mixed_s[row - d, pl.ds(c * CHUNK, CHUNK), :]
        scores = mm(qh[row0:], kk, ((1,), (1,)))
        weight = mm(gh[row0:], vv, ((1,), (1,)))
        bounded = jnp.tanh(scores * (QUERY_SCALE / CAP))
        power = jnp.exp2(bounded * (CAP / math.log(2.0)))
        if kind is not None:
            qi = row0 + lax.broadcasted_iota(jnp.int32, (rows, CHUNK), 0)
            kj = c * CHUNK + lax.broadcasted_iota(jnp.int32, (rows, CHUNK), 1)
            keep = qi >= kj if kind == "causal" else qi < kj
            power = jnp.where(keep, power, 0.0)
        slot = d * chunks + c
        pg_s[slot, pl.ds(row0, rows), :] = power - power * (bounded * bounded)
        w_s[slot, pl.ds(row0, rows), :] = weight
        pw = power * weight
        at = pl.ds(row0, rows)
        z_s[at, :] += power[:, :HEAD] + power[:, HEAD:]
        dn_s[at, :] += pw[:, :HEAD] + pw[:, HEAD:]
        pm_s[at, :] += mm(power.astype(jnp.bfloat16), mixed, ((1,), (0,)))

    def second_pass(h, row, d, c, row0):
        rows = tokens - row0
        at = pl.ds(row0, rows)
        slot = d * chunks + c
        kk = kv[h, row - d, 0, pl.ds(c * CHUNK, CHUNK), :]
        mixed = mixed_s[row - d, pl.ds(c * CHUNK, CHUNK), :]
        dot = db_s[at, :]
        grad = pg_s[slot, at, :] * (w_s[slot, at, :] - jnp.concatenate([dot, dot], 1))
        acc_s[at, :] += mm(
            grad.astype(jnp.bfloat16), jnp.concatenate([kk, mixed], 1), ((1,), (0,))
        )

    full = reach if reach < reach_full else reach_full - 1

    def each_block(row, fn):
        for c in range(chunks):
            fn(0, c, c * CHUNK, "causal")

        def step(d, carry):
            for c in range(chunks):
                fn(d, c, 0, None)
            return carry

        lax.fori_loop(1, jnp.minimum(row, full) + 1, step, 0)
        if full < reach:
            @pl.when(row >= reach)
            def _():
                for c in range(chunks):
                    fn(reach, c, 0, "window")

    def arrivals(h):
        def arrive(d):
            hop(h, me - d).wait_recv()

            @pl.when((me < last(h)) & (d < reach))
            def _():
                hop(h, me - d).start()

        @pl.when(me <= last(h))
        def _():
            loop(1, blocks + 1, arrive)

    def pass_folded():
        for folded in reversed(range(kv_heads - folds, kv_heads)):
            for row in range(shards - folds + 1, shards):
                @pl.when((me > last(folded)) & (me < row))
                def _():
                    hop(folded, row, -1).wait_recv()
                    hop(folded, row, -1).start()
                    row_hop(folded, row).wait_recv()
                    row_hop(folded, row).start()

    def kv_head(h, carry):
        @pl.when((h > 1) | ((h == 1) & (me != 1)))
        def _():
            arrivals(h)

        count = jnp.where(me < last(h), 1, jnp.where(me == last(h), shards - last(h), 0))
        loop(0, count, lambda extra: row_task(h, me + extra, extra))

        @pl.when(me <= last(h))
        def _():
            stage[h] = sketch[h].astype(stage.dtype)
            loop(1, shards, lambda offset: row_copy(h, offset).start())

        return carry

    def row_task(h, row, extra):
        if folds > 0:
            @pl.when(extra > 0)
            def _():
                hop(h, row, -1).wait_recv()
                row_hop(h, row).wait_recv()
                at = (h - (kv_heads - folds), row - (shards - folds))
                for member in range(groups):
                    q_t[member] = qg[at + (0, slice(None), pl.ds(member * HEAD, HEAD))]
                    q_t[groups + member] = qg[at + (1, slice(None), pl.ds(member * HEAD, HEAD))]

        @pl.when(extra == 0)
        def _():
            for member in range(groups):
                q_t[member] = q_ref[:, cols(h * groups + member)]
                q_t[groups + member] = g_ref[:, cols(h * groups + member)]

        own_mixed = mixed_s[row]

        def member_step(member, inner):
            qh = q_t[member]
            gh = q_t[groups + member]
            z_s[...] = jnp.zeros_like(z_s)
            dn_s[...] = jnp.zeros_like(dn_s)
            pm_s[...] = jnp.zeros_like(pm_s)
            acc_s[...] = jnp.zeros_like(acc_s)
            each_block(row, lambda d, c, row0, kind: first_pass(h, row, qh, gh, d, c, row0, kind))
            inverse = 1.0 / jnp.sum(z_s[...], axis=1, keepdims=True)
            dot = jnp.sum(dn_s[...], axis=1, keepdims=True) * inverse
            db_s[...] = jnp.broadcast_to(dot, db_s.shape)
            each_block(row, lambda d, c, row0, kind: second_pass(h, row, d, c, row0))
            scale = inverse * QUERY_SCALE
            dq = (acc_s[:, :HEAD] * scale).astype(jnp.bfloat16)
            dm = (acc_s[:, HEAD:] * scale).astype(jnp.bfloat16)
            pm = (pm_s[...] * inverse).astype(jnp.bfloat16)
            q_part = mm(own_mixed, dq, ((0,), (0,)))
            k_part = mm(dm, qh, ((0,), (0,)))
            v_part = mm(pm, gh, ((0,), (0,)))
            blocked = (shards, own_rows, HEAD)
            sketch[h, :, :, cols(2 + member)] += q_part.reshape(blocked)
            sketch[h, :, :, :HEAD] += k_part.reshape(blocked)
            sketch[h, :, :, HEAD : 2 * HEAD] += v_part.reshape(blocked)
            return inner

        lax.fori_loop(0, groups, member_step, 0)

    sketch[...] = jnp.zeros_like(sketch)
    own_rows = sketch.shape[2]
    arrivals(0)
    pass_folded()
    if kv_heads > 1:
        @pl.when(me == 1)
        def _():
            arrivals(1)

    loop(0, shards, gathered)
    lax.fori_loop(0, kv_heads, kv_head, 0)

    def collect(h):
        def add(offset):
            @pl.when(seq_at(shards - offset)[0] <= last(h))
            def _():
                row_copy(h, offset).wait_recv()
                sketch[h, me] += stage_in[h, offset].astype(jnp.float32)

        loop(1, shards, add)
        rows = sketch[h, me]
        ok_ref[:, cols(h)] = rows[:, :HEAD]
        ov_ref[:, cols(h)] = rows[:, HEAD : 2 * HEAD]
        for member in range(groups):
            oq_ref[:, cols(h * groups + member)] = rows[:, (2 + member) * HEAD : (3 + member) * HEAD]

    loop(0, kv_heads, collect)

    loop(1, peers, lambda offset: part_copy(offset).wait_send())
    loop(1, shards, lambda offset: mixed_along(offset).wait_send())
    loop(0, shards, lambda b: loop(1, peers, lambda offset: mixed_share(b, offset).wait_send()))

    def drain_rows(h):
        @pl.when(me <= last(h))
        def _():
            loop(1, shards, lambda offset: row_copy(h, offset).wait_send())

    loop(0, kv_heads, drain_rows)

    def drain(h):
        @pl.when(me < last(h))
        def _():
            loop(0, jnp.minimum(me, reach - 1) + 1, lambda d: hop(h, me - d).wait_send())

    if reach > 0:
        loop(0, kv_heads, drain)
    for h in range(kv_heads - folds, kv_heads):
        for row in range(shards - folds, shards):
            @pl.when((me > last(h)) & (me <= row))
            def _():
                hop(h, row, -1).wait_send()
                row_hop(h, row).wait_send()


STEP_H, STEP_B, STEP_ROW, STEP_SLOT, STEP_HALF = 1, 4, 16, 64, 512
INIT, FINAL, SEND, WAIT_KV, PASS_KV, WAIT_Q, RELAY = (1024 << i for i in range(7))
HOP, GATHER = 1 << 19, 1 << 22
FOREIGN = 4


def step_of(h, b, row, slot, half, *flags):
    return h * STEP_H + b * STEP_B + row * STEP_ROW + slot * STEP_SLOT + half * STEP_HALF + sum(flags)


STEPS = (
    [step_of(h, 0, 0, h, 0, INIT, FINAL, SEND) for h in range(4)],
    [
        step_of(0, 1, 1, 0, 0, INIT),
        step_of(1, 1, 1, 1, 1, INIT, HOP),
        step_of(0, 0, 1, 0, 0, WAIT_KV, PASS_KV, GATHER, FINAL),
        step_of(1, 0, 1, 1, 1, WAIT_KV, PASS_KV, FINAL),
        step_of(2, 1, 1, 2, 0, INIT, 3 * HOP),
        step_of(2, 0, 1, 2, 0, WAIT_KV, PASS_KV, FINAL),
        step_of(3, 1, 1, 3, 0, INIT, 4 * HOP),
        step_of(3, 0, 1, 3, 0, WAIT_KV, FINAL, SEND),
        step_of(3, 1, 2, 4, 0, INIT, WAIT_Q, 3 * GATHER),
        step_of(3, 0, 2, 4, 0),
        step_of(3, 2, 2, 4, 0, WAIT_KV, FINAL),
        step_of(3, 1, 3, 5, 0, INIT, WAIT_Q, 4 * GATHER),
        step_of(3, 0, 3, 5, 0),
        step_of(3, 2, 3, 5, 0),
        step_of(3, 3, 3, 5, 0, WAIT_KV, FINAL, SEND),
    ],
    [
        step_of(0, 2, 2, 0, 0, INIT),
        step_of(1, 2, 2, 1, 1, INIT, 2 * HOP),
        step_of(0, 1, 2, 0, 0, WAIT_KV, PASS_KV, 4 * HOP, 2 * GATHER),
        step_of(1, 1, 2, 1, 1, WAIT_KV, PASS_KV, HOP),
        step_of(0, 0, 2, 0, 0, WAIT_KV, PASS_KV, RELAY, GATHER, FINAL, SEND),
        step_of(1, 0, 2, 1, 1, WAIT_KV, PASS_KV, FINAL, SEND),
        step_of(2, 2, 2, 2, 0, INIT),
        step_of(2, 2, 3, 4, 1, INIT, WAIT_Q, 4 * GATHER),
        step_of(2, 1, 2, 2, 0, WAIT_KV),
        step_of(2, 1, 3, 4, 1),
        step_of(2, 3, 3, 4, 1, WAIT_KV),
        step_of(2, 0, 2, 2, 0, WAIT_KV, FINAL),
        step_of(2, 0, 3, 4, 1, FINAL, SEND),
    ],
    [
        step_of(0, 3, 3, 0, 0, INIT),
        step_of(1, 3, 3, 1, 1, INIT, 3 * HOP),
        step_of(0, 2, 3, 0, 0, WAIT_KV, 3 * GATHER),
        step_of(1, 2, 3, 1, 1, WAIT_KV, 2 * HOP),
        step_of(0, 1, 3, 0, 0, WAIT_KV, 2 * GATHER),
        step_of(1, 1, 3, 1, 1, WAIT_KV, HOP),
        step_of(0, 0, 3, 0, 0, WAIT_KV, GATHER, FINAL, SEND),
        step_of(1, 0, 3, 1, 1, WAIT_KV, FINAL, SEND),
    ],
)


def balanced_kernel(
    subs, peers, mix_scale,
    q_hbm, k_hbm, v_hbm, g_hbm, x_hbm, seed_hbm, out_ref,
    x_ref, seed_ref, qg, kv, pg_s, w_s, z_s, dn_s, pm_s, acc_s, db_s,
    part, part_in, mixed_s, sketch, stage, stage_in, fold_in,
    kv_send, kv_recv, q_send, q_recv, part_send, part_recv, hop_send, hop_recv,
    share_send, share_recv, row_send, row_recv, fold_send, fold_recv, load_sem,
):
    shards, kv_heads = 4, 4
    tokens = qg.shape[3]
    groups = qg.shape[2]
    chunks = tokens // CHUNK
    share = tokens // peers
    own_rows = sketch.shape[2]
    me = lax.axis_index("seq")
    peer = lax.axis_index("head") * subs + lax.axis_index("sub")

    def cols(head):
        return pl.ds(pl.multiple_of(head * HEAD, HEAD), HEAD)

    def peer_at(offset):
        other = lax.rem(peer + offset, peers)
        return other, {"head": lax.div(other, subs), "sub": lax.rem(other, subs)}

    def seq_at(offset):
        other = lax.rem(me + offset, shards)
        return other, {"seq": other}

    def remote(src, dst, send, recv, device):
        return pltpu.make_async_remote_copy(
            src_ref=src, dst_ref=dst, send_sem=send, recv_sem=recv,
            device_id=device, device_id_type=MESH,
        )

    def loop(low, high, fn):
        def step(i, carry):
            fn(i)
            return carry

        lax.fori_loop(low, high, step, 0)

    def kv_hop(h, b, way=1):
        return remote(
            kv.at[h, b], kv.at[h, b], kv_send.at[h, b], kv_recv.at[h, b], {"seq": me + way}
        )

    def q_hop(source, target):
        at = target - FOREIGN
        return remote(
            qg.at[source], qg.at[target], q_send.at[at], q_recv.at[at], {"seq": me - 1}
        )

    def part_copy(offset):
        other, device = peer_at(offset)
        rows = pl.ds(pl.multiple_of(other * share, share), share)
        return remote(
            part.at[rows], part_in.at[offset], part_send.at[offset], part_recv.at[offset], device
        )

    mine = pl.ds(pl.multiple_of(peer * share, share), share)

    def mixed_hop(b, way):
        return remote(
            mixed_s.at[b, mine], mixed_s.at[b, mine], hop_send.at[b, (way + 1) // 2],
            hop_recv.at[b], {"seq": me + way},
        )

    def mixed_share(b, offset):
        _, device = peer_at(offset)
        return remote(
            mixed_s.at[b, mine], mixed_s.at[b, mine], share_send.at[b, offset],
            share_recv.at[b, offset], device,
        )

    def row_copy(h, target, sender):
        return remote(
            stage.at[h, target], stage_in.at[h, sender], row_send.at[h, target],
            row_recv.at[h, sender], {"seq": target},
        )

    def fold_copy(h):
        return remote(
            stage.at[h, pl.ds(1, shards - 1)], fold_in.at[h], fold_send.at[h], fold_recv.at[h],
            {"seq": 1},
        )

    barrier = pltpu.get_barrier_semaphore()

    def greet_peer(offset):
        pl.semaphore_signal(barrier, inc=1, device_id=peer_at(offset)[1], device_id_type=MESH)

    def greet_seq(offset):
        pl.semaphore_signal(barrier, inc=1, device_id=seq_at(offset)[1], device_id_type=MESH)

    loop(1, peers, greet_peer)
    loop(1, shards, greet_seq)

    def load_kv(h, which):
        source = (k_hbm, v_hbm)[which]
        return pltpu.make_async_copy(
            source.at[:, cols(h)], kv.at[h, me, which], load_sem.at[2 + which * kv_heads + h]
        )

    def load_qg(h, which, member):
        source = (q_hbm, g_hbm)[which]
        at = 2 + 2 * kv_heads + (h * 2 + which) * groups + member
        return pltpu.make_async_copy(
            source.at[:, cols(h * groups + member)], qg.at[h, which, member], load_sem.at[at]
        )

    load_seed = pltpu.make_async_copy(seed_hbm, seed_ref, load_sem.at[0])
    load_x = pltpu.make_async_copy(x_hbm, x_ref, load_sem.at[1])

    def each_kv(fn):
        for which in range(2):
            loop(0, kv_heads, lambda h: fn(load_kv(h, which)))

    def each_qg(fn):
        for which in range(2):
            for member in range(groups):
                loop(0, kv_heads, lambda h: fn(load_qg(h, which, member)))

    each_kv(lambda copy: copy.start())
    load_seed.start()
    load_x.start()
    each_qg(lambda copy: copy.start())
    each_kv(lambda copy: copy.wait())
    pl.semaphore_wait(barrier, peers + shards - 2)

    @pl.when(me < 3)
    def _():
        kv_hop(0, me).start()

    @pl.when(me > 1)
    def _():
        kv_hop(3, me, -1).start()

    load_seed.wait()
    load_x.wait()
    seeds = seed_ref[...].astype(jnp.float32).astype(jnp.bfloat16)
    part[...] = mm(seeds, x_ref[...], ((0,), (0,))).T
    loop(1, peers, lambda offset: part_copy(offset).start())
    part_in[0] = part[mine, :]
    loop(1, peers, lambda offset: part_copy(offset).wait_recv())
    total = part_in[0]
    for offset in range(1, peers):
        total = total + part_in[offset]
    mixed_s[me, mine, :] = (total * mix_scale).astype(jnp.bfloat16)

    def spread(b):
        loop(1, peers, lambda offset: mixed_share(b, offset).start())

    def pass_mixed(b):
        mixed_hop(b, 1).wait_recv()

        @pl.when((b < me) & (me < shards - 1))
        def _():
            mixed_hop(b, 1).start()

        @pl.when((b > me) & (me > 1))
        def _():
            mixed_hop(b, -1).start()

        spread(b)

    def gathered(b):
        loop(1, peers, lambda offset: mixed_share(b, offset).wait_recv())

    @pl.when(me < shards - 1)
    def _():
        mixed_hop(me, 1).start()

    @pl.when(me > 1)
    def _():
        mixed_hop(me, -1).start()

    spread(me)
    each_qg(lambda copy: copy.wait())

    @pl.when(me == 0)
    def _():
        loop(1, kv_heads, lambda h: kv_hop(h, 0).start())

    @pl.when(me == 1)
    def _():
        kv_hop(1, 1).start()

    @pl.when(me == 2)
    def _():
        kv_hop(1, 2).start()
        q_hop(3, 4).start()

    @pl.when(me == 3)
    def _():
        q_hop(3, 5).start()
        q_hop(2, 4).start()
        kv_hop(2, 3, -1).start()

    sketch[...] = jnp.zeros_like(sketch)

    def first_pass(h, b, slot, half, d, c, row0, causal):
        rows = tokens - row0
        at = pl.ds(row0, rows)
        keys = pl.ds(c * CHUNK, CHUNK)
        qh = qg[slot, 0, :, at, :].reshape(groups * rows, HEAD)
        gh = qg[slot, 1, :, at, :].reshape(groups * rows, HEAD)
        scores = mm(qh, kv[h, b, 0, keys, :], ((1,), (1,)))
        weight = mm(gh, kv[h, b, 1, keys, :], ((1,), (1,)))
        bounded = jnp.tanh(scores * (QUERY_SCALE / CAP))
        power = jnp.exp2(bounded * (CAP / math.log(2.0)))
        if causal:
            qi = lax.broadcasted_iota(jnp.int32, (groups, rows, CHUNK), 1)
            kj = lax.broadcasted_iota(jnp.int32, (groups, rows, CHUNK), 2)
            keep = (row0 + qi >= c * CHUNK + kj).reshape(groups * rows, CHUNK)
            power = jnp.where(keep, power, 0.0)
        whole = (groups, rows, CHUNK)
        folded = (groups, rows, HEAD)
        put = half * shards + d
        pg_s[put, c, :, at, :] = (power - power * (bounded * bounded)).reshape(whole)
        w_s[put, c, :, at, :] = weight.reshape(whole)
        pw = power * weight
        z_s[half, :, at, :] += (power[:, :HEAD] + power[:, HEAD:]).reshape(folded)
        dn_s[half, :, at, :] += (pw[:, :HEAD] + pw[:, HEAD:]).reshape(folded)
        pm = mm(power.astype(jnp.bfloat16), mixed_s[b, keys, :], ((1,), (0,)))
        pm_s[half, :, at, :] += pm.reshape(folded)

    def second_pass(h, b, half, d, c, row0):
        rows = tokens - row0
        at = pl.ds(row0, rows)
        keys = pl.ds(c * CHUNK, CHUNK)
        put = half * shards + d
        dot = db_s[:, at, :]
        grad = pg_s[put, c, :, at, :] * (w_s[put, c, :, at, :] - jnp.concatenate([dot, dot], 2))
        sides = jnp.concatenate([kv[h, b, 0, keys, :], mixed_s[b, keys, :]], 1)
        term = mm(grad.astype(jnp.bfloat16).reshape(groups * rows, CHUNK), sides, ((1,), (0,)))
        acc_s[:, at, :] += term.reshape(groups, rows, 2 * HEAD)

    def finish_row(h, row, slot, half):
        inverse = 1.0 / jnp.sum(z_s[half], axis=2, keepdims=True)
        dot = jnp.sum(dn_s[half], axis=2, keepdims=True) * inverse
        db_s[...] = jnp.broadcast_to(dot, db_s.shape)
        acc_s[...] = jnp.zeros_like(acc_s)
        for c in range(chunks):
            second_pass(h, row, half, 0, c, c * CHUNK)

        def rest(d):
            for c in range(chunks):
                second_pass(h, row - d, half, d, c, 0)

        loop(1, row + 1, rest)
        scale = inverse * QUERY_SCALE
        dq = (acc_s[:, :, :HEAD] * scale).astype(jnp.bfloat16)
        dm = (acc_s[:, :, HEAD:] * scale).astype(jnp.bfloat16)
        pm = (pm_s[half] * inverse).astype(jnp.bfloat16)
        stacked = (groups * tokens, HEAD)
        blocked = (shards, own_rows, HEAD)
        k_part = mm(dm.reshape(stacked), qg[slot, 0].reshape(stacked), ((0,), (0,)))
        v_part = mm(pm.reshape(stacked), qg[slot, 1].reshape(stacked), ((0,), (0,)))
        sketch[h, :, :, :HEAD] += k_part.reshape(blocked)
        sketch[h, :, :, HEAD : 2 * HEAD] += v_part.reshape(blocked)
        q_part = mm(mixed_s[row], jnp.concatenate([dq[m] for m in range(groups)], 1), ((0,), (0,)))
        sketch[h, :, :, 2 * HEAD :] += q_part.reshape(shards, own_rows, groups * HEAD)

    def send_head(h):
        @pl.when(me == 1)
        def _():
            fold_copy(h).wait_recv()
            sketch[h, pl.ds(1, shards - 1)] += fold_in[h].astype(jnp.float32)

        stage[h] = sketch[h].astype(stage.dtype)

        @pl.when(me == 0)
        def _():
            fold_copy(h).start()

        @pl.when(me > 0)
        def _():
            loop(1, shards, lambda offset: row_copy(h, seq_at(offset)[0], me).start())

    def one_step(index):
        code = jnp.int32(0)
        for shard, codes in enumerate(STEPS):
            for i, value in enumerate(codes):
                code = jnp.where((me == shard) & (index == i), value, code)

        def field(unit, size):
            return lax.rem(lax.div(code, unit), size)

        def flag(unit):
            return field(unit, 2) == 1

        h, b, row = field(STEP_H, 4), field(STEP_B, 4), field(STEP_ROW, 4)
        slot, half = field(STEP_SLOT, 8), field(STEP_HALF, 2)

        @pl.when(flag(WAIT_Q))
        def _():
            q_hop(slot, slot).wait_recv()

        @pl.when(flag(WAIT_KV))
        def _():
            kv_hop(h, b).wait_recv()

        @pl.when(flag(PASS_KV))
        def _():
            kv_hop(h, b).start()

            @pl.when((me == 1) & (h == 1))
            def _():
                kv_hop(2, 1).start()

        @pl.when(flag(RELAY))
        def _():
            q_hop(5, 5).wait_recv()
            q_hop(5, 5).start()
            kv_hop(3, 3, -1).wait_recv()
            kv_hop(3, 3, -1).start()

        hopped, wanted = field(HOP, 8), field(GATHER, 8)

        @pl.when(hopped > 0)
        def _():
            pass_mixed(hopped - 1)

        @pl.when(wanted > 0)
        def _():
            gathered(wanted - 1)

        @pl.when(flag(INIT))
        def _():
            z_s[half] = jnp.zeros(z_s.shape[1:], z_s.dtype)
            dn_s[half] = jnp.zeros(dn_s.shape[1:], dn_s.dtype)
            pm_s[half] = jnp.zeros(pm_s.shape[1:], pm_s.dtype)

        @pl.when(b == row)
        def _():
            for c in range(chunks):
                first_pass(h, b, slot, half, 0, c, c * CHUNK, True)

        @pl.when(b != row)
        def _():
            for c in range(chunks):
                first_pass(h, b, slot, half, row - b, c, 0, False)

        @pl.when(flag(FINAL))
        def _():
            finish_row(h, row, slot, half)

        @pl.when(flag(SEND))
        def _():
            held = (me == 1) & (row == 1)
            loop(jnp.where(held, 0, h), jnp.where(held, h, h + 1), send_head)

    gathered(me)
    count = jnp.int32(0)
    for shard, codes in enumerate(STEPS):
        count = jnp.where(me == shard, len(codes), count)
    loop(0, count, one_step)

    def heads_of(sender):
        return jnp.where(sender == 2, 3, jnp.where(sender == 3, 2, jnp.where(sender == 1, 4, 0)))

    def out_copy(h):
        return pltpu.make_async_copy(sketch.at[h, me], out_ref.at[h], load_sem.at[2 + h])

    def collect(h):
        def add(sender):
            @pl.when((sender != me) & (h < heads_of(sender)))
            def _():
                row_copy(h, me, sender).wait_recv()
                sketch[h, me] += stage_in[h, sender].astype(jnp.float32)

        loop(1, shards, add)
        out_copy(h).start()

    loop(0, kv_heads, collect)
    loop(0, kv_heads, lambda h: out_copy(h).wait())

    loop(1, peers, lambda offset: part_copy(offset).wait_send())

    @pl.when(me < shards - 1)
    def _():
        loop(0, me + 1, lambda b: mixed_hop(b, 1).wait_send())

    @pl.when(me > 1)
    def _():
        loop(me, shards, lambda b: mixed_hop(b, -1).wait_send())

    def drain_share(b):
        @pl.when((me > 0) | (b <= 0))
        def _():
            loop(1, peers, lambda offset: mixed_share(b, offset).wait_send())

    loop(0, shards, drain_share)
    loop(
        0, heads_of(me),
        lambda h: loop(1, shards, lambda offset: row_copy(h, seq_at(offset)[0], me).wait_send()),
    )

    @pl.when(me == 0)
    def _():
        loop(0, kv_heads, lambda h: fold_copy(h).wait_send())

    up = jnp.where(me == 0, 4, jnp.where(me == 1, 3, jnp.where(me == 2, 2, 0)))
    loop(0, up, lambda h: loop(0, me + 1, lambda b: kv_hop(h, b).wait_send()))

    @pl.when(me == 2)
    def _():
        kv_hop(3, 2, -1).wait_send()
        kv_hop(3, 3, -1).wait_send()
        q_hop(3, 4).wait_send()
        q_hop(5, 5).wait_send()

    @pl.when(me == 3)
    def _():
        kv_hop(3, 3, -1).wait_send()
        kv_hop(2, 3, -1).wait_send()
        q_hop(3, 5).wait_send()
        q_hop(2, 4).wait_send()


def unpack_kernel(packed, oq_ref, ok_ref, ov_ref):
    kv_heads = packed.shape[0]
    queries = packed.shape[2] - 2 * HEAD
    for h in range(kv_heads):
        ok_ref[:, h * HEAD : (h + 1) * HEAD] = packed[h, :, :HEAD]
        ov_ref[:, h * HEAD : (h + 1) * HEAD] = packed[h, :, HEAD : 2 * HEAD]
        oq_ref[:, h * queries : (h + 1) * queries] = packed[h, :, 2 * HEAD :]


def balanced(queries, key_states, value_states, out_grad, layer_inputs, sketch_seeds):
    tokens, query_width = queries.shape
    kv_width = key_states.shape[1]
    kv_heads = kv_width // HEAD
    groups = query_width // kv_width
    shards = lax.axis_size("seq")
    subs = lax.axis_size("sub")
    peers = lax.axis_size("head") * subs
    features = layer_inputs.shape[0]
    rank = sketch_seeds.shape[1]
    chunks = tokens // CHUNK
    own_rows = rank // shards
    width = (groups + 2) * HEAD
    f32, bf16, dma = jnp.float32, jnp.bfloat16, pltpu.SemaphoreType.DMA
    packed = pl.pallas_call(
        functools.partial(balanced_kernel, subs, peers, (2.0 * D * tokens * shards) ** (-0.5)),
        out_shape=jax.ShapeDtypeStruct((kv_heads, own_rows, width), f32),
        in_specs=[pl.BlockSpec(memory_space=pltpu.HBM)] * 6,
        out_specs=pl.BlockSpec(memory_space=pl.ANY),
        scratch_shapes=[
            pltpu.VMEM((features, tokens), bf16),
            pltpu.VMEM((features, rank), sketch_seeds.dtype),
            pltpu.VMEM((kv_heads + 2, 2, groups, tokens, HEAD), bf16),
            pltpu.VMEM((kv_heads, shards, 2, tokens, HEAD), bf16),
            pltpu.VMEM((2 * shards, chunks, groups, tokens, CHUNK), f32),
            pltpu.VMEM((2 * shards, chunks, groups, tokens, CHUNK), f32),
            pltpu.VMEM((2, groups, tokens, HEAD), f32),
            pltpu.VMEM((2, groups, tokens, HEAD), f32),
            pltpu.VMEM((2, groups, tokens, rank), f32),
            pltpu.VMEM((groups, tokens, HEAD + rank), f32),
            pltpu.VMEM((groups, tokens, HEAD), f32),
            pltpu.VMEM((tokens, rank), f32),
            pltpu.VMEM((peers, tokens // peers, rank), f32),
            pltpu.VMEM((shards, tokens, rank), bf16),
            pltpu.VMEM((kv_heads, shards, own_rows, width), f32),
            pltpu.VMEM((kv_heads, shards, own_rows, width), bf16),
            pltpu.VMEM((kv_heads, shards, own_rows, width), bf16),
            pltpu.VMEM((kv_heads, shards - 1, own_rows, width), bf16),
            dma((kv_heads, shards)), dma((kv_heads, shards)),
            dma((2,)), dma((2,)),
            dma((peers,)), dma((peers,)),
            dma((shards, 2)), dma((shards,)),
            dma((shards, peers)), dma((shards, peers)),
            dma((kv_heads, shards)), dma((kv_heads, shards)),
            dma((kv_heads,)), dma((kv_heads,)),
            dma((2 + 2 * kv_heads * (1 + groups),)),
        ],
        compiler_params=pltpu.CompilerParams(
            collective_id=0, has_side_effects=True, vmem_limit_bytes=54 * 2**20
        ),
    )(queries, key_states, value_states, out_grad, layer_inputs, sketch_seeds)
    return pl.pallas_call(
        unpack_kernel,
        out_shape=(
            jax.ShapeDtypeStruct((own_rows, query_width), f32),
            jax.ShapeDtypeStruct((own_rows, kv_width), f32),
            jax.ShapeDtypeStruct((own_rows, kv_width), f32),
        ),
        in_specs=[pl.BlockSpec(memory_space=pltpu.VMEM)],
        out_specs=(pl.BlockSpec(memory_space=pltpu.VMEM),) * 3,
    )(packed)


def per_device(queries, key_states, value_states, out_grad, layer_inputs, sketch_seeds):
    tokens, query_width = queries.shape
    kv_width = key_states.shape[1]
    kv_heads = kv_width // HEAD
    shards = lax.axis_size("seq")
    length = tokens * shards
    reach_full = WINDOW // tokens
    reach = min(reach_full, shards - 1)
    rank = sketch_seeds.shape[1]
    subs = lax.axis_size("sub")
    peers = lax.axis_size("head") * subs
    groups = query_width // kv_width
    if shards == 4 and kv_heads == 4 and reach < reach_full and tokens == 2 * CHUNK:
        return balanced(queries, key_states, value_states, out_grad, layer_inputs, sketch_seeds)
    folds = 0
    features = layer_inputs.shape[0]
    slots = (reach + 1) * (tokens // CHUNK)
    own_rows = rank // shards
    width = (query_width + 2 * kv_width) // kv_heads
    f32, bf16, dma = jnp.float32, jnp.bfloat16, pltpu.SemaphoreType.DMA
    return pl.pallas_call(
        functools.partial(
            attention_kernel, shards, reach_full, reach, folds, subs, peers,
            (2.0 * D * length) ** (-0.5),
        ),
        out_shape=(
            jax.ShapeDtypeStruct((own_rows, query_width), f32),
            jax.ShapeDtypeStruct((own_rows, kv_width), f32),
            jax.ShapeDtypeStruct((own_rows, kv_width), f32),
        ),
        in_specs=[pl.BlockSpec(memory_space=pltpu.HBM)] * 6,
        out_specs=(pl.BlockSpec(memory_space=pltpu.VMEM),) * 3,
        scratch_shapes=[
            pltpu.VMEM((tokens, query_width), bf16),
            pltpu.VMEM((tokens, query_width), bf16),
            pltpu.VMEM((features, tokens), bf16),
            pltpu.VMEM((features, rank), sketch_seeds.dtype),
            pltpu.VMEM((max(folds, 1), max(folds, 1), 2, tokens, groups * HEAD), bf16),
            pltpu.VMEM((2 * groups, tokens, HEAD), bf16),
            pltpu.VMEM((kv_heads, shards, 2, tokens, HEAD), bf16),
            pltpu.VMEM((slots, tokens, CHUNK), f32),
            pltpu.VMEM((slots, tokens, CHUNK), f32),
            pltpu.VMEM((tokens, HEAD), f32),
            pltpu.VMEM((tokens, HEAD), f32),
            pltpu.VMEM((tokens, rank), f32),
            pltpu.VMEM((tokens, HEAD + rank), f32),
            pltpu.VMEM((tokens, HEAD), f32),
            pltpu.VMEM((tokens, rank), f32),
            pltpu.VMEM((peers, tokens // peers, rank), f32),
            pltpu.VMEM((shards, tokens, rank), bf16),
            pltpu.VMEM((kv_heads, shards, own_rows, width), f32),
            pltpu.VMEM((kv_heads, shards, own_rows, width), bf16),
            pltpu.VMEM((kv_heads, shards, own_rows, width), bf16),
            dma((kv_heads, shards)), dma((kv_heads, shards)),
            dma((peers,)), dma((peers,)),
            dma((shards,)), dma((shards,)),
            dma((shards, peers)), dma((shards, peers)),
            dma((kv_heads, shards)), dma((kv_heads, shards)),
            dma((max(folds, 1), max(folds, 1))), dma((max(folds, 1), max(folds, 1))),
            dma((4 + 2 * kv_heads,)),
        ],
        compiler_params=pltpu.CompilerParams(
            collective_id=0, has_side_effects=True, vmem_limit_bytes=62 * 2**20
        ),
    )(queries, key_states, value_states, out_grad, layer_inputs, sketch_seeds)


def solution(mesh):
    placed = (
        P(("group", "seq"), ("head", "sub")),
        P(("group", "seq"), ("head", "sub")),
        P(("group", "seq"), ("head", "sub")),
        P(("group", "seq"), ("head", "sub")),
        P(("head", "sub"), ("group", "seq")),
        P(("head", "sub"), None),
    )
    return jax.shard_map(
        per_device,
        mesh=mesh,
        in_specs=placed,
        out_specs=(
            P(("group", "seq"), ("head", "sub")),
            P(("group", "seq"), ("head", "sub")),
            P(("group", "seq"), ("head", "sub")),
        ),
        check_vma=False,
    )
```

```python
import functools
import math

import jax
import jax.numpy as jnp
from jax import lax
from jax.experimental import pallas as pl
from jax.experimental.pallas import tpu as pltpu
from jax.sharding import PartitionSpec as P

D = 4608
HEAD = 128
WINDOW = 2048
CAP = 50.0
QUERY_SCALE = 144.0 ** (-0.5)
CHUNK = 256
MESH = pl.DeviceIdType.MESH


def mm(left, right, dims):
    return lax.dot_general(left, right, (dims, ((), ())), preferred_element_type=jnp.float32)


def attention_kernel(
    shards, reach_full, reach, folds, subs, peers, mix_scale,
    q_hbm, k_hbm, v_hbm, g_hbm, x_hbm, seed_hbm, oq_ref, ok_ref, ov_ref,
    q_ref, g_ref, x_ref, seed_ref, qg, q_t, kv, pg_s, w_s, z_s, dn_s, pm_s, acc_s, db_s,
    part, part_in, mixed_s, sketch, stage, stage_in,
    send_sem, recv_sem, part_send, part_recv, hop_send, hop_recv, share_send, share_recv,
    row_send, row_recv, qg_send, qg_recv, load_sem,
):
    tokens = q_ref.shape[0]
    query_width = q_ref.shape[1]
    kv_width = k_hbm.shape[1]
    kv_heads = kv_width // HEAD
    groups = query_width // kv_width
    chunks = tokens // CHUNK
    share = tokens // peers
    me = lax.axis_index("seq")
    peer = lax.axis_index("head") * subs + lax.axis_index("sub")
    blocks = jnp.minimum(me, reach)

    def last(h):
        return shards - 1 - jnp.maximum(h - (kv_heads - 1 - folds), 0)


    def cols(head):
        return pl.ds(pl.multiple_of(head * HEAD, HEAD), HEAD)

    def peer_at(offset):
        other = lax.rem(peer + offset, peers)
        return other, {"head": lax.div(other, subs), "sub": lax.rem(other, subs)}

    def seq_at(offset):
        other = lax.rem(me + offset, shards)
        return other, {"seq": other}

    def remote(src, dst, send, recv, device):
        return pltpu.make_async_remote_copy(
            src_ref=src, dst_ref=dst, send_sem=send, recv_sem=recv,
            device_id=device, device_id_type=MESH,
        )

    def loop(low, high, fn):
        def step(i, carry):
            fn(i)
            return carry

        lax.fori_loop(low, high, step, 0)

    def hop(h, b, way=1):
        return remote(
            kv.at[h, b], kv.at[h, b], send_sem.at[h, b], recv_sem.at[h, b], {"seq": me + way}
        )

    def row_hop(h, row):
        at = (h - (kv_heads - folds), row - (shards - folds))
        return remote(
            qg.at[at], qg.at[at], qg_send.at[at], qg_recv.at[at], {"seq": me - 1}
        )

    def part_copy(offset):
        other, device = peer_at(offset)
        rows = pl.ds(pl.multiple_of(other * share, share), share)
        return remote(
            part.at[rows], part_in.at[offset], part_send.at[offset], part_recv.at[offset], device
        )

    mine = pl.ds(pl.multiple_of(peer * share, share), share)

    def mixed_along(offset):
        _, device = seq_at(offset)
        return remote(
            mixed_s.at[me, mine], mixed_s.at[me, mine], hop_send.at[offset], hop_recv.at[offset],
            device,
        )

    def mixed_share(b, offset):
        _, device = peer_at(offset)
        return remote(
            mixed_s.at[b, mine], mixed_s.at[b, mine], share_send.at[b, offset],
            share_recv.at[b, offset], device,
        )

    def row_copy(h, offset):
        other, device = seq_at(offset)
        return remote(
            stage.at[h, other], stage_in.at[h, offset], row_send.at[h, offset],
            row_recv.at[h, offset], device,
        )

    barrier = pltpu.get_barrier_semaphore()

    def greet_peer(offset):
        pl.semaphore_signal(barrier, inc=1, device_id=peer_at(offset)[1], device_id_type=MESH)

    def greet_seq(offset):
        pl.semaphore_signal(barrier, inc=1, device_id=seq_at(offset)[1], device_id_type=MESH)

    loop(1, peers, greet_peer)
    loop(1, shards, greet_seq)
    def load_kv(h, which):
        source = (k_hbm, v_hbm)[which]
        return pltpu.make_async_copy(
            source.at[:, cols(h)], kv.at[h, me, which], load_sem.at[4 + which * kv_heads + h]
        )

    loads = [
        pltpu.make_async_copy(source, target, load_sem.at[i])
        for i, (source, target) in enumerate(
            ((seed_hbm, seed_ref), (x_hbm, x_ref), (q_hbm, q_ref), (g_hbm, g_ref))
        )
    ]
    for h in range(kv_heads):
        load_kv(h, 0).start()
        load_kv(h, 1).start()
    for load in loads:
        load.start()
    for h in range(kv_heads):
        load_kv(h, 0).wait()
        load_kv(h, 1).wait()
    pl.semaphore_wait(barrier, peers + shards - 2)

    early = 1

    def send_own(low, high):
        def one(h):
            @pl.when(me < last(h))
            def _():
                hop(h, me).start()

        if reach > 0:
            loop(low, high, one)

    def send_folded(h):
        @pl.when(me > last(h))
        def _():
            at = (h - (kv_heads - folds), me - (shards - folds))
            width = groups * HEAD
            qg[at + (0,)] = q_ref[:, h * width : (h + 1) * width]
            qg[at + (1,)] = g_ref[:, h * width : (h + 1) * width]
            if h < kv_heads - 1:
                hop(h, me, -1).start()
            row_hop(h, me).start()

    send_own(0, early)
    if folds > 0:
        @pl.when(me > last(kv_heads - 1))
        def _():
            hop(kv_heads - 1, me, -1).start()

    loads[0].wait()
    loads[1].wait()
    seeds = seed_ref[...].astype(jnp.float32).astype(jnp.bfloat16)
    part[...] = mm(seeds, x_ref[...], ((0,), (0,))).T
    loop(1, peers, lambda offset: part_copy(offset).start())
    part_in[0] = part[mine, :]
    loop(1, peers, lambda offset: part_copy(offset).wait_recv())
    total = part_in[0]
    for offset in range(1, peers):
        total = total + part_in[offset]
    mixed_s[me, mine, :] = (total * mix_scale).astype(jnp.bfloat16)

    def spread(b):
        loop(1, peers, lambda offset: mixed_share(b, offset).start())

    def spread_from(offset):
        mixed_along(offset).wait_recv()
        spread(seq_at(shards - offset)[0])

    def gathered(b):
        loop(1, peers, lambda offset: mixed_share(b, offset).wait_recv())

    loop(1, shards, lambda offset: mixed_along(offset).start())
    spread(me)
    send_own(early, kv_heads)
    loads[2].wait()
    loads[3].wait()
    for h in reversed(range(kv_heads - folds, kv_heads)):
        send_folded(h)
    loop(1, shards, spread_from)

    def first_pass(h, row, qh, gh, d, c, row0, kind):
        rows = tokens - row0
        kk = kv[h, row - d, 0, pl.ds(c * CHUNK, CHUNK), :]
        vv = kv[h, row - d, 1, pl.ds(c * CHUNK, CHUNK), :]
        mixed = mixed_s[row - d, pl.ds(c * CHUNK, CHUNK), :]
        scores = mm(qh[row0:], kk, ((1,), (1,)))
        weight = mm(gh[row0:], vv, ((1,), (1,)))
        bounded = jnp.tanh(scores * (QUERY_SCALE / CAP))
        power = jnp.exp2(bounded * (CAP / math.log(2.0)))
        if kind is not None:
            qi = row0 + lax.broadcasted_iota(jnp.int32, (rows, CHUNK), 0)
            kj = c * CHUNK + lax.broadcasted_iota(jnp.int32, (rows, CHUNK), 1)
            keep = qi >= kj if kind == "causal" else qi < kj
            power = jnp.where(keep, power, 0.0)
        slot = d * chunks + c
        pg_s[slot, pl.ds(row0, rows), :] = power - power * (bounded * bounded)
        w_s[slot, pl.ds(row0, rows), :] = weight
        pw = power * weight
        at = pl.ds(row0, rows)
        z_s[at, :] += power[:, :HEAD] + power[:, HEAD:]
        dn_s[at, :] += pw[:, :HEAD] + pw[:, HEAD:]
        pm_s[at, :] += mm(power.astype(jnp.bfloat16), mixed, ((1,), (0,)))

    def second_pass(h, row, d, c, row0):
        rows = tokens - row0
        at = pl.ds(row0, rows)
        slot = d * chunks + c
        kk = kv[h, row - d, 0, pl.ds(c * CHUNK, CHUNK), :]
        mixed = mixed_s[row - d, pl.ds(c * CHUNK, CHUNK), :]
        dot = db_s[at, :]
        grad = pg_s[slot, at, :] * (w_s[slot, at, :] - jnp.concatenate([dot, dot], 1))
        acc_s[at, :] += mm(
            grad.astype(jnp.bfloat16), jnp.concatenate([kk, mixed], 1), ((1,), (0,))
        )

    full = reach if reach < reach_full else reach_full - 1

    def each_block(row, fn):
        for c in range(chunks):
            fn(0, c, c * CHUNK, "causal")

        def step(d, carry):
            for c in range(chunks):
                fn(d, c, 0, None)
            return carry

        lax.fori_loop(1, jnp.minimum(row, full) + 1, step, 0)
        if full < reach:
            @pl.when(row >= reach)
            def _():
                for c in range(chunks):
                    fn(reach, c, 0, "window")

    def arrivals(h):
        def arrive(d):
            hop(h, me - d).wait_recv()

            @pl.when((me < last(h)) & (d < reach))
            def _():
                hop(h, me - d).start()

        @pl.when(me <= last(h))
        def _():
            loop(1, blocks + 1, arrive)

    def pass_folded():
        for folded in reversed(range(kv_heads - folds, kv_heads)):
            for row in range(shards - folds + 1, shards):
                @pl.when((me > last(folded)) & (me < row))
                def _():
                    hop(folded, row, -1).wait_recv()
                    hop(folded, row, -1).start()
                    row_hop(folded, row).wait_recv()
                    row_hop(folded, row).start()

    def kv_head(h, carry):
        @pl.when((h > 1) | ((h == 1) & (me != 1)))
        def _():
            arrivals(h)

        count = jnp.where(me < last(h), 1, jnp.where(me == last(h), shards - last(h), 0))
        loop(0, count, lambda extra: row_task(h, me + extra, extra))

        @pl.when(me <= last(h))
        def _():
            stage[h] = sketch[h].astype(stage.dtype)
            loop(1, shards, lambda offset: row_copy(h, offset).start())

        return carry

    def row_task(h, row, extra):
        if folds > 0:
            @pl.when(extra > 0)
            def _():
                hop(h, row, -1).wait_recv()
                row_hop(h, row).wait_recv()
                at = (h - (kv_heads - folds), row - (shards - folds))
                for member in range(groups):
                    q_t[member] = qg[at + (0, slice(None), pl.ds(member * HEAD, HEAD))]
                    q_t[groups + member] = qg[at + (1, slice(None), pl.ds(member * HEAD, HEAD))]

        @pl.when(extra == 0)
        def _():
            for member in range(groups):
                q_t[member] = q_ref[:, cols(h * groups + member)]
                q_t[groups + member] = g_ref[:, cols(h * groups + member)]

        own_mixed = mixed_s[row]

        def member_step(member, inner):
            qh = q_t[member]
            gh = q_t[groups + member]
            z_s[...] = jnp.zeros_like(z_s)
            dn_s[...] = jnp.zeros_like(dn_s)
            pm_s[...] = jnp.zeros_like(pm_s)
            acc_s[...] = jnp.zeros_like(acc_s)
            each_block(row, lambda d, c, row0, kind: first_pass(h, row, qh, gh, d, c, row0, kind))
            inverse = 1.0 / jnp.sum(z_s[...], axis=1, keepdims=True)
            dot = jnp.sum(dn_s[...], axis=1, keepdims=True) * inverse
            db_s[...] = jnp.broadcast_to(dot, db_s.shape)
            each_block(row, lambda d, c, row0, kind: second_pass(h, row, d, c, row0))
            scale = inverse * QUERY_SCALE
            dq = (acc_s[:, :HEAD] * scale).astype(jnp.bfloat16)
            dm = (acc_s[:, HEAD:] * scale).astype(jnp.bfloat16)
            pm = (pm_s[...] * inverse).astype(jnp.bfloat16)
            q_part = mm(own_mixed, dq, ((0,), (0,)))
            k_part = mm(dm, qh, ((0,), (0,)))
            v_part = mm(pm, gh, ((0,), (0,)))
            blocked = (shards, own_rows, HEAD)
            sketch[h, :, :, cols(2 + member)] += q_part.reshape(blocked)
            sketch[h, :, :, :HEAD] += k_part.reshape(blocked)
            sketch[h, :, :, HEAD : 2 * HEAD] += v_part.reshape(blocked)
            return inner

        lax.fori_loop(0, groups, member_step, 0)

    sketch[...] = jnp.zeros_like(sketch)
    own_rows = sketch.shape[2]
    arrivals(0)
    pass_folded()
    if kv_heads > 1:
        @pl.when(me == 1)
        def _():
            arrivals(1)

    loop(0, shards, gathered)
    lax.fori_loop(0, kv_heads, kv_head, 0)

    def collect(h):
        def add(offset):
            @pl.when(seq_at(shards - offset)[0] <= last(h))
            def _():
                row_copy(h, offset).wait_recv()
                sketch[h, me] += stage_in[h, offset].astype(jnp.float32)

        loop(1, shards, add)
        rows = sketch[h, me]
        ok_ref[:, cols(h)] = rows[:, :HEAD]
        ov_ref[:, cols(h)] = rows[:, HEAD : 2 * HEAD]
        for member in range(groups):
            oq_ref[:, cols(h * groups + member)] = rows[:, (2 + member) * HEAD : (3 + member) * HEAD]

    loop(0, kv_heads, collect)

    loop(1, peers, lambda offset: part_copy(offset).wait_send())
    loop(1, shards, lambda offset: mixed_along(offset).wait_send())
    loop(0, shards, lambda b: loop(1, peers, lambda offset: mixed_share(b, offset).wait_send()))

    def drain_rows(h):
        @pl.when(me <= last(h))
        def _():
            loop(1, shards, lambda offset: row_copy(h, offset).wait_send())

    loop(0, kv_heads, drain_rows)

    def drain(h):
        @pl.when(me < last(h))
        def _():
            loop(0, jnp.minimum(me, reach - 1) + 1, lambda d: hop(h, me - d).wait_send())

    if reach > 0:
        loop(0, kv_heads, drain)
    for h in range(kv_heads - folds, kv_heads):
        for row in range(shards - folds, shards):
            @pl.when((me > last(h)) & (me <= row))
            def _():
                hop(h, row, -1).wait_send()
                row_hop(h, row).wait_send()


STEP_H, STEP_B, STEP_ROW, STEP_SLOT, STEP_HALF = 1, 4, 16, 64, 512
INIT, FINAL, SEND, WAIT_KV, PASS_KV, WAIT_Q, RELAY = (1024 << i for i in range(7))
HOP, GATHER = 1 << 19, 1 << 22
FOREIGN = 4


def step_of(h, b, row, slot, half, *flags):
    return h * STEP_H + b * STEP_B + row * STEP_ROW + slot * STEP_SLOT + half * STEP_HALF + sum(flags)


STEPS = (
    [step_of(h, 0, 0, h, 0, INIT, FINAL, SEND) for h in range(4)],
    [
        step_of(0, 1, 1, 0, 0, INIT),
        step_of(1, 1, 1, 1, 1, INIT, HOP),
        step_of(0, 0, 1, 0, 0, WAIT_KV, PASS_KV, GATHER, FINAL),
        step_of(1, 0, 1, 1, 1, WAIT_KV, PASS_KV, FINAL),
        step_of(2, 1, 1, 2, 0, INIT, 3 * HOP),
        step_of(2, 0, 1, 2, 0, WAIT_KV, PASS_KV, FINAL),
        step_of(3, 1, 1, 3, 0, INIT, 4 * HOP),
        step_of(3, 0, 1, 3, 0, WAIT_KV, FINAL),
        step_of(3, 1, 2, 4, 0, INIT, WAIT_Q, 3 * GATHER),
        step_of(3, 0, 2, 4, 0),
        step_of(3, 2, 2, 4, 0, WAIT_KV, FINAL, SEND),
        step_of(3, 1, 3, 5, 0, INIT, WAIT_Q, 4 * GATHER),
        step_of(3, 0, 3, 5, 0),
        step_of(3, 2, 3, 5, 0),
        step_of(3, 3, 3, 5, 0, WAIT_KV, FINAL, SEND),
    ],
    [
        step_of(0, 2, 2, 0, 0, INIT),
        step_of(1, 2, 2, 1, 1, INIT, 2 * HOP),
        step_of(0, 1, 2, 0, 0, WAIT_KV, PASS_KV, 4 * HOP, 2 * GATHER),
        step_of(1, 1, 2, 1, 1, WAIT_KV, PASS_KV, HOP),
        step_of(0, 0, 2, 0, 0, WAIT_KV, PASS_KV, RELAY, GATHER, FINAL, SEND),
        step_of(1, 0, 2, 1, 1, WAIT_KV, PASS_KV, FINAL, SEND),
        step_of(2, 2, 2, 2, 0, INIT),
        step_of(2, 2, 3, 4, 1, INIT, WAIT_Q, 4 * GATHER),
        step_of(2, 1, 2, 2, 0, WAIT_KV),
        step_of(2, 1, 3, 4, 1),
        step_of(2, 3, 3, 4, 1, WAIT_KV),
        step_of(2, 0, 2, 2, 0, WAIT_KV, FINAL),
        step_of(2, 0, 3, 4, 1, FINAL, SEND),
    ],
    [
        step_of(0, 3, 3, 0, 0, INIT),
        step_of(1, 3, 3, 1, 1, INIT, 3 * HOP),
        step_of(0, 2, 3, 0, 0, WAIT_KV, 3 * GATHER),
        step_of(1, 2, 3, 1, 1, WAIT_KV, 2 * HOP),
        step_of(0, 1, 3, 0, 0, WAIT_KV, 2 * GATHER),
        step_of(1, 1, 3, 1, 1, WAIT_KV, HOP),
        step_of(0, 0, 3, 0, 0, WAIT_KV, GATHER, FINAL, SEND),
        step_of(1, 0, 3, 1, 1, WAIT_KV, FINAL, SEND),
    ],
)


def balanced_kernel(
    subs, peers, mix_scale,
    q_hbm, k_hbm, v_hbm, g_hbm, x_hbm, seed_hbm, out_ref,
    x_ref, seed_ref, qg, kv, pg_s, w_s, z_s, dn_s, pm_s, acc_s, db_s,
    part, part_in, mixed_s, sketch, stage, stage_in, fold_in,
    kv_send, kv_recv, q_send, q_recv, part_send, part_recv, hop_send, hop_recv,
    share_send, share_recv, row_send, row_recv, fold_send, fold_recv, load_sem,
):
    shards, kv_heads = 4, 4
    tokens = qg.shape[3]
    groups = qg.shape[2]
    chunks = tokens // CHUNK
    share = tokens // peers
    own_rows = sketch.shape[2]
    me = lax.axis_index("seq")
    peer = lax.axis_index("head") * subs + lax.axis_index("sub")

    def cols(head):
        return pl.ds(pl.multiple_of(head * HEAD, HEAD), HEAD)

    def peer_at(offset):
        other = lax.rem(peer + offset, peers)
        return other, {"head": lax.div(other, subs), "sub": lax.rem(other, subs)}

    def seq_at(offset):
        other = lax.rem(me + offset, shards)
        return other, {"seq": other}

    def remote(src, dst, send, recv, device):
        return pltpu.make_async_remote_copy(
            src_ref=src, dst_ref=dst, send_sem=send, recv_sem=recv,
            device_id=device, device_id_type=MESH,
        )

    def loop(low, high, fn):
        def step(i, carry):
            fn(i)
            return carry

        lax.fori_loop(low, high, step, 0)

    def kv_hop(h, b, way=1):
        return remote(
            kv.at[h, b], kv.at[h, b], kv_send.at[h, b], kv_recv.at[h, b], {"seq": me + way}
        )

    def q_hop(source, target):
        at = target - FOREIGN
        return remote(
            qg.at[source], qg.at[target], q_send.at[at], q_recv.at[at], {"seq": me - 1}
        )

    def part_copy(offset):
        other, device = peer_at(offset)
        rows = pl.ds(pl.multiple_of(other * share, share), share)
        return remote(
            part.at[rows], part_in.at[offset], part_send.at[offset], part_recv.at[offset], device
        )

    mine = pl.ds(pl.multiple_of(peer * share, share), share)

    def mixed_hop(b, way):
        return remote(
            mixed_s.at[b, mine], mixed_s.at[b, mine], hop_send.at[b, (way + 1) // 2],
            hop_recv.at[b], {"seq": me + way},
        )

    def mixed_share(b, offset):
        _, device = peer_at(offset)
        return remote(
            mixed_s.at[b, mine], mixed_s.at[b, mine], share_send.at[b, offset],
            share_recv.at[b, offset], device,
        )

    def row_copy(h, target, sender):
        return remote(
            stage.at[h, target], stage_in.at[h, sender], row_send.at[h, target],
            row_recv.at[h, sender], {"seq": target},
        )

    def fold_copy(h):
        return remote(
            stage.at[h, pl.ds(1, shards - 1)], fold_in.at[h], fold_send.at[h], fold_recv.at[h],
            {"seq": 1},
        )

    barrier = pltpu.get_barrier_semaphore()

    def greet_peer(offset):
        pl.semaphore_signal(barrier, inc=1, device_id=peer_at(offset)[1], device_id_type=MESH)

    def greet_seq(offset):
        pl.semaphore_signal(barrier, inc=1, device_id=seq_at(offset)[1], device_id_type=MESH)

    loop(1, peers, greet_peer)
    loop(1, shards, greet_seq)

    def load_kv(h, which):
        source = (k_hbm, v_hbm)[which]
        return pltpu.make_async_copy(
            source.at[:, cols(h)], kv.at[h, me, which], load_sem.at[2 + which * kv_heads + h]
        )

    def load_qg(h, which, member):
        source = (q_hbm, g_hbm)[which]
        at = 2 + 2 * kv_heads + (h * 2 + which) * groups + member
        return pltpu.make_async_copy(
            source.at[:, cols(h * groups + member)], qg.at[h, which, member], load_sem.at[at]
        )

    load_seed = pltpu.make_async_copy(seed_hbm, seed_ref, load_sem.at[0])
    load_x = pltpu.make_async_copy(x_hbm, x_ref, load_sem.at[1])

    def each_kv(fn):
        for which in range(2):
            loop(0, kv_heads, lambda h: fn(load_kv(h, which)))

    def each_qg(fn):
        for which in range(2):
            for member in range(groups):
                loop(0, kv_heads, lambda h: fn(load_qg(h, which, member)))

    each_kv(lambda copy: copy.start())
    load_seed.start()
    load_x.start()
    each_qg(lambda copy: copy.start())
    each_kv(lambda copy: copy.wait())
    pl.semaphore_wait(barrier, peers + shards - 2)

    @pl.when(me < 3)
    def _():
        kv_hop(0, me).start()

    @pl.when(me > 1)
    def _():
        kv_hop(3, me, -1).start()

    load_seed.wait()
    load_x.wait()
    seeds = seed_ref[...].astype(jnp.float32).astype(jnp.bfloat16)
    part[...] = mm(seeds, x_ref[...], ((0,), (0,))).T
    loop(1, peers, lambda offset: part_copy(offset).start())
    part_in[0] = part[mine, :]
    loop(1, peers, lambda offset: part_copy(offset).wait_recv())
    total = part_in[0]
    for offset in range(1, peers):
        total = total + part_in[offset]
    mixed_s[me, mine, :] = (total * mix_scale).astype(jnp.bfloat16)

    def spread(b):
        loop(1, peers, lambda offset: mixed_share(b, offset).start())

    def pass_mixed(b):
        mixed_hop(b, 1).wait_recv()

        @pl.when((b < me) & (me < shards - 1))
        def _():
            mixed_hop(b, 1).start()

        @pl.when((b > me) & (me > 1))
        def _():
            mixed_hop(b, -1).start()

        spread(b)

    def gathered(b):
        loop(1, peers, lambda offset: mixed_share(b, offset).wait_recv())

    @pl.when(me < shards - 1)
    def _():
        mixed_hop(me, 1).start()

    @pl.when(me > 1)
    def _():
        mixed_hop(me, -1).start()

    spread(me)
    each_qg(lambda copy: copy.wait())

    @pl.when(me == 0)
    def _():
        loop(1, kv_heads, lambda h: kv_hop(h, 0).start())

    @pl.when(me == 1)
    def _():
        kv_hop(1, 1).start()

    @pl.when(me == 2)
    def _():
        kv_hop(1, 2).start()
        q_hop(3, 4).start()

    @pl.when(me == 3)
    def _():
        q_hop(3, 5).start()
        q_hop(2, 4).start()
        kv_hop(2, 3, -1).start()

    sketch[...] = jnp.zeros_like(sketch)

    def first_pass(h, b, slot, half, d, c, row0, causal):
        rows = tokens - row0
        at = pl.ds(row0, rows)
        keys = pl.ds(c * CHUNK, CHUNK)
        qh = qg[slot, 0, :, at, :].reshape(groups * rows, HEAD)
        gh = qg[slot, 1, :, at, :].reshape(groups * rows, HEAD)
        scores = mm(qh, kv[h, b, 0, keys, :], ((1,), (1,)))
        weight = mm(gh, kv[h, b, 1, keys, :], ((1,), (1,)))
        bounded = jnp.tanh(scores * (QUERY_SCALE / CAP))
        power = jnp.exp2(bounded * (CAP / math.log(2.0)))
        if causal:
            qi = lax.broadcasted_iota(jnp.int32, (groups, rows, CHUNK), 1)
            kj = lax.broadcasted_iota(jnp.int32, (groups, rows, CHUNK), 2)
            keep = (row0 + qi >= c * CHUNK + kj).reshape(groups * rows, CHUNK)
            power = jnp.where(keep, power, 0.0)
        whole = (groups, rows, CHUNK)
        folded = (groups, rows, HEAD)
        put = half * shards + d
        pg_s[put, c, :, at, :] = (power - power * (bounded * bounded)).reshape(whole)
        w_s[put, c, :, at, :] = weight.reshape(whole)
        pw = power * weight
        z_s[half, :, at, :] += (power[:, :HEAD] + power[:, HEAD:]).reshape(folded)
        dn_s[half, :, at, :] += (pw[:, :HEAD] + pw[:, HEAD:]).reshape(folded)
        pm = mm(power.astype(jnp.bfloat16), mixed_s[b, keys, :], ((1,), (0,)))
        pm_s[half, :, at, :] += pm.reshape(folded)

    def second_pass(h, b, half, d, c, row0):
        rows = tokens - row0
        at = pl.ds(row0, rows)
        keys = pl.ds(c * CHUNK, CHUNK)
        put = half * shards + d
        dot = db_s[:, at, :]
        grad = pg_s[put, c, :, at, :] * (w_s[put, c, :, at, :] - jnp.concatenate([dot, dot], 2))
        sides = jnp.concatenate([kv[h, b, 0, keys, :], mixed_s[b, keys, :]], 1)
        term = mm(grad.astype(jnp.bfloat16).reshape(groups * rows, CHUNK), sides, ((1,), (0,)))
        acc_s[:, at, :] += term.reshape(groups, rows, 2 * HEAD)

    def finish_row(h, row, slot, half):
        inverse = 1.0 / jnp.sum(z_s[half], axis=2, keepdims=True)
        dot = jnp.sum(dn_s[half], axis=2, keepdims=True) * inverse
        db_s[...] = jnp.broadcast_to(dot, db_s.shape)
        acc_s[...] = jnp.zeros_like(acc_s)
        for c in range(chunks):
            second_pass(h, row, half, 0, c, c * CHUNK)

        def rest(d):
            for c in range(chunks):
                second_pass(h, row - d, half, d, c, 0)

        loop(1, row + 1, rest)
        scale = inverse * QUERY_SCALE
        dq = (acc_s[:, :, :HEAD] * scale).astype(jnp.bfloat16)
        dm = (acc_s[:, :, HEAD:] * scale).astype(jnp.bfloat16)
        pm = (pm_s[half] * inverse).astype(jnp.bfloat16)
        stacked = (groups * tokens, HEAD)
        blocked = (shards, own_rows, HEAD)
        k_part = mm(dm.reshape(stacked), qg[slot, 0].reshape(stacked), ((0,), (0,)))
        v_part = mm(pm.reshape(stacked), qg[slot, 1].reshape(stacked), ((0,), (0,)))
        sketch[h, :, :, :HEAD] += k_part.reshape(blocked)
        sketch[h, :, :, HEAD : 2 * HEAD] += v_part.reshape(blocked)
        q_part = mm(mixed_s[row], jnp.concatenate([dq[m] for m in range(groups)], 1), ((0,), (0,)))
        sketch[h, :, :, 2 * HEAD :] += q_part.reshape(shards, own_rows, groups * HEAD)

    def send_head(h):
        @pl.when(me == 1)
        def _():
            fold_copy(h).wait_recv()
            sketch[h, pl.ds(1, shards - 1)] += fold_in[h].astype(jnp.float32)

        stage[h] = sketch[h].astype(stage.dtype)

        @pl.when(me == 0)
        def _():
            fold_copy(h).start()

        @pl.when(me > 0)
        def _():
            loop(1, shards, lambda offset: row_copy(h, seq_at(offset)[0], me).start())

    def one_step(index):
        code = jnp.int32(0)
        for shard, codes in enumerate(STEPS):
            for i, value in enumerate(codes):
                code = jnp.where((me == shard) & (index == i), value, code)

        def field(unit, size):
            return lax.rem(lax.div(code, unit), size)

        def flag(unit):
            return field(unit, 2) == 1

        h, b, row = field(STEP_H, 4), field(STEP_B, 4), field(STEP_ROW, 4)
        slot, half = field(STEP_SLOT, 8), field(STEP_HALF, 2)

        @pl.when(flag(WAIT_Q))
        def _():
            q_hop(slot, slot).wait_recv()

        @pl.when(flag(WAIT_KV))
        def _():
            kv_hop(h, b).wait_recv()

        @pl.when(flag(PASS_KV))
        def _():
            kv_hop(h, b).start()

            @pl.when((me == 1) & (h == 1))
            def _():
                kv_hop(2, 1).start()

        @pl.when(flag(RELAY))
        def _():
            q_hop(5, 5).wait_recv()
            q_hop(5, 5).start()
            kv_hop(3, 3, -1).wait_recv()
            kv_hop(3, 3, -1).start()

        hopped, wanted = field(HOP, 8), field(GATHER, 8)

        @pl.when(hopped > 0)
        def _():
            pass_mixed(hopped - 1)

        @pl.when(wanted > 0)
        def _():
            gathered(wanted - 1)

        @pl.when(flag(INIT))
        def _():
            z_s[half] = jnp.zeros(z_s.shape[1:], z_s.dtype)
            dn_s[half] = jnp.zeros(dn_s.shape[1:], dn_s.dtype)
            pm_s[half] = jnp.zeros(pm_s.shape[1:], pm_s.dtype)

        @pl.when(b == row)
        def _():
            for c in range(chunks):
                first_pass(h, b, slot, half, 0, c, c * CHUNK, True)

        @pl.when(b != row)
        def _():
            for c in range(chunks):
                first_pass(h, b, slot, half, row - b, c, 0, False)

        @pl.when(flag(FINAL))
        def _():
            finish_row(h, row, slot, half)

        @pl.when(flag(SEND))
        def _():
            held = (me == 1) & (row == 2)
            loop(jnp.where(held, 0, h), jnp.where(held, h, h + 1), send_head)

    gathered(me)
    count = jnp.int32(0)
    for shard, codes in enumerate(STEPS):
        count = jnp.where(me == shard, len(codes), count)
    loop(0, count, one_step)

    def heads_of(sender):
        return jnp.where(sender == 2, 3, jnp.where(sender == 3, 2, jnp.where(sender == 1, 4, 0)))

    def collect(h):
        def add(sender):
            @pl.when((sender != me) & (h < heads_of(sender)))
            def _():
                row_copy(h, me, sender).wait_recv()
                sketch[h, me] += stage_in[h, sender].astype(jnp.float32)

        loop(1, shards, add)
        out_ref[h] = sketch[h, me]

    loop(0, kv_heads, collect)

    loop(1, peers, lambda offset: part_copy(offset).wait_send())

    @pl.when(me < shards - 1)
    def _():
        loop(0, me + 1, lambda b: mixed_hop(b, 1).wait_send())

    @pl.when(me > 1)
    def _():
        loop(me, shards, lambda b: mixed_hop(b, -1).wait_send())

    def drain_share(b):
        @pl.when((me > 0) | (b <= 0))
        def _():
            loop(1, peers, lambda offset: mixed_share(b, offset).wait_send())

    loop(0, shards, drain_share)
    loop(
        0, heads_of(me),
        lambda h: loop(1, shards, lambda offset: row_copy(h, seq_at(offset)[0], me).wait_send()),
    )

    @pl.when(me == 0)
    def _():
        loop(0, kv_heads, lambda h: fold_copy(h).wait_send())

    up = jnp.where(me == 0, 4, jnp.where(me == 1, 3, jnp.where(me == 2, 2, 0)))
    loop(0, up, lambda h: loop(0, me + 1, lambda b: kv_hop(h, b).wait_send()))

    @pl.when(me == 2)
    def _():
        kv_hop(3, 2, -1).wait_send()
        kv_hop(3, 3, -1).wait_send()
        q_hop(3, 4).wait_send()
        q_hop(5, 5).wait_send()

    @pl.when(me == 3)
    def _():
        kv_hop(3, 3, -1).wait_send()
        kv_hop(2, 3, -1).wait_send()
        q_hop(3, 5).wait_send()
        q_hop(2, 4).wait_send()


def unpack_kernel(packed, oq_ref, ok_ref, ov_ref):
    kv_heads = packed.shape[0]
    queries = packed.shape[2] - 2 * HEAD
    for h in range(kv_heads):
        ok_ref[:, h * HEAD : (h + 1) * HEAD] = packed[h, :, :HEAD]
        ov_ref[:, h * HEAD : (h + 1) * HEAD] = packed[h, :, HEAD : 2 * HEAD]
        oq_ref[:, h * queries : (h + 1) * queries] = packed[h, :, 2 * HEAD :]


def balanced(queries, key_states, value_states, out_grad, layer_inputs, sketch_seeds):
    tokens, query_width = queries.shape
    kv_width = key_states.shape[1]
    kv_heads = kv_width // HEAD
    groups = query_width // kv_width
    shards = lax.axis_size("seq")
    subs = lax.axis_size("sub")
    peers = lax.axis_size("head") * subs
    features = layer_inputs.shape[0]
    rank = sketch_seeds.shape[1]
    chunks = tokens // CHUNK
    own_rows = rank // shards
    width = (groups + 2) * HEAD
    f32, bf16, dma = jnp.float32, jnp.bfloat16, pltpu.SemaphoreType.DMA
    packed = pl.pallas_call(
        functools.partial(balanced_kernel, subs, peers, (2.0 * D * tokens * shards) ** (-0.5)),
        out_shape=jax.ShapeDtypeStruct((kv_heads, own_rows, width), f32),
        in_specs=[pl.BlockSpec(memory_space=pltpu.HBM)] * 6,
        out_specs=pl.BlockSpec(memory_space=pltpu.VMEM),
        scratch_shapes=[
            pltpu.VMEM((features, tokens), bf16),
            pltpu.VMEM((features, rank), sketch_seeds.dtype),
            pltpu.VMEM((kv_heads + 2, 2, groups, tokens, HEAD), bf16),
            pltpu.VMEM((kv_heads, shards, 2, tokens, HEAD), bf16),
            pltpu.VMEM((2 * shards, chunks, groups, tokens, CHUNK), f32),
            pltpu.VMEM((2 * shards, chunks, groups, tokens, CHUNK), f32),
            pltpu.VMEM((2, groups, tokens, HEAD), f32),
            pltpu.VMEM((2, groups, tokens, HEAD), f32),
            pltpu.VMEM((2, groups, tokens, rank), f32),
            pltpu.VMEM((groups, tokens, HEAD + rank), f32),
            pltpu.VMEM((groups, tokens, HEAD), f32),
            pltpu.VMEM((tokens, rank), f32),
            pltpu.VMEM((peers, tokens // peers, rank), f32),
            pltpu.VMEM((shards, tokens, rank), bf16),
            pltpu.VMEM((kv_heads, shards, own_rows, width), f32),
            pltpu.VMEM((kv_heads, shards, own_rows, width), bf16),
            pltpu.VMEM((kv_heads, shards, own_rows, width), bf16),
            pltpu.VMEM((kv_heads, shards - 1, own_rows, width), bf16),
            dma((kv_heads, shards)), dma((kv_heads, shards)),
            dma((2,)), dma((2,)),
            dma((peers,)), dma((peers,)),
            dma((shards, 2)), dma((shards,)),
            dma((shards, peers)), dma((shards, peers)),
            dma((kv_heads, shards)), dma((kv_heads, shards)),
            dma((kv_heads,)), dma((kv_heads,)),
            dma((2 + 2 * kv_heads * (1 + groups),)),
        ],
        compiler_params=pltpu.CompilerParams(
            collective_id=0, has_side_effects=True, vmem_limit_bytes=62 * 2**20
        ),
    )(queries, key_states, value_states, out_grad, layer_inputs, sketch_seeds)
    return pl.pallas_call(
        unpack_kernel,
        out_shape=(
            jax.ShapeDtypeStruct((own_rows, query_width), f32),
            jax.ShapeDtypeStruct((own_rows, kv_width), f32),
            jax.ShapeDtypeStruct((own_rows, kv_width), f32),
        ),
        in_specs=[pl.BlockSpec(memory_space=pltpu.VMEM)],
        out_specs=(pl.BlockSpec(memory_space=pltpu.VMEM),) * 3,
    )(packed)


def per_device(queries, key_states, value_states, out_grad, layer_inputs, sketch_seeds):
    tokens, query_width = queries.shape
    kv_width = key_states.shape[1]
    kv_heads = kv_width // HEAD
    shards = lax.axis_size("seq")
    length = tokens * shards
    reach_full = WINDOW // tokens
    reach = min(reach_full, shards - 1)
    rank = sketch_seeds.shape[1]
    subs = lax.axis_size("sub")
    peers = lax.axis_size("head") * subs
    groups = query_width // kv_width
    if shards == 4 and kv_heads == 4 and reach < reach_full and tokens == 2 * CHUNK:
        return balanced(queries, key_states, value_states, out_grad, layer_inputs, sketch_seeds)
    folds = 0
    features = layer_inputs.shape[0]
    slots = (reach + 1) * (tokens // CHUNK)
    own_rows = rank // shards
    width = (query_width + 2 * kv_width) // kv_heads
    f32, bf16, dma = jnp.float32, jnp.bfloat16, pltpu.SemaphoreType.DMA
    return pl.pallas_call(
        functools.partial(
            attention_kernel, shards, reach_full, reach, folds, subs, peers,
            (2.0 * D * length) ** (-0.5),
        ),
        out_shape=(
            jax.ShapeDtypeStruct((own_rows, query_width), f32),
            jax.ShapeDtypeStruct((own_rows, kv_width), f32),
            jax.ShapeDtypeStruct((own_rows, kv_width), f32),
        ),
        in_specs=[pl.BlockSpec(memory_space=pltpu.HBM)] * 6,
        out_specs=(pl.BlockSpec(memory_space=pltpu.VMEM),) * 3,
        scratch_shapes=[
            pltpu.VMEM((tokens, query_width), bf16),
            pltpu.VMEM((tokens, query_width), bf16),
            pltpu.VMEM((features, tokens), bf16),
            pltpu.VMEM((features, rank), sketch_seeds.dtype),
            pltpu.VMEM((max(folds, 1), max(folds, 1), 2, tokens, groups * HEAD), bf16),
            pltpu.VMEM((2 * groups, tokens, HEAD), bf16),
            pltpu.VMEM((kv_heads, shards, 2, tokens, HEAD), bf16),
            pltpu.VMEM((slots, tokens, CHUNK), f32),
            pltpu.VMEM((slots, tokens, CHUNK), f32),
            pltpu.VMEM((tokens, HEAD), f32),
            pltpu.VMEM((tokens, HEAD), f32),
            pltpu.VMEM((tokens, rank), f32),
            pltpu.VMEM((tokens, HEAD + rank), f32),
            pltpu.VMEM((tokens, HEAD), f32),
            pltpu.VMEM((tokens, rank), f32),
            pltpu.VMEM((peers, tokens // peers, rank), f32),
            pltpu.VMEM((shards, tokens, rank), bf16),
            pltpu.VMEM((kv_heads, shards, own_rows, width), f32),
            pltpu.VMEM((kv_heads, shards, own_rows, width), bf16),
            pltpu.VMEM((kv_heads, shards, own_rows, width), bf16),
            dma((kv_heads, shards)), dma((kv_heads, shards)),
            dma((peers,)), dma((peers,)),
            dma((shards,)), dma((shards,)),
            dma((shards, peers)), dma((shards, peers)),
            dma((kv_heads, shards)), dma((kv_heads, shards)),
            dma((max(folds, 1), max(folds, 1))), dma((max(folds, 1), max(folds, 1))),
            dma((4 + 2 * kv_heads,)),
        ],
        compiler_params=pltpu.CompilerParams(
            collective_id=0, has_side_effects=True, vmem_limit_bytes=62 * 2**20
        ),
    )(queries, key_states, value_states, out_grad, layer_inputs, sketch_seeds)


def solution(mesh):
    placed = (
        P(("group", "seq"), ("head", "sub")),
        P(("group", "seq"), ("head", "sub")),
        P(("group", "seq"), ("head", "sub")),
        P(("group", "seq"), ("head", "sub")),
        P(("head", "sub"), ("group", "seq")),
        P(("head", "sub"), None),
    )
    return jax.shard_map(
        per_device,
        mesh=mesh,
        in_specs=placed,
        out_specs=(
            P(("group", "seq"), ("head", "sub")),
            P(("group", "seq"), ("head", "sub")),
            P(("group", "seq"), ("head", "sub")),
        ),
        check_vma=False,
    )
```
